32 devices in a mesh: ka: 4 (over y, x), hist: 8 (over z, core).
Axes of the slice: x: 2, y: 2, z: 4, core: 2. Of those that a mesh axis runs over, the one named last changes fastest.
Arguments:
- step_index: int32 [1], replicated, may hold values from 9 to 32
- band_energy: float32 [32, 3, 512], P('hist', None, 'ka'), may hold values from -1 to 3
- kernel_row: bfloat16 [32, 2, 3, 3, 512], P('hist', None, None, None, 'ka'), may hold values from -0.5 to 0.5
- lattice_history: bfloat16 [32, 2, 3, 3, 32, 512], P('hist', None, None, None, None, 'ka'), may hold values from -6 to 6, as said below
- diagonal_inverse: float32 [2, 3, 3, 512], P(None, None, None, 'ka'), may hold values from -3 to 3
- multiplicity: int32 [512], P('ka'), may hold values from 1 to 32, as said below
- state_energy: float32 [64], replicated, may hold values from -3 to 3
- connection: int32 [64, 6], replicated, may hold values from 0 to 63, as said below
- predicted_row: float32 [2, 64, 32], P(None, None, 'hist'), may hold values from -6 to 6
- pseudo_history: bfloat16 [32, 2, 64, 32], P('hist'), may hold values from -6 to 6, as said below
Outputs:
- lattice_row: bfloat16 [32, 2, 3, 3, 512], P('hist', None, None, None, 'ka')
- local_row: float32 [2, 3, 3, 32], P(None, None, None, 'hist')
- pseudo_row: float32 [2, 64, 32], P(None, None, 'hist')
The draws below stay inside these ranges and needn't reach their ends.
Inputs may be any that keep to these rules, and one draw needn't show every extreme that they name: `lattice_history`: the stored lattice propagators vanish where the column time j exceeds the row time m. `pseudo_history`: the stored pseudo-particle propagators vanish where the column time j exceeds the row time m. `multiplicity`: powers of two. For each flavour f, s -> connection[s, f] is an involution without fixed points; two states that flavour f links differ in that flavour's occupation, under a numbering of the states drawn from the seed.
All inputs are finite; a program needn't handle non-finite values.
Results may differ from the reference program's by a relative error of at most 0.012.
Values may be sent and summed in bfloat16 or wider, within the bound.
A program may use at most 64 MiB of HBM per device.

```python
import math
import jax
import jax.numpy as jnp
from jax import lax

ORB = 3
FLAV = 6
STATES = 64
K_DEV = 128
TIMES = 32
KPTS = 512
N_KA = 4


def draw_kernel_row(key, part):
    first, second = jax.random.split(jax.random.fold_in(key, 11), 2)
    spread = 0.6 / math.sqrt(3.0 * TIMES)
    common = jax.random.normal(first, (TIMES, 2, 3, 3, 1), jnp.float32)
    own = jax.random.normal(second, (TIMES, 2, 3, 3, KPTS), jnp.float32)
    values = (common + own) * spread
    return jnp.clip(values, -0.5, 0.5).astype(jnp.bfloat16)


def causal_mask(length):
    rows = jnp.arange(length, dtype=jnp.int32)
    return (rows[None, :] <= rows[:, None]).astype(jnp.float32)


def draw_lattice_history(key, part):
    first, second = jax.random.split(jax.random.fold_in(key, 23), 2)
    common = jax.random.normal(first, (TIMES, 2, 3, 3, TIMES, 1), jnp.float32)
    own = jax.random.normal(second, (TIMES, 2, 3, 3, TIMES, KPTS), jnp.float32)
    values = 0.7 * common + 0.7 * own
    mask = causal_mask(TIMES)[:, None, None, None, :, None]
    return (jnp.clip(values, -6.0, 6.0) * mask).astype(jnp.bfloat16)


def draw_pseudo_history(key, part):
    first = jax.random.fold_in(jax.random.fold_in(key, 37), 0)
    values = jax.random.normal(first, (TIMES, 2, STATES, TIMES), jnp.float32)
    mask = causal_mask(TIMES)[:, None, None, :]
    return (jnp.clip(values, -6.0, 6.0) * mask).astype(jnp.bfloat16)


def draw_diagonal_inverse(key, part):
    first, second, third = jax.random.split(jax.random.fold_in(key, 41), 3)
    identity = jnp.eye(3, dtype=jnp.float32)[:, :, None]
    diag_part = 0.2 * jax.random.normal(first, (3, 3, KPTS), jnp.float32)
    off_real = 0.3 * jax.random.normal(second, (3, 3, KPTS), jnp.float32)
    off_imag = 0.3 * jax.random.normal(third, (3, 3, KPTS), jnp.float32)
    part_real = identity * (1.0 + diag_part) + (1.0 - identity) * off_real
    return jnp.clip(jnp.stack([part_real, off_imag], axis=0), -3.0, 3.0)


def draw_multiplicity(key, part):
    index = jnp.arange(KPTS, dtype=jnp.int32)
    highest = 2 + 4 * index // KPTS
    powers = jax.random.randint(jax.random.fold_in(key, 53), (KPTS,), 0, highest + 1)
    return jnp.left_shift(jnp.ones((KPTS,), jnp.int32), powers)


def draw_connection(key, part):
    labels = jax.random.permutation(jax.random.fold_in(key, 67), STATES)
    positions = jnp.argsort(labels, stable=True).astype(jnp.int32)
    flips = jnp.left_shift(jnp.ones((FLAV,), jnp.int32), jnp.arange(FLAV, dtype=jnp.int32))
    target = jnp.bitwise_xor(positions[:, None], flips[None, :])
    return labels[target].astype(jnp.int32)


def block_levels(stream_key, dims, cuts, low, top_value):
    def one(axis_at, blocks):
        heights = jax.random.uniform(jax.random.fold_in(jax.random.fold_in(stream_key, 6), axis_at), (blocks,), jnp.float32, low / len(cuts), top_value / len(cuts))
        return jnp.repeat(jnp.exp(heights), dims[axis_at] // blocks).reshape((-1,) + (1,) * (len(dims) - axis_at - 1))

    factor_of = one(*cuts[0])
    for cut in cuts[1:]:
        factor_of = factor_of * one(*cut)
    return factor_of


def centred(key, extent, deviation, most, shards=(), held_as=jnp.bfloat16):
    array = deviation * jax.random.normal(key, extent, jnp.float32)
    if shards:
        array = array * block_levels(key, extent, shards, -0.22, 0.18)
    return jnp.clip(array, -most, most).astype(held_as)


def setup_inputs(seed: int = 0) -> dict:
    splits = jax.random.split(jax.random.key(seed), 11)
    step_index = jax.random.randint(splits[0], (1,), TIMES // 4 + 1, TIMES + 1).astype(jnp.int32)
    band_energy = jnp.clip(-1.0 + 4.0 * jax.random.uniform(splits[1], (TIMES, ORB, KPTS), jnp.float32) ** block_levels(splits[1], (TIMES, ORB, KPTS), ((0, 8), (2, 4)), -0.2, 0.2), -1.0, 3.0)
    kernel_row = draw_kernel_row(jax.random.fold_in(splits[10], 71), 0)
    lattice_history = draw_lattice_history(jax.random.fold_in(splits[10], 71), 0)
    diagonal_inverse = draw_diagonal_inverse(jax.random.fold_in(splits[10], 71), 0)
    multiplicity = draw_multiplicity(jax.random.fold_in(splits[10], 71), 0)
    state_energy = jnp.clip(jax.random.uniform(splits[6], (STATES,), jnp.float32, -3.0, 3.0), -3.0, 3.0)
    connection = draw_connection(jax.random.fold_in(splits[10], 71), 0)
    predicted_row = centred(splits[8], (2, STATES, TIMES), 1.0, 6.0, ((2, 8),), jnp.float32)
    pseudo_history = draw_pseudo_history(jax.random.fold_in(splits[10], 71), 0)
    return dict(step_index=step_index, band_energy=band_energy, kernel_row=kernel_row, lattice_history=lattice_history, diagonal_inverse=diagonal_inverse, multiplicity=multiplicity, state_energy=state_energy, connection=connection, predicted_row=predicted_row, pseudo_history=pseudo_history)


time_step = 0.05
coupling = 0.02


def complex_form(kernel):
    part_real = kernel[:, 0]
    part_imag = kernel[:, 1]
    upper = jnp.stack([part_real, -part_imag], axis=2)
    lower_half = jnp.stack([part_imag, part_real], axis=2)
    return jnp.stack([upper, lower_half], axis=1)


def contract(matrix, vector):
    return jnp.einsum('abk,jbck->jack', matrix, vector, precision=lax.Precision.HIGHEST)


def reference(step_index, band_energy, kernel_row, lattice_history, diagonal_inverse, multiplicity, state_energy, connection, predicted_row, pseudo_history):
    current = step_index[0]
    all_times = jnp.arange(TIMES, dtype=jnp.int32)
    before_now = (all_times < current).astype(jnp.float32)
    weight = jnp.where(all_times == 0, 0.5, 1.0).astype(jnp.float32) * before_now
    in_range = (all_times <= current).astype(jnp.float32)
    earlier = jnp.cumsum(band_energy, axis=0) - band_energy
    upto_now = jnp.sum(band_energy * before_now[:, None, None], axis=0)
    angles = time_step * (upto_now[None] - earlier)
    free_pair = jnp.stack([-jnp.sin(angles), -jnp.cos(angles)], axis=1) * in_range[:, None, None, None]
    identity = jnp.eye(3, dtype=jnp.float32)
    free_rows = free_pair[:, :, :, None, :] * identity[None, None, :, :, None]
    kernel = kernel_row.astype(jnp.float32) * weight[:, None, None, None, None]
    kernel_pairs = complex_form(kernel)
    pieces = []
    for k_block in range(N_KA):
        lower_k = k_block * K_DEV
        upper_k = lower_k + K_DEV
        pieces.append(jnp.einsum('msapbk,mpbcjk->jsack', kernel_pairs[..., lower_k:upper_k], lattice_history[..., lower_k:upper_k].astype(jnp.float32), precision=lax.Precision.HIGHEST))
    volterra_terms = jnp.concatenate(pieces, axis=4)
    right_side = volterra_terms + free_rows
    out_real = contract(diagonal_inverse[0], right_side[:, 0]) - contract(diagonal_inverse[1], right_side[:, 1])
    out_imag = contract(diagonal_inverse[0], right_side[:, 1]) + contract(diagonal_inverse[1], right_side[:, 0])
    fresh_rows = jnp.stack([out_real, out_imag], axis=1)
    lattice_row = fresh_rows.astype(jnp.bfloat16)
    weights_k = multiplicity.astype(jnp.float32)
    summed = jnp.einsum('jsack,k->sacj', fresh_rows, weights_k, precision=lax.Precision.HIGHEST)
    local_rows = summed / jnp.sum(weights_k)
    hybrid = jnp.repeat(jnp.diagonal(local_rows, axis1=1, axis2=2), 2, axis=2)
    hyb_real = hybrid[0].T
    hyb_imag = hybrid[1].T
    onehot = (connection[:, :, None] == jnp.arange(STATES, dtype=jnp.int32)[None, None, :]).astype(jnp.float32)
    reached = jnp.einsum('sft,ptm->psfm', onehot, predicted_row, precision=lax.Precision.HIGHEST)
    self_real = coupling * jnp.sum(hyb_real[None] * reached[0] - hyb_imag[None] * reached[1], axis=1)
    self_imag = coupling * jnp.sum(hyb_real[None] * reached[1] + hyb_imag[None] * reached[0], axis=1)
    wself_real = (self_real * weight[None, :]).T
    wself_imag = (self_imag * weight[None, :]).T
    hist_real = pseudo_history[:, 0].astype(jnp.float32)
    hist_imag = pseudo_history[:, 1].astype(jnp.float32)
    sum_real = jnp.sum(wself_real[:, :, None] * hist_real - wself_imag[:, :, None] * hist_imag, axis=0)
    sum_imag = jnp.sum(wself_real[:, :, None] * hist_imag + wself_imag[:, :, None] * hist_real, axis=0)
    elapsed = (current - all_times).astype(jnp.float32)
    spins = state_energy[:, None] * time_step * elapsed[None, :]
    pseudo_real = -jnp.sin(spins) * in_range[None, :] + sum_real
    pseudo_imag = -jnp.cos(spins) * in_range[None, :] + sum_imag
    pseudo_row = jnp.stack([pseudo_real, pseudo_imag], axis=0)
    return lattice_row, local_rows, pseudo_row
```

```python
import functools

import jax
import jax.numpy as jnp
from jax import lax
from jax.experimental import pallas as pl
from jax.experimental.pallas import tpu as pltpu
from jax.sharding import PartitionSpec as P

time_step = 0.05
coupling = 0.02
tile_rows = 16
layout_bytes = 4 * 1024 * 1024
highest = lax.Precision.HIGHEST


def weighted_sums(mult, values):
    upper = values.astype(jnp.bfloat16)
    lower = (values - upper.astype(jnp.float32)).astype(jnp.bfloat16)
    return dot_rows(mult, upper) + dot_rows(mult, lower)


def dot_rows(left, right, precision=None):
    return lax.dot_general(
        left,
        right,
        (((1,), (1,)), ((), ())),
        precision=precision,
        preferred_element_type=jnp.float32,
    )


def kernel(
    n_hist,
    n_ka,
    step_ref,
    band_any,
    krow_any,
    hist_any,
    dinv_any,
    mult_any,
    energy_any,
    conn_any,
    pred_any,
    pseudo_any,
    total_out,
    local_out,
    pseudo_out,
    band_ref,
    krow_ref,
    hist_ref,
    dinv_ref,
    mult_ref,
    energy_ref,
    conn_ref,
    pred_ref,
    pseudo_ref,
    kw,
    suffix,
    stage,
    esend,
    erecv,
    lsend,
    lrecv,
    psend,
    precv,
    drep,
    frep,
    total,
    ksend,
    krecv,
    turned,
    qsend,
    qrecv,
    load_sem,
    esend_sem,
    erecv_sem,
    lsend_sem,
    lrecv_sem,
    psend_sem,
    precv_sem,
    ksend_sem,
    krecv_sem,
    qsend_sem,
    qrecv_sem,
):
    orb, block, lanes = band_ref.shape
    times = hist_ref.shape[4]
    states = energy_ref.shape[1]
    pairs = 2 * orb * orb
    rows = pairs * block
    per_tile = tile_rows // block
    me = lax.axis_index("hist")
    my_ka = lax.axis_index("ka")

    barrier = pltpu.get_barrier_semaphore()

    def greet(hop, carry):
        pl.semaphore_signal(
            barrier, inc=1, device_id={"hist": lax.rem(me + hop, n_hist)},
            device_id_type=pl.DeviceIdType.MESH,
        )
        return carry

    lax.fori_loop(1, n_hist, greet, 0)
    for hop in range(1, n_ka):
        pl.semaphore_signal(
            barrier, inc=1, device_id={"ka": lax.rem(my_ka + hop, n_ka)},
            device_id_type=pl.DeviceIdType.MESH,
        )

    sources = (
        krow_any, band_any, mult_any, hist_any, dinv_any, energy_any, conn_any, pred_any, pseudo_any
    )
    targets = (
        krow_ref, band_ref, mult_ref, hist_ref, dinv_ref, energy_ref, conn_ref, pred_ref, pseudo_ref
    )
    loads = [
        pltpu.make_async_copy(source, target, load_sem.at[i])
        for i, (source, target) in enumerate(zip(sources, targets))
    ]
    for load in loads:
        load.start()

    current = step_ref[0]
    first = me * block
    before = [jnp.where(first + m < current, 1.0, 0.0) for m in range(block)]
    weight = [
        jnp.where(first + m == 0, 0.5, 1.0) * before[m] for m in range(block)
    ]

    for load in loads[:3]:
        load.wait()
    for m in range(block):
        kw[m] = krow_ref[m].astype(jnp.float32) * weight[m]

    esend[...] = jnp.zeros(esend.shape, jnp.float32)
    for c in range(orb):
        run = jnp.zeros((1, lanes), jnp.float32)
        for m in reversed(range(block)):
            run = run + band_ref[c, m : m + 1, :] * before[m]
            suffix[c * block + m : c * block + m + 1, :] = run
        esend[c : c + 1, :] = run
    mult = jnp.broadcast_to(mult_ref[...].astype(jnp.float32), (8, lanes)).astype(jnp.bfloat16)

    pl.semaphore_wait(barrier, n_hist - 1 + n_ka - 1)

    def hist_copy(src, dst, send_sem, recv_sem, source, target):
        return pltpu.make_async_remote_copy(
            src_ref=src,
            dst_ref=dst.at[source],
            send_sem=send_sem.at[target],
            recv_sem=recv_sem.at[source],
            device_id={"hist": target},
            device_id_type=pl.DeviceIdType.MESH,
        )

    def energy_copy(source, target):
        return hist_copy(esend, erecv, esend_sem, erecv_sem, source, target)

    def sum_copy(source, target):
        return hist_copy(lsend.at[target], lrecv, lsend_sem, lrecv_sem, source, target)

    def part_copy(source, target):
        return hist_copy(psend.at[target], precv, psend_sem, precv_sem, source, target)

    def pseudo_copy(source, target):
        return hist_copy(qsend.at[target], qrecv, qsend_sem, qrecv_sem, source, target)

    def give_energy(target, carry):
        energy_copy(me, target).start()
        return carry

    lax.fori_loop(0, me, give_energy, 0)
    for load in loads[3:]:
        load.wait()

    def one_tile(tile, carry):
        at = pl.ds(pl.multiple_of(tile * tile_rows, tile_rows), tile_rows)
        zero = jnp.zeros((tile_rows, lanes), jnp.float32)
        real = [[zero] * orb for _ in range(orb)]
        imag = [[zero] * orb for _ in range(orb)]
        for m in range(block):
            for b in range(orb):
                k_re = [kw[m, a, b, 0:1, :] for a in range(orb)]
                k_im = [kw[m, a, b, 1:2, :] for a in range(orb)]
                for c in range(orb):
                    h_re = hist_ref[m, 0, b, c, at, :].astype(jnp.float32)
                    h_im = hist_ref[m, 1, b, c, at, :].astype(jnp.float32)
                    for a in range(orb):
                        real[a][c] += k_re[a] * h_re - k_im[a] * h_im
                        imag[a][c] += k_re[a] * h_im + k_im[a] * h_re
        for a in range(orb):
            for c in range(orb):
                out_re, out_im = zero, zero
                for b in range(orb):
                    d_re = dinv_ref[a, b, 0:1, :]
                    d_im = dinv_ref[a, b, 1:2, :]
                    out_re += d_re * real[b][c] - d_im * imag[b][c]
                    out_im += d_re * imag[b][c] + d_im * real[b][c]
                for s, value in enumerate((out_re, out_im)):
                    row = ((s * orb + a) * orb + c) * block
                    for d in range(per_tile):
                        stage[d, row : row + block, :] = value[d * block : (d + 1) * block]
        sums = weighted_sums(mult, stage[...].reshape(per_tile * rows, lanes))
        for d in range(per_tile):
            target = tile * per_tile + d
            lsend[target, :, :rows] = sums[:1, d * rows : (d + 1) * rows]

            @pl.when(target < me)
            def _():
                sum_copy(me, target).start()

        for d in range(per_tile):
            psend[tile * per_tile + d] = stage[d].astype(jnp.bfloat16)
        return carry

    lax.fori_loop(0, first // tile_rows + 1, one_tile, 0)

    def give_part(target, carry):
        part_copy(me, target).start()
        return carry

    lax.fori_loop(0, me, give_part, 0)

    for s in range(2):
        for a in range(orb):
            for c in range(orb):
                row = ((s * orb + a) * orb + c) * block
                drep[row : row + block, :] = jnp.broadcast_to(
                    dinv_ref[a, c, s : s + 1, :], (block, lanes)
                )
    total[rows:, :] = jnp.ones((lanes - rows, lanes), jnp.float32)
    for m in range(block):
        h_re = pseudo_ref[m, 0].astype(jnp.float32)
        h_im = pseudo_ref[m, 1].astype(jnp.float32)
        turned[m, 0] = jnp.concatenate([h_re, h_im], axis=1)
        turned[m, 1] = jnp.concatenate([-h_im, h_re], axis=1)

    row_of = lax.broadcasted_iota(jnp.int32, (block, 2 * states), 0)
    lane_of = lax.broadcasted_iota(jnp.int32, (block, 2 * states), 1)
    row_time = first + row_of
    row_weight = jnp.where(row_time == 0, 0.5, 1.0) * jnp.where(row_time < current, 1.0, 0.0)
    conn = jnp.concatenate([conn_ref[...], conn_ref[...]], axis=1)
    reach = lax.broadcasted_iota(jnp.int32, (states, 2 * states), 0)
    reached = []
    for a in range(orb):
        hit = jnp.where(conn[2 * a : 2 * a + 1] == reach, 1.0, 0.0) + jnp.where(
            conn[2 * a + 1 : 2 * a + 2] == reach, 1.0, 0.0
        )
        reached.append(
            [
                jnp.dot(pred_ref[p], hit, precision=highest, preferred_element_type=jnp.float32)
                * row_weight
                * coupling
                for p in range(2)
            ]
        )
    energies = jnp.concatenate([energy_ref[...], energy_ref[...]], axis=1)
    spins = energies * time_step * (current - row_time).astype(jnp.float32)
    free_pseudo = jnp.where(lane_of < states, -jnp.sin(spins), -jnp.cos(spins))
    free_pseudo = free_pseudo * jnp.where(row_time <= current, 1.0, 0.0)

    def take_energy(source, later):
        energy_copy(source, me).wait_recv()
        return later + erecv[source]

    later = lax.fori_loop(
        me + 1, n_hist, take_energy, jnp.zeros(esend.shape, jnp.float32)
    )
    for c in range(orb):
        for j in range(block):
            frep[c * block + j : c * block + j + 1, :] = (
                later[c : c + 1] + suffix[c * block + j : c * block + j + 1, :]
            )
    size = orb * block
    angle = time_step * frep[:size, :]
    when = first + lax.rem(lax.broadcasted_iota(jnp.int32, (size, lanes), 0), block)
    inside = jnp.where(when <= current, 1.0, 0.0)
    free_re = -jnp.sin(angle) * inside
    free_im = -jnp.cos(angle) * inside
    for a in range(orb):
        frep[a * size : (a + 1) * size, :] = free_re
        frep[(orb + a) * size : (orb + a + 1) * size, :] = free_im
    half = rows // 2
    f_re, f_im = frep[:half, :], frep[half:, :]
    d_re, d_im = drep[:half, :], drep[half:, :]
    total[:half, :] = d_re * f_re - d_im * f_im
    total[half:rows, :] = d_re * f_im + d_im * f_re

    free_sums = weighted_sums(mult, total[...])[:1]

    def take_sum(source, value):
        sum_copy(source, me).wait_recv()
        return value + lrecv[source][:, :rows]

    own_sums = lsend[me][:, :rows] + free_sums[:, :rows]
    ksend[...] = free_sums
    ksend[:, :rows] = lax.fori_loop(me + 1, n_hist, take_sum, own_sums)

    def local_copy(source, target):
        return pltpu.make_async_remote_copy(
            src_ref=ksend,
            dst_ref=krecv.at[source],
            send_sem=ksend_sem.at[target],
            recv_sem=krecv_sem.at[source],
            device_id={"ka": target},
            device_id_type=pl.DeviceIdType.MESH,
        )

    for hop in range(1, n_ka):
        local_copy(my_ka, lax.rem(my_ka + hop, n_ka)).start()
    local = ksend[...]
    for hop in range(1, n_ka):
        source = lax.rem(my_ka + hop, n_ka)
        local_copy(source, my_ka).wait_recv()
        local = local + krecv[source]
    local = jnp.broadcast_to(local / local[:, rows : rows + 1], (8, lanes))
    local_out[...] = local

    lane8 = lax.broadcasted_iota(jnp.int32, local.shape, 1)
    row8 = lax.broadcasted_iota(jnp.int32, local.shape, 0)

    def diagonal(s, a):
        lane = ((s * orb + a) * orb + a) * block + row8
        picked = jnp.where((lane8 == lane) & (row8 < block), local, 0.0)
        return jnp.sum(picked, axis=1, keepdims=True)[:block]

    self_re = jnp.zeros((block, 2 * states), jnp.float32)
    self_im = self_re
    for a in range(orb):
        h_re, h_im = diagonal(0, a), diagonal(1, a)
        r_re, r_im = reached[a]
        self_re += h_re * r_re - h_im * r_im
        self_im += h_re * r_im + h_im * r_re
    part = jnp.zeros((times, 2 * states), jnp.float32)
    for m in range(block):
        part += self_re[m : m + 1] * turned[m, 0] + self_im[m : m + 1] * turned[m, 1]
    for q in range(n_hist):
        qsend[q] = part[q * block : (q + 1) * block]

    def give_pseudo(target, carry):
        pseudo_copy(me, target).start()
        return carry

    lax.fori_loop(0, me, give_pseudo, 0)

    def take_part(source, value):
        part_copy(source, me).wait_recv()
        return value + precv[source].astype(jnp.float32)

    fresh = total[:rows, :] + psend[me].astype(jnp.float32)
    total_out[...] = lax.fori_loop(me + 1, n_hist, take_part, fresh)

    def take_pseudo(source, value):
        pseudo_copy(source, me).wait_recv()
        return value + qrecv[source]

    pseudo_out[...] = lax.fori_loop(me + 1, n_hist, take_pseudo, free_pseudo + qsend[me])

    def settle(target, carry):
        energy_copy(me, target).wait_send()
        sum_copy(me, target).wait_send()
        part_copy(me, target).wait_send()
        pseudo_copy(me, target).wait_send()
        return carry

    lax.fori_loop(0, me, settle, 0)
    for hop in range(1, n_ka):
        local_copy(my_ka, lax.rem(my_ka + hop, n_ka)).wait_send()


def lay_out(total_ref, local_ref, pseudo_ref, lattice_out, local_out, pseudo_out):
    block, orb = lattice_out.shape[:2]
    states = pseudo_out.shape[2]
    half = total_ref.shape[0] // 2
    for a in range(orb):
        for c in range(orb):
            row = (a * orb + c) * block
            for j in range(block):
                pair = total_ref[pl.ds(row + j, 2, stride=half), :]
                lattice_out[j, a, c] = pair.astype(jnp.bfloat16)
            for s in range(2):
                at = s * half + row
                local_out[a, c, s : s + 1, :] = local_ref[0:1, at : at + block]
    for p in range(2):
        pseudo_out[p] = pseudo_ref[:, p * states : (p + 1) * states]


def per_device(
    n_hist,
    n_ka,
    step_index,
    band_energy,
    kernel_row,
    lattice_history,
    diagonal_inverse,
    multiplicity,
    state_energy,
    connection,
    predicted_row,
    pseudo_history,
):
    block, orb, lanes = band_energy.shape
    times = lattice_history.shape[4]
    states = state_energy.shape[0]
    pairs = 2 * orb * orb
    rows = pairs * block
    per_tile = tile_rows // block
    vmem = pl.BlockSpec(memory_space=pltpu.VMEM)
    f32, bf16 = jnp.float32, jnp.bfloat16
    dma = pltpu.SemaphoreType.DMA
    operands = (
        jnp.transpose(band_energy, (1, 0, 2)),
        jnp.transpose(kernel_row, (0, 2, 3, 1, 4)),
        lattice_history,
        jnp.transpose(diagonal_inverse, (1, 2, 0, 3)),
        multiplicity[None],
        state_energy[None],
        jnp.transpose(connection),
        jnp.transpose(predicted_row, (0, 2, 1)),
        jnp.transpose(pseudo_history, (0, 1, 3, 2)),
    )
    results = pl.pallas_call(
        functools.partial(kernel, n_hist, n_ka),
        out_shape=(
            pltpu.VMEM((rows, lanes), f32),
            pltpu.VMEM((8, lanes), f32),
            pltpu.VMEM((block, 2 * states), f32),
        ),
        in_specs=[pl.BlockSpec(memory_space=pltpu.SMEM)]
        + [pl.BlockSpec(memory_space=pl.ANY)] * len(operands),
        out_specs=(vmem, vmem, vmem),
        scratch_shapes=[
            *[pltpu.VMEM(array.shape, array.dtype) for array in operands],
            pltpu.VMEM((block, orb, orb, 2, lanes), f32),
            pltpu.VMEM((orb * block, lanes), f32),
            pltpu.VMEM((per_tile, rows, lanes), f32),
            pltpu.VMEM((8, lanes), f32),
            pltpu.VMEM((n_hist, 8, lanes), f32),
            pltpu.VMEM((n_hist, 1, lanes), f32),
            pltpu.VMEM((n_hist, 1, lanes), f32),
            pltpu.VMEM((n_hist, rows, lanes), bf16),
            pltpu.VMEM((n_hist, rows, lanes), bf16),
            pltpu.VMEM((rows, lanes), f32),
            pltpu.VMEM((rows, lanes), f32),
            pltpu.VMEM((lanes, lanes), f32),
            pltpu.VMEM((1, lanes), f32),
            pltpu.VMEM((n_ka, 1, lanes), f32),
            pltpu.VMEM((block, 2, times, 2 * states), f32),
            pltpu.VMEM((n_hist, block, 2 * states), f32),
            pltpu.VMEM((n_hist, block, 2 * states), f32),
            dma((len(operands),)),
            dma((n_hist,)),
            dma((n_hist,)),
            dma((n_hist,)),
            dma((n_hist,)),
            dma((n_hist,)),
            dma((n_hist,)),
            dma((n_ka,)),
            dma((n_ka,)),
            dma((n_hist,)),
            dma((n_hist,)),
        ],
        compiler_params=pltpu.CompilerParams(collective_id=0, has_side_effects=True),
    )(
        step_index,
        *operands,
    )
    lattice, local, pseudo = pl.pallas_call(
        lay_out,
        out_shape=(
            jax.ShapeDtypeStruct((block, orb, orb, 2, lanes), bf16),
            jax.ShapeDtypeStruct((orb, orb, 2, block), f32),
            jax.ShapeDtypeStruct((2, block, states), f32),
        ),
        in_specs=[vmem] * 3,
        out_specs=(vmem, vmem, vmem),
        compiler_params=pltpu.CompilerParams(vmem_limit_bytes=layout_bytes),
    )(*results)
    return (
        jnp.transpose(lattice, (0, 3, 1, 2, 4)),
        jnp.transpose(local, (2, 0, 1, 3)),
        jnp.transpose(pseudo, (0, 2, 1)),
    )


def solution(mesh):
    in_specs = (
        P(),
        P("hist", None, "ka"),
        P("hist", None, None, None, "ka"),
        P("hist", None, None, None, None, "ka"),
        P(None, None, None, "ka"),
        P("ka"),
        P(),
        P(),
        P(None, None, "hist"),
        P("hist", None, None, None),
    )
    out_specs = (
        P("hist", None, None, None, "ka"),
        P(None, None, None, "hist"),
        P(None, None, "hist"),
    )
    return jax.shard_map(
        functools.partial(per_device, mesh.shape["hist"], mesh.shape["ka"]),
        mesh=mesh,
        in_specs=in_specs,
        out_specs=out_specs,
        check_vma=False,
    )
```

```python
import functools

import jax
import jax.numpy as jnp
from jax import lax
from jax.experimental import pallas as pl
from jax.experimental.pallas import tpu as pltpu
from jax.sharding import PartitionSpec as P

time_step = 0.05
coupling = 0.02
tile_rows = 16
group_rows = 8
lane_count = 128
layout_bytes = 4 * 1024 * 1024


def two_parts(values):
    upper = values.astype(jnp.bfloat16).astype(jnp.float32)
    return upper, values - upper


def stacked(values):
    return jnp.concatenate(two_parts(values), axis=0).astype(jnp.bfloat16)


def dot(left, right, contract):
    return lax.dot_general(
        left,
        right,
        (((1,), (contract,)), ((), ())),
        preferred_element_type=jnp.float32,
    )


def folded(values):
    return values[:group_rows] + values[group_rows:]


def kernel(
    n_hist,
    n_ka,
    step_ref,
    band_any,
    krow_any,
    hist_any,
    dinv_any,
    mult_any,
    energy_any,
    conn_any,
    pred_any,
    pseudo_any,
    total_out,
    local_out,
    pseudo_out,
    band_recv,
    krow_ref,
    hist_ref,
    dinv_ref,
    mult_ref,
    energy_ref,
    conn_ref,
    pred_ref,
    pseudo_ref,
    kw,
    d_same,
    d_turn,
    band_all,
    free_all,
    vsend,
    vrecv,
    xsend,
    xrecv,
    psend,
    precv,
    csend,
    crecv,
    hist_p,
    hist_r,
    hits,
    mix,
    stage,
    load_sem,
    esend_sem,
    erecv_sem,
    vsend_sem,
    vrecv_sem,
    psend_sem,
    precv_sem,
    csend_sem,
    crecv_sem,
    xsend_sem,
    xrecv_sem,
):
    _, orb, block, lanes = band_recv.shape
    times = hist_ref.shape[4]
    states = energy_ref.shape[1]
    pairs = 2 * orb * orb
    rows = pairs * block
    per_tile = tile_rows // block
    width = vsend.shape[1]
    cols = orb * times
    f32, bf16 = jnp.float32, jnp.bfloat16
    me = lax.axis_index("hist")
    my_ka = lax.axis_index("ka")
    first = me * block

    barrier = pltpu.get_barrier_semaphore()

    def greet(target, carry):
        pl.semaphore_signal(
            barrier, inc=1, device_id={"hist": target}, device_id_type=pl.DeviceIdType.MESH
        )
        return carry

    lax.fori_loop(me + 1, n_hist, greet, 0)
    for hop in range(1, n_ka):
        pl.semaphore_signal(
            barrier, inc=1, device_id={"ka": lax.rem(my_ka + hop, n_ka)},
            device_id_type=pl.DeviceIdType.MESH,
        )

    sources = (
        krow_any, dinv_any, mult_any, hist_any, band_any, pred_any, pseudo_any, energy_any, conn_any
    )
    targets = (
        krow_ref, dinv_ref, mult_ref, hist_ref, band_recv.at[me], pred_ref, pseudo_ref, energy_ref,
        conn_ref,
    )
    loads = [
        pltpu.make_async_copy(source, target, load_sem.at[i])
        for i, (source, target) in enumerate(zip(sources, targets))
    ]
    for load in loads:
        load.start()

    def hist_copy(src, dst, send_sem, recv_sem, source, target):
        return pltpu.make_async_remote_copy(
            src_ref=src,
            dst_ref=dst.at[source],
            send_sem=send_sem.at[target],
            recv_sem=recv_sem.at[source],
            device_id={"hist": target},
            device_id_type=pl.DeviceIdType.MESH,
        )

    def energy_copy(source, target):
        return hist_copy(band_any, band_recv, esend_sem, erecv_sem, source, target)

    def sum_copy(source, target):
        return hist_copy(vsend, vrecv, vsend_sem, vrecv_sem, source, target)

    def part_copy(source, target):
        return hist_copy(psend.at[target], precv, psend_sem, precv_sem, source, target)

    def column_copy(source, target):
        return hist_copy(csend.at[target], crecv, csend_sem, crecv_sem, source, target)

    def local_copy(source, target):
        return pltpu.make_async_remote_copy(
            src_ref=xsend,
            dst_ref=xrecv.at[source],
            send_sem=xsend_sem.at[target],
            recv_sem=xrecv_sem.at[source],
            device_id={"ka": target},
            device_id_type=pl.DeviceIdType.MESH,
        )

    def give(copy):
        def one(target, carry):
            copy(me, target).start()
            return carry

        lax.fori_loop(0, me, one, 0)

    def take(copy):
        def one(source, carry):
            copy(source, me).wait_recv()
            return carry

        lax.fori_loop(me + 1, n_hist, one, 0)

    current = step_ref[0]
    weight = [
        jnp.where(first + m == 0, 0.5, 1.0) * jnp.where(first + m < current, 1.0, 0.0)
        for m in range(block)
    ]
    d_same[...] = jnp.zeros(d_same.shape, f32)
    d_turn[...] = jnp.zeros(d_turn.shape, f32)
    vsend[...] = jnp.zeros(vsend.shape, f32)

    with jax.named_scope("WBAR"):
        pl.semaphore_wait(barrier, me + n_ka - 1)
    give(energy_copy)

    with jax.named_scope("LOAD"):
        for load in loads[:3]:
            load.wait()
    mult = mult_ref[...].astype(f32)
    for m in range(block):
        kw[m] = krow_ref[m].astype(f32) * weight[m]
    for a in range(orb):
        for c in range(orb):
            d_re = dinv_ref[a, c, 0:1, :] * mult
            d_im = dinv_ref[a, c, 1:2, :] * mult
            d_same[c, a : a + 1, :] = d_re
            d_same[c, orb + a : orb + a + 1, :] = d_im
            d_turn[c, a : a + 1, :] = -d_im
            d_turn[c, orb + a : orb + a + 1, :] = d_re
    same = [d_same[c] for c in range(orb)]
    turn = [d_turn[c] for c in range(orb)]
    with jax.named_scope("LOADH"):
        loads[3].wait()
    left, right = [], []
    for m in range(block):
        for b in range(orb):
            plain = jnp.zeros((group_rows, lanes), f32)
            turned = plain
            for c in range(orb):
                k_re = kw[m, c, b, 0:1, :]
                k_im = kw[m, c, b, 1:2, :]
                plain += same[c] * k_re + turn[c] * k_im
                turned += turn[c] * k_re - same[c] * k_im
            for p, factor in enumerate((plain, turned)):
                left.append(stacked(factor))
                right.append(hist_ref[m, p, b].reshape(cols, lanes))
    with jax.named_scope("VDOT"):
        sums = dot(jnp.concatenate(left, axis=1), jnp.concatenate(right, axis=1), 1)
        vsend[:, :cols] = folded(sums)
    give(sum_copy)

    with jax.named_scope("PC"):
        for load in loads[4:]:
            load.wait()
        half = group_rows * 2
        for m in range(block):
            h_re = pseudo_ref[m, 0].astype(f32)
            h_im = pseudo_ref[m, 1].astype(f32)
            both = jnp.concatenate([h_re, h_im], axis=1)
            for t in range(n_hist):
                hist_p[t * half + m * block : t * half + (m + 1) * block, :] = both[
                    t * block : (t + 1) * block
                ]
        given = jnp.concatenate([pred_ref[0], pred_ref[1]], axis=1)
        tail = jnp.concatenate(
            [*two_parts(given), jnp.zeros((half - 2 * block, lanes), f32)], axis=0
        ).astype(bf16)
        for t in range(n_hist):
            csend[t, :half, :] = hist_p[t * half : (t + 1) * half, :].astype(bf16)
            csend[t, half:, :] = tail
    give(column_copy)

    def one_tile(tile, carry):
        at = pl.ds(pl.multiple_of(tile * tile_rows, tile_rows), tile_rows)
        zero = jnp.zeros((tile_rows, lanes), f32)
        real = [[zero] * orb for _ in range(orb)]
        imag = [[zero] * orb for _ in range(orb)]
        for m in range(block):
            for b in range(orb):
                k_re = [kw[m, a, b, 0:1, :] for a in range(orb)]
                k_im = [kw[m, a, b, 1:2, :] for a in range(orb)]
                for c in range(orb):
                    h_re = hist_ref[m, 0, b, c, at, :].astype(f32)
                    h_im = hist_ref[m, 1, b, c, at, :].astype(f32)
                    for a in range(orb):
                        real[a][c] += k_re[a] * h_re - k_im[a] * h_im
                        imag[a][c] += k_re[a] * h_im + k_im[a] * h_re
        for a in range(orb):
            for c in range(orb):
                out_re, out_im = zero, zero
                for b in range(orb):
                    d_re = dinv_ref[a, b, 0:1, :]
                    d_im = dinv_ref[a, b, 1:2, :]
                    out_re += d_re * real[b][c] - d_im * imag[b][c]
                    out_im += d_re * imag[b][c] + d_im * real[b][c]
                for s, value in enumerate((out_re, out_im)):
                    row = ((s * orb + a) * orb + c) * block
                    for d in range(per_tile):
                        stage[d, row : row + block, :] = value[d * block : (d + 1) * block]
        for d in range(per_tile):
            target = tile * per_tile + d
            psend[target] = stage[d].astype(bf16)

            @pl.when(target < me)
            def _():
                part_copy(me, target).start()

        return carry

    with jax.named_scope("TILES"):
        lax.fori_loop(0, first // tile_rows + 1, one_tile, 0)

    crecv[me] = csend[me]
    row_of = lax.broadcasted_iota(jnp.int32, (times, lanes), 0)
    lane_of = lax.broadcasted_iota(jnp.int32, (group_rows, width), 1)
    group_of = lax.broadcasted_iota(jnp.int32, (group_rows, width), 0)
    conn = jnp.concatenate([conn_ref[...], conn_ref[...]], axis=1)
    reach = lax.broadcasted_iota(jnp.int32, (2 * states, 2 * states), 0)
    for a in range(orb):
        for p in range(2):
            at = (2 * a + p) * lanes
            hit = jnp.where(conn[2 * a : 2 * a + 1] + p * states == reach, 1.0, 0.0) + jnp.where(
                conn[2 * a + 1 : 2 * a + 2] + p * states == reach, 1.0, 0.0
            )
            hits[:, at : at + 2 * states] = hit.astype(bf16)
    mix[cols:width, :] = jnp.zeros((width - cols, mix.shape[1]), bf16)
    mix[width + cols :, :] = jnp.zeros((width - cols, mix.shape[1]), bf16)
    line = lax.broadcasted_iota(jnp.int32, (block, 2 * states), 0) + first
    lane = lax.broadcasted_iota(jnp.int32, (block, 2 * states), 1)
    energies = jnp.concatenate([energy_ref[...], energy_ref[...]], axis=1)
    spins = energies * time_step * (current - line).astype(f32)
    free_pseudo = jnp.where(lane < states, -jnp.sin(spins), -jnp.cos(spins))
    free_pseudo = free_pseudo * jnp.where(line <= current, 1.0, 0.0)
    count = jnp.sum(mult, axis=1, keepdims=True)
    step_row = lax.broadcasted_iota(jnp.int32, (times, times), 0)
    step_col = lax.broadcasted_iota(jnp.int32, (times, times), 1)
    later = jnp.where((step_col >= step_row) & (step_col < current), 1.0, 0.0).astype(bf16)
    inside = (row_of <= current) & (row_of >= first)

    with jax.named_scope("TAKEE"):
        take(energy_copy)
    with jax.named_scope("FREE"):
        for t in range(n_hist):
            for c in range(orb):
                band_all[c, t * block : (t + 1) * block, :] = band_recv[t, c]
        angle = jnp.zeros((times, orb * lanes), f32)
        rest = jnp.concatenate(
            [jnp.where(row_of >= first, band_all[c], 0.0) for c in range(orb)], axis=1
        )
        for _ in range(3):
            piece = rest.astype(bf16)
            angle += dot(later, piece, 0)
            rest = rest - piece.astype(f32)
        angle = angle * time_step
        pieces = []
        for c in range(orb):
            part = angle[:, c * lanes : (c + 1) * lanes]
            free_re = jnp.where(inside, -jnp.sin(part), 0.0)
            free_im = jnp.where(inside, -jnp.cos(part), 0.0)
            free_all[0, c] = free_re
            free_all[1, c] = free_im
            two_re, two_im = two_parts(free_re), two_parts(free_im)
            right = jnp.concatenate([two_re[0], two_im[0], two_re[1], two_im[1]], axis=1)
            left = jnp.concatenate([stacked(same[c]), stacked(turn[c])] * 2, axis=1)
            pieces.append(folded(dot(left, right.astype(bf16), 1)))
        pieces.append(jnp.zeros((group_rows, width - cols), f32))
        own = jnp.concatenate(pieces, axis=1) + vsend[...]
        own = jnp.where(lane_of == cols, count, own)

    def take_sum(source, value):
        sum_copy(source, me).wait_recv()
        return value + vrecv[source]

    with jax.named_scope("TAKEV"):
        xsend[...] = lax.fori_loop(me + 1, n_hist, take_sum, own)
    for hop in range(1, n_ka):
        local_copy(my_ka, lax.rem(my_ka + hop, n_ka)).start()

    with jax.named_scope("TOTAL"):
        at = pl.ds(pl.multiple_of(first, block), block)
        for c in range(orb):
            f_re = free_all[0, c, at, :]
            f_im = free_all[1, c, at, :]
            for a in range(orb):
                d_re = dinv_ref[a, c, 0:1, :]
                d_im = dinv_ref[a, c, 1:2, :]
                row = (a * orb + c) * block
                total_out[row : row + block, :] = d_re * f_re - d_im * f_im
                row += rows // 2
                total_out[row : row + block, :] = d_re * f_im + d_im * f_re

    with jax.named_scope("TAKEC"):
        take(column_copy)
    with jax.named_scope("MIX"):
        for t in range(n_hist):
            hist_p[t * half : (t + 1) * half, :] = crecv[t, :half, :].astype(f32)
            tail = crecv[t, half:, :].astype(f32)
            for p in range(2):
                at = p * times + t * block
                hist_r[at : at + block, :] = tail[p * block : (p + 1) * block]
        known = jnp.concatenate([row_of >= first] * 2, axis=0)
        given = jnp.where(known, hist_r[...], 0.0).astype(bf16)
        reached = dot(given, hits[...], 0)
        reached = reached[:times] + reached[times:]
        row_weight = jnp.where(row_of == 0, 0.5 * coupling, coupling)
        row_weight = row_weight * jnp.where(row_of < current, 1.0, 0.0)
        sign = jnp.where(
            lax.broadcasted_iota(jnp.int32, (times, lanes), 1) < states, -1.0, 1.0
        )
        r_re = [reached[:, 2 * a * lanes : (2 * a + 1) * lanes] * row_weight for a in range(orb)]
        r_im = [
            reached[:, (2 * a + 1) * lanes : (2 * a + 2) * lanes] * row_weight for a in range(orb)
        ]
        for j in range(block):
            plain = jnp.where(row_of >= first, hist_p[pl.ds(j, times, stride=block), :], 0.0)
            turned = pltpu.roll(plain, states, 1) * sign
            at = slice(j * lanes, (j + 1) * lanes)
            for a in range(orb):
                low, high = a * times, (a + 1) * times
                mix[low:high, at] = (r_re[a] * plain + r_im[a] * turned).astype(bf16)
                mix[width + low : width + high, at] = (
                    r_re[a] * turned - r_im[a] * plain
                ).astype(bf16)

    with jax.named_scope("TAKEX"):
        local = xsend[...]
        for hop in range(1, n_ka):
            source = lax.rem(my_ka + hop, n_ka)
            local_copy(source, my_ka).wait_recv()
            local = local + xrecv[source]
    with jax.named_scope("FINAL"):
        scale = 1.0 / local[:, cols : cols + 1]
        picked = jnp.where(lane_of // times == lax.rem(group_of, orb), local, 0.0)
        picked = jnp.concatenate(
            [jnp.where(group_of < orb, picked, 0.0), jnp.where(group_of < orb, 0.0, picked)], axis=1
        )
        sums = folded(dot(stacked(picked), mix[...], 0))
        sums = jnp.sum(sums, axis=0, keepdims=True)
        for j in range(block):
            pseudo_out[j : j + 1, :] = (
                free_pseudo[j : j + 1] + sums[:, j * lanes : (j + 1) * lanes] * scale[:1]
            )
        local_out[...] = pltpu.roll(local * scale, width - first, 1)

    def take_part(source, value):
        part_copy(source, me).wait_recv()
        return value + precv[source].astype(f32)

    with jax.named_scope("TAKEP"):
        fresh = total_out[...] + psend[me].astype(f32)
        total_out[...] = lax.fori_loop(me + 1, n_hist, take_part, fresh)

    def settle(target, carry):
        energy_copy(me, target).wait_send()
        sum_copy(me, target).wait_send()
        column_copy(me, target).wait_send()
        part_copy(me, target).wait_send()
        return carry

    lax.fori_loop(0, me, settle, 0)
    for hop in range(1, n_ka):
        local_copy(my_ka, lax.rem(my_ka + hop, n_ka)).wait_send()


def lay_out(times, total_ref, local_ref, pseudo_ref, lattice_out, local_out, pseudo_out):
    block, orb = lattice_out.shape[:2]
    states = pseudo_out.shape[2]
    half = total_ref.shape[0] // 2
    for a in range(orb):
        for c in range(orb):
            row = (a * orb + c) * block
            for j in range(block):
                pair = total_ref[pl.ds(row + j, 2, stride=half), :]
                lattice_out[j, a, c] = pair.astype(jnp.bfloat16)
            for s in range(2):
                row = s * orb + a
                local_out[a, c, s : s + 1, :] = local_ref[
                    row : row + 1, c * times : c * times + block
                ]
    for p in range(2):
        pseudo_out[p] = pseudo_ref[:, p * states : (p + 1) * states]


def per_device(
    n_hist,
    n_ka,
    step_index,
    band_energy,
    kernel_row,
    lattice_history,
    diagonal_inverse,
    multiplicity,
    state_energy,
    connection,
    predicted_row,
    pseudo_history,
):
    block, orb, lanes = band_energy.shape
    times = lattice_history.shape[4]
    states = state_energy.shape[0]
    pairs = 2 * orb * orb
    rows = pairs * block
    per_tile = tile_rows // block
    width = -(-(orb * times + 1) // lane_count) * lane_count
    vmem = pl.BlockSpec(memory_space=pltpu.VMEM)
    f32, bf16 = jnp.float32, jnp.bfloat16
    dma = pltpu.SemaphoreType.DMA
    operands = (
        jnp.transpose(band_energy, (1, 0, 2)),
        jnp.transpose(kernel_row, (0, 2, 3, 1, 4)),
        lattice_history,
        jnp.transpose(diagonal_inverse, (1, 2, 0, 3)),
        multiplicity[None],
        state_energy[None],
        jnp.transpose(connection),
        jnp.transpose(predicted_row, (0, 2, 1)),
        jnp.transpose(pseudo_history, (0, 1, 3, 2)),
    )
    results = pl.pallas_call(
        functools.partial(kernel, n_hist, n_ka),
        out_shape=(
            pltpu.VMEM((rows, lanes), f32),
            pltpu.VMEM((group_rows, width), f32),
            pltpu.VMEM((block, 2 * states), f32),
        ),
        in_specs=[pl.BlockSpec(memory_space=pltpu.SMEM)]
        + [pl.BlockSpec(memory_space=pl.ANY)] * len(operands),
        out_specs=(vmem, vmem, vmem),
        scratch_shapes=[
            pltpu.VMEM((n_hist, *operands[0].shape), f32),
            *[pltpu.VMEM(array.shape, array.dtype) for array in operands[1:]],
            pltpu.VMEM((block, orb, orb, 2, lanes), f32),
            pltpu.VMEM((orb, group_rows, lanes), f32),
            pltpu.VMEM((orb, group_rows, lanes), f32),
            pltpu.VMEM((orb, times, lanes), f32),
            pltpu.VMEM((2, orb, times, lanes), f32),
            pltpu.VMEM((group_rows, width), f32),
            pltpu.VMEM((n_hist, group_rows, width), f32),
            pltpu.VMEM((group_rows, width), f32),
            pltpu.VMEM((n_ka, group_rows, width), f32),
            pltpu.VMEM((n_hist, rows, lanes), bf16),
            pltpu.VMEM((n_hist, rows, lanes), bf16),
            pltpu.VMEM((n_hist, 4 * group_rows, lanes), bf16),
            pltpu.VMEM((n_hist, 4 * group_rows, lanes), bf16),
            pltpu.VMEM((times * block, lanes), f32),
            pltpu.VMEM((2 * times, lanes), f32),
            pltpu.VMEM((2 * states, 2 * orb * lanes), bf16),
            pltpu.VMEM((2 * width, 2 * block * states), bf16),
            pltpu.VMEM((per_tile, rows, lanes), f32),
            dma((len(operands),)),
            *[dma((n_hist,)) for _ in range(8)],
            dma((n_ka,)),
            dma((n_ka,)),
        ],
        compiler_params=pltpu.CompilerParams(collective_id=0, has_side_effects=True),
    )(
        step_index,
        *operands,
    )
    lattice, local, pseudo = pl.pallas_call(
        functools.partial(lay_out, times),
        out_shape=(
            jax.ShapeDtypeStruct((block, orb, orb, 2, lanes), bf16),
            jax.ShapeDtypeStruct((orb, orb, 2, block), f32),
            jax.ShapeDtypeStruct((2, block, states), f32),
        ),
        in_specs=[vmem] * 3,
        out_specs=(vmem, vmem, vmem),
        compiler_params=pltpu.CompilerParams(vmem_limit_bytes=layout_bytes),
    )(*results)
    return (
        jnp.transpose(lattice, (0, 3, 1, 2, 4)),
        jnp.transpose(local, (2, 0, 1, 3)),
        jnp.transpose(pseudo, (0, 2, 1)),
    )


def solution(mesh):
    in_specs = (
        P(),
        P("hist", None, "ka"),
        P("hist", None, None, None, "ka"),
        P("hist", None, None, None, None, "ka"),
        P(None, None, None, "ka"),
        P("ka"),
        P(),
        P(),
        P(None, None, "hist"),
        P("hist", None, None, None),
    )
    out_specs = (
        P("hist", None, None, None, "ka"),
        P(None, None, None, "hist"),
        P(None, None, "hist"),
    )
    return jax.shard_map(
        functools.partial(per_device, mesh.shape["hist"], mesh.shape["ka"]),
        mesh=mesh,
        in_specs=in_specs,
        out_specs=out_specs,
        check_vma=False,
    )
```

```python
import functools

import jax
import jax.numpy as jnp
from jax import lax
from jax.experimental import pallas as pl
from jax.experimental.pallas import tpu as pltpu
from jax.sharding import PartitionSpec as P

time_step = 0.05
coupling = 0.02
tile_rows = 16
group_rows = 8
lead = 2
lane_count = 128
layout_bytes = 4 * 1024 * 1024


def two_parts(values):
    upper = values.astype(jnp.bfloat16).astype(jnp.float32)
    return upper, values - upper


def stacked(values):
    return jnp.concatenate(two_parts(values), axis=0).astype(jnp.bfloat16)


def dot(left, right, contract):
    return lax.dot_general(
        left,
        right,
        (((1,), (contract,)), ((), ())),
        preferred_element_type=jnp.float32,
    )


def folded(values):
    return values[:group_rows] + values[group_rows:]


def kernel(
    n_hist,
    n_ka,
    step_ref,
    band_any,
    krow_any,
    hist_any,
    dinv_any,
    mult_any,
    energy_any,
    conn_any,
    pred_any,
    pseudo_any,
    total_out,
    local_out,
    pseudo_out,
    band_recv,
    krow_ref,
    hist_ref,
    dinv_ref,
    mult_ref,
    energy_ref,
    conn_ref,
    pred_ref,
    pseudo_ref,
    kw,
    d_same,
    d_turn,
    band_all,
    free_all,
    vsend,
    vrecv,
    xsend,
    xfree,
    xrecv,
    psend,
    precv,
    csend,
    crecv,
    hist_p,
    hist_r,
    hits,
    mix,
    stage,
    load_sem,
    sent_energy,
    sent_sum,
    sent_direct,
    sent_column,
    sent_part,
    sent_local,
    got_energy,
    got_sum,
    got_column,
    got_part,
    got_local,
    opened,
):
    _, orb, block, lanes = band_recv.shape
    times = hist_ref.shape[4]
    states = energy_ref.shape[1]
    pairs = 2 * orb * orb
    rows = pairs * block
    per_tile = tile_rows // block
    width = vsend.shape[1]
    cols = orb * times
    f32, bf16 = jnp.float32, jnp.bfloat16
    me = lax.axis_index("hist")
    my_ka = lax.axis_index("ka")
    first = me * block

    barrier = pltpu.get_barrier_semaphore()

    def signal(sem, hist, ka):
        pl.semaphore_signal(
            sem, inc=1, device_id={"hist": hist, "ka": ka}, device_id_type=pl.DeviceIdType.MESH
        )

    def greet(target, carry):
        signal(barrier, target, my_ka)
        return carry

    lax.fori_loop(me + 1, n_hist, greet, 0)
    is_root = (my_ka == 0) & (me < lead)

    @pl.when(is_root)
    def _():
        def one(target, carry):
            for ka in range(1, n_ka):
                signal(barrier, target, ka)
            return carry

        lax.fori_loop(me + 1, n_hist, one, 0)

    for ka in range(n_ka):

        @pl.when((me > 0) | (my_ka != ka))
        def _():
            signal(barrier, 0, ka)

    def load(source, target, place):
        copy = pltpu.make_async_copy(source, target, load_sem.at[place])
        copy.start()
        return copy

    pairs_in = [(krow_any, krow_ref), (dinv_any, dinv_ref), (mult_any, mult_ref)]
    pairs_in += [(hist_any.at[m], hist_ref.at[m]) for m in range(block)]
    pairs_in += [
        (pred_any, pred_ref),
        (pseudo_any, pseudo_ref),
        (energy_any, energy_ref),
        (conn_any, conn_ref),
        (band_any, band_recv.at[me]),
    ]
    loads = [load(source, target, i) for i, (source, target) in enumerate(pairs_in)]
    small, large, others = loads[:3], loads[3 : 3 + block], loads[3 + block :]

    def remote(src, dst, send_sem, recv_sem, hist, ka):
        return pltpu.make_async_remote_copy(
            src_ref=src,
            dst_ref=dst,
            send_sem=send_sem,
            recv_sem=recv_sem,
            device_id={"hist": hist, "ka": ka},
            device_id_type=pl.DeviceIdType.MESH,
        )

    def energy_copy(target):
        return remote(band_any, band_recv.at[me], sent_energy, got_energy, target, my_ka)

    def sum_copy(target):
        return remote(vsend, vrecv.at[me, my_ka], sent_sum, got_sum, target, my_ka)

    def direct_copy(target):
        return remote(vsend, vrecv.at[me, my_ka], sent_direct, got_sum, target, 0)

    def part_copy(target):
        return remote(psend.at[target], precv.at[me], sent_part, got_part, target, my_ka)

    def column_copy(target):
        return remote(csend.at[target], crecv.at[me], sent_column, got_column, target, my_ka)

    def local_copy(src, hop):
        target = lax.rem(my_ka + hop, n_ka)
        return remote(src, xrecv.at[hop - 1], sent_local, got_local, me, target)

    def give(copy, stop):
        def one(target, carry):
            copy(target).start()
            return carry

        lax.fori_loop(0, stop, one, 0)

    def wait_bytes(ref, sem):
        pltpu.make_async_copy(ref, ref, sem).wait()

    def take(ref, sem):
        for t in range(n_hist - 1):

            @pl.when(me == t)
            def _():
                wait_bytes(ref.at[pl.ds(t + 1, n_hist - 1 - t)], sem)

    current = step_ref[0]
    weight = [
        jnp.where(first + m == 0, 0.5, 1.0) * jnp.where(first + m < current, 1.0, 0.0)
        for m in range(block)
    ]
    d_same[...] = jnp.zeros(d_same.shape, f32)
    d_turn[...] = jnp.zeros(d_turn.shape, f32)
    vsend[...] = jnp.zeros(vsend.shape, f32)

    direct = jnp.where(my_ka == 0, 0, jnp.minimum(me, lead))
    with jax.named_scope("WBAR"):

        @pl.when(me > 0)
        def _():
            pl.semaphore_wait(barrier, me + direct)

    give(energy_copy, me)

    with jax.named_scope("LOAD"):
        for copy in small:
            copy.wait()
    mult = mult_ref[...].astype(f32)
    for m in range(block):
        kw[m] = krow_ref[m].astype(f32) * weight[m]
    for a in range(orb):
        for c in range(orb):
            d_re = dinv_ref[a, c, 0:1, :] * mult
            d_im = dinv_ref[a, c, 1:2, :] * mult
            d_same[c, a : a + 1, :] = d_re
            d_same[c, orb + a : orb + a + 1, :] = d_im
            d_turn[c, a : a + 1, :] = -d_im
            d_turn[c, orb + a : orb + a + 1, :] = d_re
    same = [d_same[c] for c in range(orb)]
    turn = [d_turn[c] for c in range(orb)]
    left = []
    for m in range(block):
        left.append([])
        for b in range(orb):
            plain = jnp.zeros((group_rows, lanes), f32)
            turned = plain
            for c in range(orb):
                k_re = kw[m, c, b, 0:1, :]
                k_im = kw[m, c, b, 1:2, :]
                plain += same[c] * k_re + turn[c] * k_im
                turned += turn[c] * k_re - same[c] * k_im
            left[m] += [stacked(plain), stacked(turned)]
    sums = jnp.zeros((2 * group_rows, cols), f32)
    for m in range(block):
        with jax.named_scope("LOADH"):
            large[m].wait()
        right = [hist_ref[m, p, b].reshape(cols, lanes) for b in range(orb) for p in range(2)]
        sums += dot(jnp.concatenate(left[m], axis=1), jnp.concatenate(right, axis=1), 1)
    with jax.named_scope("VSEND"):
        vsend[:, :cols] = folded(sums)

        give(direct_copy, direct)
        give(sum_copy, me)

    with jax.named_scope("PC"):
        for copy in others:
            copy.wait()
        half = group_rows * 2
        for m in range(block):
            h_re = pseudo_ref[m, 0].astype(f32)
            h_im = pseudo_ref[m, 1].astype(f32)
            both = jnp.concatenate([h_re, h_im], axis=1)
            for t in range(n_hist):
                hist_p[t * half + m * block : t * half + (m + 1) * block, :] = both[
                    t * block : (t + 1) * block
                ]
        given = jnp.concatenate([pred_ref[0], pred_ref[1]], axis=1)
        tail = jnp.concatenate(
            [*two_parts(given), jnp.zeros((half - 2 * block, lanes), f32)], axis=0
        ).astype(bf16)
        for t in range(n_hist):
            csend[t, :half, :] = hist_p[t * half : (t + 1) * half, :].astype(bf16)
            csend[t, half:, :] = tail
    give(column_copy, me)

    def one_tile(tile, carry):
        at = pl.ds(pl.multiple_of(tile * tile_rows, tile_rows), tile_rows)
        zero = jnp.zeros((tile_rows, lanes), f32)
        real = [[zero] * orb for _ in range(orb)]
        imag = [[zero] * orb for _ in range(orb)]
        for m in range(block):
            for b in range(orb):
                k_re = [kw[m, a, b, 0:1, :] for a in range(orb)]
                k_im = [kw[m, a, b, 1:2, :] for a in range(orb)]
                for c in range(orb):
                    h_re = hist_ref[m, 0, b, c, at, :].astype(f32)
                    h_im = hist_ref[m, 1, b, c, at, :].astype(f32)
                    for a in range(orb):
                        real[a][c] += k_re[a] * h_re - k_im[a] * h_im
                        imag[a][c] += k_re[a] * h_im + k_im[a] * h_re
        for a in range(orb):
            for c in range(orb):
                out_re, out_im = zero, zero
                for b in range(orb):
                    d_re = dinv_ref[a, b, 0:1, :]
                    d_im = dinv_ref[a, b, 1:2, :]
                    out_re += d_re * real[b][c] - d_im * imag[b][c]
                    out_im += d_re * imag[b][c] + d_im * real[b][c]
                for s, value in enumerate((out_re, out_im)):
                    row = ((s * orb + a) * orb + c) * block
                    for d in range(per_tile):
                        stage[d, row : row + block, :] = value[d * block : (d + 1) * block]
        for d in range(per_tile):
            target = tile * per_tile + d
            psend[target] = stage[d].astype(bf16)

            @pl.when(target < me)
            def _():
                part_copy(target).start()

        return carry

    with jax.named_scope("TILES"):
        lax.fori_loop(0, first // tile_rows + 1, one_tile, 0)

    crecv[me] = csend[me]
    row_of = lax.broadcasted_iota(jnp.int32, (times, lanes), 0)
    lane_of = lax.broadcasted_iota(jnp.int32, (group_rows, width), 1)
    group_of = lax.broadcasted_iota(jnp.int32, (group_rows, width), 0)
    conn = jnp.concatenate([conn_ref[...], conn_ref[...]], axis=1)
    reach = lax.broadcasted_iota(jnp.int32, (2 * states, 2 * states), 0)
    for a in range(orb):
        for p in range(2):
            at = (2 * a + p) * lanes
            hit = jnp.where(conn[2 * a : 2 * a + 1] + p * states == reach, 1.0, 0.0) + jnp.where(
                conn[2 * a + 1 : 2 * a + 2] + p * states == reach, 1.0, 0.0
            )
            hits[:, at : at + 2 * states] = hit.astype(bf16)
    mix[cols:width, :] = jnp.zeros((width - cols, mix.shape[1]), bf16)
    mix[width + cols :, :] = jnp.zeros((width - cols, mix.shape[1]), bf16)
    line = lax.broadcasted_iota(jnp.int32, (block, 2 * states), 0) + first
    lane = lax.broadcasted_iota(jnp.int32, (block, 2 * states), 1)
    energies = jnp.concatenate([energy_ref[...], energy_ref[...]], axis=1)
    spins = energies * time_step * (current - line).astype(f32)
    free_pseudo = jnp.where(lane < states, -jnp.sin(spins), -jnp.cos(spins))
    free_pseudo = free_pseudo * jnp.where(line <= current, 1.0, 0.0)
    count = jnp.sum(mult, axis=1, keepdims=True)
    step_row = lax.broadcasted_iota(jnp.int32, (times, times), 0)
    step_col = lax.broadcasted_iota(jnp.int32, (times, times), 1)
    later = jnp.where((step_col >= step_row) & (step_col < current), 1.0, 0.0).astype(bf16)
    inside = (row_of <= current) & (row_of >= first)

    with jax.named_scope("WOPEN"):

        @pl.when(me == 0)
        def _():
            pl.semaphore_wait(barrier, n_hist * n_ka - 1)

            def one(target, carry):
                signal(opened, target, my_ka)
                return carry

            lax.fori_loop(1, n_hist, one, 0)

    with jax.named_scope("TAKEE"):
        take(band_recv, got_energy)
    with jax.named_scope("FREE"):
        for t in range(n_hist):
            for c in range(orb):
                band_all[c, t * block : (t + 1) * block, :] = band_recv[t, c]
        angle = jnp.zeros((times, orb * lanes), f32)
        rest = jnp.concatenate(
            [jnp.where(row_of >= first, band_all[c], 0.0) for c in range(orb)], axis=1
        )
        for _ in range(3):
            piece = rest.astype(bf16)
            angle += dot(later, piece, 0)
            rest = rest - piece.astype(f32)
        angle = angle * time_step
        pieces = []
        for c in range(orb):
            part = angle[:, c * lanes : (c + 1) * lanes]
            free_re = jnp.where(inside, -jnp.sin(part), 0.0)
            free_im = jnp.where(inside, -jnp.cos(part), 0.0)
            free_all[0, c] = free_re
            free_all[1, c] = free_im
            two_re, two_im = two_parts(free_re), two_parts(free_im)
            right = jnp.concatenate([two_re[0], two_im[0], two_re[1], two_im[1]], axis=1)
            left = jnp.concatenate([stacked(same[c]), stacked(turn[c])] * 2, axis=1)
            pieces.append(folded(dot(left, right.astype(bf16), 1)))
        pieces.append(jnp.zeros((group_rows, width - cols), f32))
        own = jnp.concatenate(pieces, axis=1) + vsend[...]
        own = jnp.where(lane_of == cols, count, own)

    xfree[...] = own
    with jax.named_scope("WOPEN2"):

        @pl.when(me > 0)
        def _():
            pl.semaphore_wait(opened, 1)

    for hop in range(1, n_ka):
        target = lax.rem(my_ka + hop, n_ka)

        @pl.when((me < lead) & (target == 0))
        def _():
            local_copy(xfree, hop).start()

    with jax.named_scope("TAKEV"):

        for t in range(n_hist - 1):
            later_rows = pl.ds(t + 1, n_hist - 1 - t)

            @pl.when((me == t) & is_root)
            def _():
                wait_bytes(vrecv.at[later_rows], got_sum)

            @pl.when((me == t) & jnp.logical_not(is_root))
            def _():
                wait_bytes(vrecv.at[later_rows, my_ka], got_sum)

    xsend[...] = lax.fori_loop(
        me + 1, n_hist, lambda source, value: value + vrecv[source, my_ka], own
    )
    for hop in range(1, n_ka):
        target = lax.rem(my_ka + hop, n_ka)

        @pl.when((me >= lead) | (target != 0))
        def _():
            local_copy(xsend, hop).start()

    @pl.when(is_root)
    def _():
        def one(source, value):
            for ka in range(1, n_ka):
                value = value + vrecv[source, ka]
            return value

        xfree[...] = lax.fori_loop(me + 1, n_hist, one, xsend[...])

    with jax.named_scope("TOTAL"):
        at = pl.ds(pl.multiple_of(first, block), block)
        for c in range(orb):
            f_re = free_all[0, c, at, :]
            f_im = free_all[1, c, at, :]
            for a in range(orb):
                d_re = dinv_ref[a, c, 0:1, :]
                d_im = dinv_ref[a, c, 1:2, :]
                row = (a * orb + c) * block
                total_out[row : row + block, :] = d_re * f_re - d_im * f_im
                row += rows // 2
                total_out[row : row + block, :] = d_re * f_im + d_im * f_re

    with jax.named_scope("TAKEC"):
        take(crecv, got_column)
    with jax.named_scope("MIX"):
        for t in range(n_hist):
            hist_p[t * half : (t + 1) * half, :] = crecv[t, :half, :].astype(f32)
            tail = crecv[t, half:, :].astype(f32)
            for p in range(2):
                at = p * times + t * block
                hist_r[at : at + block, :] = tail[p * block : (p + 1) * block]
        known = jnp.concatenate([row_of >= first] * 2, axis=0)
        given = jnp.where(known, hist_r[...], 0.0).astype(bf16)
        reached = dot(given, hits[...], 0)
        reached = reached[:times] + reached[times:]
        row_weight = jnp.where(row_of == 0, 0.5 * coupling, coupling)
        row_weight = row_weight * jnp.where(row_of < current, 1.0, 0.0)
        sign = jnp.where(
            lax.broadcasted_iota(jnp.int32, (times, lanes), 1) < states, -1.0, 1.0
        )
        r_re = [reached[:, 2 * a * lanes : (2 * a + 1) * lanes] * row_weight for a in range(orb)]
        r_im = [
            reached[:, (2 * a + 1) * lanes : (2 * a + 2) * lanes] * row_weight for a in range(orb)
        ]
        for j in range(block):
            plain = jnp.where(row_of >= first, hist_p[pl.ds(j, times, stride=block), :], 0.0)
            turned = pltpu.roll(plain, states, 1) * sign
            at = slice(j * lanes, (j + 1) * lanes)
            for a in range(orb):
                low, high = a * times, (a + 1) * times
                mix[low:high, at] = (r_re[a] * plain + r_im[a] * turned).astype(bf16)
                mix[width + low : width + high, at] = (
                    r_re[a] * turned - r_im[a] * plain
                ).astype(bf16)

    with jax.named_scope("TAKEX"):
        wait_bytes(xrecv, got_local)
        local = jnp.where(is_root, xfree[...], xsend[...])
        for hop in range(1, n_ka):
            local = local + xrecv[hop - 1]
    with jax.named_scope("FINAL"):
        scale = 1.0 / local[:, cols : cols + 1]
        picked = jnp.where(lane_of // times == lax.rem(group_of, orb), local, 0.0)
        picked = jnp.concatenate(
            [jnp.where(group_of < orb, picked, 0.0), jnp.where(group_of < orb, 0.0, picked)], axis=1
        )
        sums = folded(dot(stacked(picked), mix[...], 0))
        sums = jnp.sum(sums, axis=0, keepdims=True)
        for j in range(block):
            pseudo_out[j : j + 1, :] = (
                free_pseudo[j : j + 1] + sums[:, j * lanes : (j + 1) * lanes] * scale[:1]
            )
        local_out[...] = pltpu.roll(local * scale, width - first, 1)

    with jax.named_scope("TAKEP"):
        take(precv, got_part)
        total_out[...] = lax.fori_loop(
            me + 1,
            n_hist,
            lambda source, value: value + precv[source].astype(f32),
            total_out[...] + psend[me].astype(f32),
        )

    with jax.named_scope("SETTLE"):
        for t in range(1, n_hist):

            @pl.when(me == t)
            def _():
                wait_bytes(band_recv.at[pl.ds(0, t)], sent_energy)
                wait_bytes(vrecv.at[pl.ds(0, t), 0], sent_sum)
                wait_bytes(csend.at[pl.ds(0, t)], sent_column)
                wait_bytes(psend.at[pl.ds(0, t)], sent_part)

        for t in range(1, lead + 1):

            @pl.when(direct == t)
            def _():
                wait_bytes(vrecv.at[pl.ds(0, t), 0], sent_direct)

        wait_bytes(xrecv, sent_local)


def lay_out(times, total_ref, local_ref, pseudo_ref, lattice_out, local_out, pseudo_out):
    block, orb = lattice_out.shape[:2]
    states = pseudo_out.shape[2]
    half = total_ref.shape[0] // 2
    for a in range(orb):
        for c in range(orb):
            row = (a * orb + c) * block
            for j in range(block):
                pair = total_ref[pl.ds(row + j, 2, stride=half), :]
                lattice_out[j, a, c] = pair.astype(jnp.bfloat16)
            for s in range(2):
                row = s * orb + a
                local_out[a, c, s : s + 1, :] = local_ref[
                    row : row + 1, c * times : c * times + block
                ]
    for p in range(2):
        pseudo_out[p] = pseudo_ref[:, p * states : (p + 1) * states]


def per_device(
    n_hist,
    n_ka,
    step_index,
    band_energy,
    kernel_row,
    lattice_history,
    diagonal_inverse,
    multiplicity,
    state_energy,
    connection,
    predicted_row,
    pseudo_history,
):
    block, orb, lanes = band_energy.shape
    times = lattice_history.shape[4]
    states = state_energy.shape[0]
    pairs = 2 * orb * orb
    rows = pairs * block
    per_tile = tile_rows // block
    width = -(-(orb * times + 1) // lane_count) * lane_count
    vmem = pl.BlockSpec(memory_space=pltpu.VMEM)
    f32, bf16 = jnp.float32, jnp.bfloat16
    dma = pltpu.SemaphoreType.DMA
    operands = (
        jnp.transpose(band_energy, (1, 0, 2)),
        jnp.transpose(kernel_row, (0, 2, 3, 1, 4)),
        lattice_history,
        jnp.transpose(diagonal_inverse, (1, 2, 0, 3)),
        multiplicity[None],
        state_energy[None],
        jnp.transpose(connection),
        jnp.transpose(predicted_row, (0, 2, 1)),
        jnp.transpose(pseudo_history, (0, 1, 3, 2)),
    )
    results = pl.pallas_call(
        functools.partial(kernel, n_hist, n_ka),
        out_shape=(
            pltpu.VMEM((rows, lanes), f32),
            pltpu.VMEM((group_rows, width), f32),
            pltpu.VMEM((block, 2 * states), f32),
        ),
        in_specs=[pl.BlockSpec(memory_space=pltpu.SMEM)]
        + [pl.BlockSpec(memory_space=pl.ANY)] * len(operands),
        out_specs=(vmem, vmem, vmem),
        scratch_shapes=[
            pltpu.VMEM((n_hist, *operands[0].shape), f32),
            *[pltpu.VMEM(array.shape, array.dtype) for array in operands[1:]],
            pltpu.VMEM((block, orb, orb, 2, lanes), f32),
            pltpu.VMEM((orb, group_rows, lanes), f32),
            pltpu.VMEM((orb, group_rows, lanes), f32),
            pltpu.VMEM((orb, times, lanes), f32),
            pltpu.VMEM((2, orb, times, lanes), f32),
            pltpu.VMEM((group_rows, width), f32),
            pltpu.VMEM((n_hist, n_ka, group_rows, width), f32),
            pltpu.VMEM((group_rows, width), f32),
            pltpu.VMEM((group_rows, width), f32),
            pltpu.VMEM((n_ka - 1, group_rows, width), f32),
            pltpu.VMEM((n_hist, rows, lanes), bf16),
            pltpu.VMEM((n_hist, rows, lanes), bf16),
            pltpu.VMEM((n_hist, 4 * group_rows, lanes), bf16),
            pltpu.VMEM((n_hist, 4 * group_rows, lanes), bf16),
            pltpu.VMEM((times * block, lanes), f32),
            pltpu.VMEM((2 * times, lanes), f32),
            pltpu.VMEM((2 * states, 2 * orb * lanes), bf16),
            pltpu.VMEM((2 * width, 2 * block * states), bf16),
            pltpu.VMEM((per_tile, rows, lanes), f32),
            dma((len(operands) - 1 + block,)),
            *[dma] * 11,
            pltpu.SemaphoreType.REGULAR,
        ],
        compiler_params=pltpu.CompilerParams(collective_id=0, has_side_effects=True),
    )(
        step_index,
        *operands,
    )
    lattice, local, pseudo = pl.pallas_call(
        functools.partial(lay_out, times),
        out_shape=(
            jax.ShapeDtypeStruct((block, orb, orb, 2, lanes), bf16),
            jax.ShapeDtypeStruct((orb, orb, 2, block), f32),
            jax.ShapeDtypeStruct((2, block, states), f32),
        ),
        in_specs=[vmem] * 3,
        out_specs=(vmem, vmem, vmem),
        compiler_params=pltpu.CompilerParams(vmem_limit_bytes=layout_bytes),
    )(*results)
    return (
        jnp.transpose(lattice, (0, 3, 1, 2, 4)),
        jnp.transpose(local, (2, 0, 1, 3)),
        jnp.transpose(pseudo, (0, 2, 1)),
    )


def solution(mesh):
    in_specs = (
        P(),
        P("hist", None, "ka"),
        P("hist", None, None, None, "ka"),
        P("hist", None, None, None, None, "ka"),
        P(None, None, None, "ka"),
        P("ka"),
        P(),
        P(),
        P(None, None, "hist"),
        P("hist", None, None, None),
    )
    out_specs = (
        P("hist", None, None, None, "ka"),
        P(None, None, None, "hist"),
        P(None, None, "hist"),
    )
    return jax.shard_map(
        functools.partial(per_device, mesh.shape["hist"], mesh.shape["ka"]),
        mesh=mesh,
        in_specs=in_specs,
        out_specs=out_specs,
        check_vma=False,
    )
```

```python
import functools

import jax
import jax.numpy as jnp
from jax import lax
from jax.experimental import pallas as pl
from jax.experimental.pallas import tpu as pltpu
from jax.sharding import PartitionSpec as P

time_step = 0.05
coupling = 0.02
tile_rows = 16
group_rows = 8
lead = 2
lane_count = 128
layout_bytes = 4 * 1024 * 1024


def two_parts(values):
    upper = values.astype(jnp.bfloat16).astype(jnp.float32)
    return upper, values - upper


def stacked(values):
    return jnp.concatenate(two_parts(values), axis=0).astype(jnp.bfloat16)


def dot(left, right, contract):
    return lax.dot_general(
        left,
        right,
        (((1,), (contract,)), ((), ())),
        preferred_element_type=jnp.float32,
    )


def folded(values):
    return values[:group_rows] + values[group_rows:]


def minus_sine_cosine(angle):
    quarter = jnp.floor(angle * 0.6366197723675814 + 0.5)
    rest = angle - quarter * 1.5703125
    rest = rest - quarter * 4.837512969970703125e-4
    rest = rest - quarter * 7.54978995489188216e-8
    square = rest * rest
    sine = (-1.9515295891e-4 * square + 8.3321608736e-3) * square - 1.6666654611e-1
    sine = sine * square * rest + rest
    cosine = (2.443315711809948e-5 * square - 1.388731625493765e-3) * square
    cosine = (cosine + 4.166664568298827e-2) * square * square - 0.5 * square + 1.0
    half = jnp.floor(quarter * 0.5)
    odd = quarter - 2.0 * half > 0.5
    sign = 2.0 * (half - 2.0 * jnp.floor(half * 0.5)) - 1.0
    return sign * jnp.where(odd, cosine, sine), sign * jnp.where(odd, -sine, cosine)


def kernel(
    n_hist,
    n_ka,
    step_ref,
    band_any,
    krow_any,
    hist_any,
    dinv_any,
    mult_any,
    energy_any,
    conn_any,
    pred_any,
    pseudo_any,
    lattice_out,
    local_out,
    pseudo_out,
    band_recv,
    krow_ref,
    hist_ref,
    dinv_ref,
    mult_ref,
    energy_ref,
    conn_ref,
    pred_ref,
    pseudo_ref,
    kw,
    d_same,
    d_turn,
    band_all,
    free_all,
    vsend,
    vrecv,
    xsend,
    xfree,
    xrecv,
    psend,
    precv,
    csend,
    crecv,
    gsend,
    grecv,
    total,
    hist_p,
    hist_r,
    hits,
    mix,
    stage,
    load_sem,
    sent_energy,
    sent_sum,
    sent_direct,
    sent_column,
    sent_given,
    sent_part,
    sent_local,
    got_energy,
    got_sum,
    got_direct,
    got_column,
    got_given,
    got_part,
    got_local,
    opened,
):
    _, orb, block, lanes = band_recv.shape
    times = hist_ref.shape[4]
    states = energy_ref.shape[1]
    pairs = 2 * orb * orb
    rows = pairs * block
    per_tile = tile_rows // block
    width = vsend.shape[1]
    cols = orb * times
    f32, bf16 = jnp.float32, jnp.bfloat16
    me = lax.axis_index("hist")
    my_ka = lax.axis_index("ka")
    first = me * block

    barrier = pltpu.get_barrier_semaphore()

    def signal(sem, hist, ka):
        pl.semaphore_signal(
            sem, inc=1, device_id={"hist": hist, "ka": ka}, device_id_type=pl.DeviceIdType.MESH
        )

    def greet(target, carry):
        signal(barrier, target, my_ka)
        return carry

    lax.fori_loop(me + 1, n_hist, greet, 0)
    is_root = (my_ka == 0) & (me < lead)

    @pl.when(is_root)
    def _():
        def one(target, carry):
            for ka in range(1, n_ka):
                signal(barrier, target, ka)
            return carry

        lax.fori_loop(me + 1, n_hist, one, 0)

    for ka in range(n_ka):

        @pl.when((me > 0) | (my_ka != ka))
        def _():
            signal(barrier, 0, ka)

    def load(source, target, place):
        copy = pltpu.make_async_copy(source, target, load_sem.at[place])
        copy.start()
        return copy

    pairs_in = [(krow_any, krow_ref), (dinv_any, dinv_ref), (mult_any, mult_ref)]
    pairs_in += [(hist_any.at[m], hist_ref.at[m]) for m in range(block)]
    pairs_in += [
        (pred_any, pred_ref),
        (pseudo_any, pseudo_ref),
        (energy_any, energy_ref),
        (conn_any, conn_ref),
        (band_any, band_recv.at[me]),
    ]
    loads = [load(source, target, i) for i, (source, target) in enumerate(pairs_in)]
    small, large, others = loads[:3], loads[3 : 3 + block], loads[3 + block :]

    def remote(src, dst, send_sem, recv_sem, hist, ka):
        return pltpu.make_async_remote_copy(
            src_ref=src,
            dst_ref=dst,
            send_sem=send_sem,
            recv_sem=recv_sem,
            device_id={"hist": hist, "ka": ka},
            device_id_type=pl.DeviceIdType.MESH,
        )

    def energy_copy(target):
        return remote(band_any, band_recv.at[me], sent_energy, got_energy, target, my_ka)

    def sum_copy(target):
        return remote(vsend, vrecv.at[me, my_ka], sent_sum, got_sum, target, my_ka)

    def direct_copy(target):
        return remote(vsend, vrecv.at[me, my_ka], sent_direct, got_direct, target, 0)

    def part_copy(target):
        return remote(psend.at[target], precv.at[me], sent_part, got_part, target, my_ka)

    def column_copy(target):
        return remote(csend.at[target], crecv.at[me], sent_column, got_column, target, my_ka)

    def given_copy(target):
        return remote(gsend, grecv.at[me], sent_given, got_given, target, my_ka)

    def local_copy(src, hop):
        target = lax.rem(my_ka + hop, n_ka)
        return remote(src, xrecv.at[hop - 1], sent_local, got_local, me, target)

    def give(copy, stop):
        def one(target, carry):
            copy(target).start()
            return carry

        lax.fori_loop(0, stop, one, 0)

    def wait_bytes(ref, sem):
        pltpu.make_async_copy(ref, ref, sem).wait()

    def take(ref, sem):
        for t in range(n_hist - 1):

            @pl.when(me == t)
            def _():
                wait_bytes(ref.at[pl.ds(t + 1, n_hist - 1 - t)], sem)

    current = step_ref[0]
    weight = [
        jnp.where(first + m == 0, 0.5, 1.0) * jnp.where(first + m < current, 1.0, 0.0)
        for m in range(block)
    ]
    d_same[...] = jnp.zeros(d_same.shape, f32)
    d_turn[...] = jnp.zeros(d_turn.shape, f32)
    vsend[...] = jnp.zeros(vsend.shape, f32)

    direct = jnp.where(my_ka == 0, 0, jnp.minimum(me, lead))
    with jax.named_scope("WBAR"):

        @pl.when(me > 0)
        def _():
            pl.semaphore_wait(barrier, me + direct)

    give(energy_copy, me)

    with jax.named_scope("LOAD"):
        for copy in small:
            copy.wait()
    mult = mult_ref[...].astype(f32)
    for m in range(block):
        kw[m] = krow_ref[m].astype(f32) * weight[m]
    for a in range(orb):
        for c in range(orb):
            d_re = dinv_ref[a, c, 0:1, :] * mult
            d_im = dinv_ref[a, c, 1:2, :] * mult
            d_same[c, a : a + 1, :] = d_re
            d_same[c, orb + a : orb + a + 1, :] = d_im
            d_turn[c, a : a + 1, :] = -d_im
            d_turn[c, orb + a : orb + a + 1, :] = d_re
    same = [d_same[c] for c in range(orb)]
    turn = [d_turn[c] for c in range(orb)]
    left = []
    for m in range(block):
        left.append([])
        for b in range(orb):
            plain = jnp.zeros((group_rows, lanes), f32)
            turned = plain
            for c in range(orb):
                k_re = kw[m, c, b, 0:1, :]
                k_im = kw[m, c, b, 1:2, :]
                plain += same[c] * k_re + turn[c] * k_im
                turned += turn[c] * k_re - same[c] * k_im
            left[m] += [stacked(plain), stacked(turned)]
    sums = jnp.zeros((2 * group_rows, cols), f32)
    for m in range(block):
        with jax.named_scope("LOADH"):
            large[m].wait()
        right = [hist_ref[m, p, b].reshape(cols, lanes) for b in range(orb) for p in range(2)]
        sums += dot(jnp.concatenate(left[m], axis=1), jnp.concatenate(right, axis=1), 1)
    with jax.named_scope("VSEND"):
        vsend[:, :cols] = folded(sums)

        give(direct_copy, direct)
        give(sum_copy, me)

    with jax.named_scope("PC"):
        for copy in others:
            copy.wait()
        half = block * block
        for m in range(block):
            h_re = pseudo_ref[m, 0].astype(f32)
            h_im = pseudo_ref[m, 1].astype(f32)
            both = jnp.concatenate([h_re, h_im], axis=1)
            for t in range(n_hist):
                hist_p[t * half + m * block : t * half + (m + 1) * block, :] = both[
                    t * block : (t + 1) * block
                ]
        for t in range(n_hist):
            csend[t] = hist_p[t * half : (t + 1) * half, :].astype(bf16)
        gsend[...] = jnp.concatenate([pred_ref[0], pred_ref[1]], axis=1)
    give(column_copy, me)
    give(given_copy, me)

    def one_tile(tile, carry):
        at = pl.ds(pl.multiple_of(tile * tile_rows, tile_rows), tile_rows)
        zero = jnp.zeros((tile_rows, lanes), f32)
        real = [[zero] * orb for _ in range(orb)]
        imag = [[zero] * orb for _ in range(orb)]
        for m in range(block):
            for b in range(orb):
                k_re = [kw[m, a, b, 0:1, :] for a in range(orb)]
                k_im = [kw[m, a, b, 1:2, :] for a in range(orb)]
                for c in range(orb):
                    h_re = hist_ref[m, 0, b, c, at, :].astype(f32)
                    h_im = hist_ref[m, 1, b, c, at, :].astype(f32)
                    for a in range(orb):
                        real[a][c] += k_re[a] * h_re - k_im[a] * h_im
                        imag[a][c] += k_re[a] * h_im + k_im[a] * h_re
        for a in range(orb):
            for c in range(orb):
                out_re, out_im = zero, zero
                for b in range(orb):
                    d_re = dinv_ref[a, b, 0:1, :]
                    d_im = dinv_ref[a, b, 1:2, :]
                    out_re += d_re * real[b][c] - d_im * imag[b][c]
                    out_im += d_re * imag[b][c] + d_im * real[b][c]
                for s, value in enumerate((out_re, out_im)):
                    row = ((s * orb + a) * orb + c) * block
                    for d in range(per_tile):
                        stage[d, row : row + block, :] = value[d * block : (d + 1) * block]
        for d in range(per_tile):
            target = tile * per_tile + d
            psend[target] = stage[d].astype(bf16)

            @pl.when(target < me)
            def _():
                part_copy(target).start()

        return carry

    with jax.named_scope("TILES"):
        lax.fori_loop(0, first // tile_rows + 1, one_tile, 0)

    crecv[me] = csend[me]
    grecv[me] = gsend[...]
    row_of = lax.broadcasted_iota(jnp.int32, (times, lanes), 0)
    lane_of = lax.broadcasted_iota(jnp.int32, (group_rows, width), 1)
    group_of = lax.broadcasted_iota(jnp.int32, (group_rows, width), 0)
    conn = jnp.concatenate([conn_ref[...], conn_ref[...]], axis=1)
    reach = lax.broadcasted_iota(jnp.int32, (2 * states, 2 * states), 0)
    for a in range(orb):
        for p in range(2):
            at = (2 * a + p) * lanes
            hit = jnp.where(conn[2 * a : 2 * a + 1] + p * states == reach, 1.0, 0.0) + jnp.where(
                conn[2 * a + 1 : 2 * a + 2] + p * states == reach, 1.0, 0.0
            )
            hits[:, at : at + 2 * states] = hit.astype(bf16)
    mix[cols:width, :] = jnp.zeros((width - cols, mix.shape[1]), bf16)
    mix[width + cols :, :] = jnp.zeros((width - cols, mix.shape[1]), bf16)
    line = lax.broadcasted_iota(jnp.int32, (block, 2 * states), 0) + first
    lane = lax.broadcasted_iota(jnp.int32, (block, 2 * states), 1)
    energies = jnp.concatenate([energy_ref[...], energy_ref[...]], axis=1)
    spins = energies * time_step * (current - line).astype(f32)
    free_pseudo = jnp.where(lane < states, *minus_sine_cosine(spins))
    free_pseudo = free_pseudo * jnp.where(line <= current, 1.0, 0.0)
    count = jnp.sum(mult, axis=1, keepdims=True)
    step_row = lax.broadcasted_iota(jnp.int32, (times, times), 0)
    step_col = lax.broadcasted_iota(jnp.int32, (times, times), 1)
    later = jnp.where((step_col >= step_row) & (step_col < current), 1.0, 0.0).astype(bf16)
    inside = (row_of <= current) & (row_of >= first)

    with jax.named_scope("WOPEN"):

        @pl.when(me == 0)
        def _():
            pl.semaphore_wait(barrier, n_hist * n_ka - 1)

            def one(target, carry):
                signal(opened, target, my_ka)
                return carry

            lax.fori_loop(1, n_hist, one, 0)

    with jax.named_scope("TAKEE"):
        take(band_recv, got_energy)
    with jax.named_scope("FREE"):
        for t in range(n_hist):
            for c in range(orb):
                band_all[c, t * block : (t + 1) * block, :] = band_recv[t, c]
        rest = jnp.concatenate(
            [jnp.where(row_of >= first, band_all[c], 0.0) for c in range(orb)], axis=1
        )
        bands = []
        for _ in range(3):
            bands.append(rest.astype(bf16))
            rest = rest - bands[-1].astype(f32)
        angle = dot(
            jnp.concatenate([later] * 3, axis=1), jnp.concatenate(bands, axis=0), 0
        )
        angle = angle * time_step
        pieces = []
        for c in range(orb):
            part = angle[:, c * lanes : (c + 1) * lanes]
            free_re, free_im = minus_sine_cosine(part)
            free_re = jnp.where(inside, free_re, 0.0)
            free_im = jnp.where(inside, free_im, 0.0)
            free_all[0, c] = free_re
            free_all[1, c] = free_im
            two_re, two_im = two_parts(free_re), two_parts(free_im)
            right = jnp.concatenate([two_re[0], two_im[0], two_re[1], two_im[1]], axis=1)
            left = jnp.concatenate([stacked(same[c]), stacked(turn[c])] * 2, axis=1)
            pieces.append(folded(dot(left, right.astype(bf16), 1)))
        pieces.append(jnp.zeros((group_rows, width - cols), f32))
        own = jnp.concatenate(pieces, axis=1) + vsend[...]
        own = jnp.where(lane_of == cols, count, own)

    xfree[...] = own
    with jax.named_scope("WOPEN2"):

        @pl.when(me > 0)
        def _():
            pl.semaphore_wait(opened, 1)

    for hop in range(1, n_ka):
        target = lax.rem(my_ka + hop, n_ka)

        @pl.when((me < lead) & (target == 0))
        def _():
            local_copy(xfree, hop).start()

    with jax.named_scope("TAKEV"):

        take(vrecv.at[:, my_ka], got_sum)

    xsend[...] = lax.fori_loop(
        me + 1, n_hist, lambda source, value: value + vrecv[source, my_ka], own
    )
    for hop in range(1, n_ka):
        target = lax.rem(my_ka + hop, n_ka)

        @pl.when((me >= lead) | (target != 0))
        def _():
            local_copy(xsend, hop).start()

    with jax.named_scope("TOTAL"):
        at = pl.ds(pl.multiple_of(first, block), block)
        for c in range(orb):
            f_re = free_all[0, c, at, :]
            f_im = free_all[1, c, at, :]
            for a in range(orb):
                d_re = dinv_ref[a, c, 0:1, :]
                d_im = dinv_ref[a, c, 1:2, :]
                row = (a * orb + c) * block
                total[row : row + block, :] = d_re * f_re - d_im * f_im
                row += rows // 2
                total[row : row + block, :] = d_re * f_im + d_im * f_re

    with jax.named_scope("TAKEC"):
        take(crecv, got_column)
        take(grecv, got_given)
    with jax.named_scope("MIX"):
        for t in range(n_hist):
            hist_p[t * half : (t + 1) * half, :] = crecv[t].astype(f32)
            hist_r[t * block : (t + 1) * block, :] = grecv[t]
        given = jnp.where(row_of >= first, hist_r[...], 0.0)
        given = jnp.concatenate(two_parts(given), axis=0).astype(bf16)
        reached = dot(given, hits[...], 0)
        reached = reached[:times] + reached[times:]
        row_weight = jnp.where(row_of == 0, 0.5 * coupling, coupling)
        row_weight = row_weight * jnp.where(row_of < current, 1.0, 0.0)
        sign = jnp.where(
            lax.broadcasted_iota(jnp.int32, (times, lanes), 1) < states, -1.0, 1.0
        )
        r_re = [reached[:, 2 * a * lanes : (2 * a + 1) * lanes] * row_weight for a in range(orb)]
        r_im = [
            reached[:, (2 * a + 1) * lanes : (2 * a + 2) * lanes] * row_weight for a in range(orb)
        ]
        for j in range(block):
            plain = jnp.where(row_of >= first, hist_p[pl.ds(j, times, stride=block), :], 0.0)
            turned = pltpu.roll(plain, states, 1) * sign
            at = slice(j * lanes, (j + 1) * lanes)
            for a in range(orb):
                low, high = a * times, (a + 1) * times
                mix[low:high, at] = (r_re[a] * plain + r_im[a] * turned).astype(bf16)
                mix[width + low : width + high, at] = (
                    r_re[a] * turned - r_im[a] * plain
                ).astype(bf16)

    with jax.named_scope("TAKEP"):
        take(precv, got_part)
        total[...] = lax.fori_loop(
            me + 1,
            n_hist,
            lambda source, value: value + precv[source].astype(f32),
            total[...] + psend[me].astype(f32),
        )
        for a in range(orb):
            for c in range(orb):
                for j in range(block):
                    at = pl.ds((a * orb + c) * block + j, 2, stride=rows // 2)
                    lattice_out[j, a, c] = total[at, :].astype(bf16)

    with jax.named_scope("TAKED"):

        @pl.when(is_root)
        def _():
            for t in range(min(lead, n_hist - 1)):

                @pl.when(me == t)
                def _():
                    far = vrecv.at[pl.ds(t + 1, n_hist - 1 - t), pl.ds(1, n_ka - 1)]
                    wait_bytes(far, got_direct)

            def one(source, value):
                for ka in range(1, n_ka):
                    value = value + vrecv[source, ka]
                return value

            xfree[...] = lax.fori_loop(me + 1, n_hist, one, xsend[...])

    with jax.named_scope("TAKEX"):
        wait_bytes(xrecv, got_local)
        local = jnp.where(is_root, xfree[...], xsend[...])
        for hop in range(1, n_ka):
            local = local + xrecv[hop - 1]
    with jax.named_scope("FINAL"):
        scale = 1.0 / local[:, cols : cols + 1]
        picked = jnp.where(lane_of // times == lax.rem(group_of, orb), local, 0.0)
        picked = jnp.concatenate(
            [jnp.where(group_of < orb, picked, 0.0), jnp.where(group_of < orb, 0.0, picked)], axis=1
        )
        sums = folded(dot(stacked(picked), mix[...], 0))
        sums = jnp.sum(sums, axis=0, keepdims=True)
        for j in range(block):
            row = free_pseudo[j : j + 1] + sums[:, j * lanes : (j + 1) * lanes] * scale[:1]
            for p in range(2):
                pseudo_out[p, j : j + 1, :] = row[:, p * states : (p + 1) * states]
        local = local * scale
        for c in range(orb):
            own = pltpu.roll(local, width - first - c * times, 1)[:, :block]
            for a in range(orb):
                for p in range(2):
                    local_out[a, c, p : p + 1, :] = own[p * orb + a : p * orb + a + 1]

    with jax.named_scope("SETTLE"):
        for t in range(1, n_hist):

            @pl.when(me == t)
            def _():
                wait_bytes(band_recv.at[pl.ds(0, t)], sent_energy)
                wait_bytes(vrecv.at[pl.ds(0, t), 0], sent_sum)
                wait_bytes(csend.at[pl.ds(0, t)], sent_column)
                wait_bytes(grecv.at[pl.ds(0, t)], sent_given)
                wait_bytes(psend.at[pl.ds(0, t)], sent_part)

        for t in range(1, lead + 1):

            @pl.when(direct == t)
            def _():
                wait_bytes(vrecv.at[pl.ds(0, t), 0], sent_direct)

        wait_bytes(xrecv, sent_local)


def put_out(*refs):
    sources, targets, sems = refs[:3], refs[3:6], refs[6]
    copies = [
        pltpu.make_async_copy(source, target, sems.at[i])
        for i, (source, target) in enumerate(zip(sources, targets))
    ]
    for copy in copies:
        copy.start()
    for copy in copies:
        copy.wait()


def per_device(
    n_hist,
    n_ka,
    step_index,
    band_energy,
    kernel_row,
    lattice_history,
    diagonal_inverse,
    multiplicity,
    state_energy,
    connection,
    predicted_row,
    pseudo_history,
):
    block, orb, lanes = band_energy.shape
    times = lattice_history.shape[4]
    states = state_energy.shape[0]
    pairs = 2 * orb * orb
    rows = pairs * block
    per_tile = tile_rows // block
    width = -(-(orb * times + 1) // lane_count) * lane_count
    vmem = pl.BlockSpec(memory_space=pltpu.VMEM)
    f32, bf16 = jnp.float32, jnp.bfloat16
    dma = pltpu.SemaphoreType.DMA
    operands = (
        jnp.transpose(band_energy, (1, 0, 2)),
        jnp.transpose(kernel_row, (0, 2, 3, 1, 4)),
        lattice_history,
        jnp.transpose(diagonal_inverse, (1, 2, 0, 3)),
        multiplicity[None],
        state_energy[None],
        jnp.transpose(connection),
        jnp.transpose(predicted_row, (0, 2, 1)),
        jnp.transpose(pseudo_history, (0, 1, 3, 2)),
    )
    results = pl.pallas_call(
        functools.partial(kernel, n_hist, n_ka),
        out_shape=(
            pltpu.VMEM((block, orb, orb, 2, lanes), bf16),
            pltpu.VMEM((orb, orb, 2, block), f32),
            pltpu.VMEM((2, block, states), f32),
        ),
        in_specs=[pl.BlockSpec(memory_space=pltpu.SMEM)]
        + [pl.BlockSpec(memory_space=pl.ANY)] * len(operands),
        out_specs=(vmem, vmem, vmem),
        scratch_shapes=[
            pltpu.VMEM((n_hist, *operands[0].shape), f32),
            *[pltpu.VMEM(array.shape, array.dtype) for array in operands[1:]],
            pltpu.VMEM((block, orb, orb, 2, lanes), f32),
            pltpu.VMEM((orb, group_rows, lanes), f32),
            pltpu.VMEM((orb, group_rows, lanes), f32),
            pltpu.VMEM((orb, times, lanes), f32),
            pltpu.VMEM((2, orb, times, lanes), f32),
            pltpu.VMEM((group_rows, width), f32),
            pltpu.VMEM((n_hist, n_ka, group_rows, width), f32),
            pltpu.VMEM((group_rows, width), f32),
            pltpu.VMEM((group_rows, width), f32),
            pltpu.VMEM((n_ka - 1, group_rows, width), f32),
            pltpu.VMEM((n_hist, rows, lanes), bf16),
            pltpu.VMEM((n_hist, rows, lanes), bf16),
            pltpu.VMEM((n_hist, block * block, lanes), bf16),
            pltpu.VMEM((n_hist, block * block, lanes), bf16),
            pltpu.VMEM((block, 2 * states), f32),
            pltpu.VMEM((n_hist, block, 2 * states), f32),
            pltpu.VMEM((rows, lanes), f32),
            pltpu.VMEM((times * block, lanes), f32),
            pltpu.VMEM((times, lanes), f32),
            pltpu.VMEM((2 * states, 2 * orb * lanes), bf16),
            pltpu.VMEM((2 * width, 2 * block * states), bf16),
            pltpu.VMEM((per_tile, rows, lanes), f32),
            dma((len(operands) - 1 + block,)),
            *[dma] * 14,
            pltpu.SemaphoreType.REGULAR,
        ],
        compiler_params=pltpu.CompilerParams(collective_id=0, has_side_effects=True),
    )(
        step_index,
        *operands,
    )
    lattice, local, pseudo = pl.pallas_call(
        put_out,
        out_shape=tuple(jax.ShapeDtypeStruct(array.shape, array.dtype) for array in results),
        in_specs=[vmem] * 3,
        out_specs=[pl.BlockSpec(memory_space=pl.ANY)] * 3,
        scratch_shapes=[dma((3,))],
        compiler_params=pltpu.CompilerParams(vmem_limit_bytes=layout_bytes),
    )(*results)
    return (
        jnp.transpose(lattice, (0, 3, 1, 2, 4)),
        jnp.transpose(local, (2, 0, 1, 3)),
        jnp.transpose(pseudo, (0, 2, 1)),
    )


def solution(mesh):
    in_specs = (
        P(),
        P("hist", None, "ka"),
        P("hist", None, None, None, "ka"),
        P("hist", None, None, None, None, "ka"),
        P(None, None, None, "ka"),
        P("ka"),
        P(),
        P(),
        P(None, None, "hist"),
        P("hist", None, None, None),
    )
    out_specs = (
        P("hist", None, None, None, "ka"),
        P(None, None, None, "hist"),
        P(None, None, "hist"),
    )
    return jax.shard_map(
        functools.partial(per_device, mesh.shape["hist"], mesh.shape["ka"]),
        mesh=mesh,
        in_specs=in_specs,
        out_specs=out_specs,
        check_vma=False,
    )
```

```python
import functools

import jax
import jax.numpy as jnp
from jax import lax
from jax.experimental import pallas as pl
from jax.experimental.pallas import tpu as pltpu
from jax.sharding import PartitionSpec as P

time_step = 0.05
coupling = 0.02
tile_rows = 16
group_rows = 8
lead = 2
lane_count = 128
layout_bytes = 4 * 1024 * 1024


def two_parts(values):
    upper = values.astype(jnp.bfloat16).astype(jnp.float32)
    return upper, values - upper


def stacked(values):
    return jnp.concatenate(two_parts(values), axis=0).astype(jnp.bfloat16)


def dot(left, right, contract):
    return lax.dot_general(
        left,
        right,
        (((1,), (contract,)), ((), ())),
        preferred_element_type=jnp.float32,
    )


def folded(values):
    return values[:group_rows] + values[group_rows:]


def minus_sine_cosine(angle):
    quarter = jnp.floor(angle * 0.6366197723675814 + 0.5)
    rest = angle - quarter * 1.5703125
    rest = rest - quarter * 4.837512969970703125e-4
    rest = rest - quarter * 7.54978995489188216e-8
    square = rest * rest
    sine = (-1.9515295891e-4 * square + 8.3321608736e-3) * square - 1.6666654611e-1
    sine = sine * square * rest + rest
    cosine = (2.443315711809948e-5 * square - 1.388731625493765e-3) * square
    cosine = (cosine + 4.166664568298827e-2) * square * square - 0.5 * square + 1.0
    half = jnp.floor(quarter * 0.5)
    odd = quarter - 2.0 * half > 0.5
    sign = 2.0 * (half - 2.0 * jnp.floor(half * 0.5)) - 1.0
    return sign * jnp.where(odd, cosine, sine), sign * jnp.where(odd, -sine, cosine)


def kernel(
    n_hist,
    n_ka,
    step_ref,
    band_any,
    krow_any,
    hist_any,
    dinv_any,
    mult_any,
    energy_any,
    conn_any,
    pred_any,
    pseudo_any,
    lattice_out,
    local_out,
    pseudo_out,
    band_recv,
    krow_ref,
    hist_ref,
    dinv_ref,
    mult_ref,
    energy_ref,
    conn_ref,
    pred_ref,
    pseudo_ref,
    kw,
    d_both,
    d_far,
    band_far,
    band_all,
    free_all,
    vsend,
    vrecv,
    wsend,
    wrecv,
    own_far,
    xsend,
    xfree,
    xsum,
    xrecv,
    psend,
    precv,
    csend,
    crecv,
    gsend,
    grecv,
    total,
    hist_p,
    hist_r,
    hits,
    mix,
    stage,
    load_sem,
    sent_energy,
    sent_sum,
    sent_direct,
    sent_band,
    sent_pack,
    sent_own,
    sent_column,
    sent_given,
    sent_part,
    sent_local,
    got_energy,
    got_sum,
    got_direct,
    got_band,
    got_pack,
    got_own,
    got_column,
    got_given,
    got_part,
    got_local,
    opened,
):
    _, orb, block, lanes = band_recv.shape
    times = hist_ref.shape[4]
    states = energy_ref.shape[1]
    pairs = 2 * orb * orb
    rows = pairs * block
    per_tile = tile_rows // block
    width = vsend.shape[1]
    cols = orb * times
    f32, bf16 = jnp.float32, jnp.bfloat16
    me = lax.axis_index("hist")
    my_ka = lax.axis_index("ka")
    first = me * block

    barrier = pltpu.get_barrier_semaphore()

    def signal(sem, hist, ka):
        pl.semaphore_signal(
            sem, inc=1, device_id={"hist": hist, "ka": ka}, device_id_type=pl.DeviceIdType.MESH
        )

    def greet(target, carry):
        signal(barrier, target, my_ka)
        return carry

    lax.fori_loop(me + 1, n_hist, greet, 0)
    is_root = (my_ka == 0) & (me < lead)

    @pl.when(is_root)
    def _():
        def one(target, carry):
            for ka in range(1, n_ka):
                signal(barrier, target, ka)
            return carry

        lax.fori_loop(jnp.maximum(me, 1), n_hist, one, 0)

    for ka in range(n_ka):

        @pl.when((me > 0) | (my_ka != ka))
        def _():
            signal(barrier, 0, ka)

    def load(source, target, place):
        copy = pltpu.make_async_copy(source, target, load_sem.at[place])
        copy.start()
        return copy

    pairs_in = [(krow_any, krow_ref), (dinv_any, dinv_ref), (mult_any, mult_ref)]
    pairs_in += [(hist_any.at[m], hist_ref.at[m]) for m in range(block)]
    pairs_in += [
        (pred_any, pred_ref),
        (pseudo_any, pseudo_ref),
        (energy_any, energy_ref),
        (conn_any, conn_ref),
        (band_any, band_recv.at[me]),
    ]
    loads = [load(source, target, i) for i, (source, target) in enumerate(pairs_in)]
    small, large, others = loads[:3], loads[3 : 3 + block], loads[3 + block :]

    def remote(src, dst, send_sem, recv_sem, hist, ka):
        return pltpu.make_async_remote_copy(
            src_ref=src,
            dst_ref=dst,
            send_sem=send_sem,
            recv_sem=recv_sem,
            device_id={"hist": hist, "ka": ka},
            device_id_type=pl.DeviceIdType.MESH,
        )

    def energy_copy(target):
        return remote(band_any, band_recv.at[me], sent_energy, got_energy, target, my_ka)

    def sum_copy(target):
        return remote(vsend, vrecv.at[me, my_ka], sent_sum, got_sum, target, my_ka)

    def direct_copy(target):
        return remote(wsend, wrecv.at[me, my_ka], sent_direct, got_direct, target, 0)

    def band_copy(target):
        return remote(band_any, band_far.at[me], sent_band, got_band, target, 0)

    def pack_copy():
        return remote(d_both, d_far, sent_pack, got_pack, me, 0)

    def own_copy():
        return remote(xfree, own_far, sent_own, got_own, me, 0)

    def part_copy(target):
        return remote(psend.at[target], precv.at[me], sent_part, got_part, target, my_ka)

    def column_copy(target):
        return remote(csend.at[target], crecv.at[me], sent_column, got_column, target, my_ka)

    def given_copy(target):
        return remote(gsend, grecv.at[me], sent_given, got_given, target, my_ka)

    def local_copy(src, hop):
        target = lax.rem(my_ka + hop, n_ka)
        return remote(src, xrecv.at[hop - 1], sent_local, got_local, me, target)

    def give(copy, start, stop):
        def one(target, carry):
            copy(target).start()
            return carry

        lax.fori_loop(start, stop, one, 0)

    def wait_bytes(ref, sem):
        pltpu.make_async_copy(ref, ref, sem).wait()

    def take(ref, sem):
        for t in range(n_hist - 1):

            @pl.when(me == t)
            def _():
                wait_bytes(ref.at[pl.ds(t + 1, n_hist - 1 - t)], sem)

    current = step_ref[0]
    weight = [
        jnp.where(first + m == 0, 0.5, 1.0) * jnp.where(first + m < current, 1.0, 0.0)
        for m in range(block)
    ]
    d_both[...] = jnp.zeros(d_both.shape, f32)
    vsend[...] = jnp.zeros(vsend.shape, f32)
    wsend[...] = jnp.zeros(wsend.shape, bf16)

    near = jnp.minimum(me, lead)
    direct = jnp.where(my_ka == 0, 0, near)
    beside_root = (my_ka != 0) & (me < lead)
    is_far = my_ka == n_ka - 1
    banded = jnp.where(is_far, near, 0)
    early = jnp.where(my_ka == 0, near, 0)
    with jax.named_scope("WBAR"):

        @pl.when(me > 0)
        def _():
            pl.semaphore_wait(barrier, me + direct + jnp.where(beside_root, 1, 0))

    give(band_copy, 0, banded)
    give(energy_copy, 0, me)

    with jax.named_scope("LOAD"):
        for copy in small:
            copy.wait()
    mult = mult_ref[...].astype(f32)
    for m in range(block):
        kw[m] = krow_ref[m].astype(f32) * weight[m]
    for a in range(orb):
        for c in range(orb):
            d_re = dinv_ref[a, c, 0:1, :] * mult
            d_im = dinv_ref[a, c, 1:2, :] * mult
            d_both[0, c, a : a + 1, :] = d_re
            d_both[0, c, orb + a : orb + a + 1, :] = d_im
            d_both[1, c, a : a + 1, :] = -d_im
            d_both[1, c, orb + a : orb + a + 1, :] = d_re
    same = [d_both[0, c] for c in range(orb)]
    turn = [d_both[1, c] for c in range(orb)]
    left = []
    for m in range(block):
        left.append([])
        for b in range(orb):
            plain = jnp.zeros((group_rows, lanes), f32)
            turned = plain
            for c in range(orb):
                k_re = kw[m, c, b, 0:1, :]
                k_im = kw[m, c, b, 1:2, :]
                plain += same[c] * k_re + turn[c] * k_im
                turned += turn[c] * k_re - same[c] * k_im
            left[m] += [stacked(plain), stacked(turned)]
    sums = jnp.zeros((2 * group_rows, cols), f32)
    for m in range(block):
        with jax.named_scope("LOADH"):
            large[m].wait()
        right = [hist_ref[m, p, b].reshape(cols, lanes) for b in range(orb) for p in range(2)]
        sums += dot(jnp.concatenate(left[m], axis=1), jnp.concatenate(right, axis=1), 1)
    with jax.named_scope("VSEND"):
        sums = folded(sums)
        vsend[:, :cols] = sums
        wsend[:, :cols] = sums.astype(bf16)
        give(direct_copy, 0, direct)
        give(sum_copy, 0, me)

    with jax.named_scope("PC"):
        for copy in others:
            copy.wait()
        half = block * block
        for m in range(block):
            h_re = pseudo_ref[m, 0].astype(f32)
            h_im = pseudo_ref[m, 1].astype(f32)
            both = jnp.concatenate([h_re, h_im], axis=1)
            for t in range(n_hist):
                hist_p[t * half + m * block : t * half + (m + 1) * block, :] = both[
                    t * block : (t + 1) * block
                ]
        for t in range(n_hist):
            csend[t] = hist_p[t * half : (t + 1) * half, :].astype(bf16)
        gsend[...] = jnp.concatenate([pred_ref[0], pred_ref[1]], axis=1)
    give(column_copy, 0, near)
    give(given_copy, 0, near)

    def one_tile(tile, carry):
        at = pl.ds(pl.multiple_of(tile * tile_rows, tile_rows), tile_rows)
        zero = jnp.zeros((tile_rows, lanes), f32)
        real = [[zero] * orb for _ in range(orb)]
        imag = [[zero] * orb for _ in range(orb)]
        for m in range(block):
            for b in range(orb):
                k_re = [kw[m, a, b, 0:1, :] for a in range(orb)]
                k_im = [kw[m, a, b, 1:2, :] for a in range(orb)]
                for c in range(orb):
                    h_re = hist_ref[m, 0, b, c, at, :].astype(f32)
                    h_im = hist_ref[m, 1, b, c, at, :].astype(f32)
                    for a in range(orb):
                        real[a][c] += k_re[a] * h_re - k_im[a] * h_im
                        imag[a][c] += k_re[a] * h_im + k_im[a] * h_re
        for a in range(orb):
            for c in range(orb):
                out_re, out_im = zero, zero
                for b in range(orb):
                    d_re = dinv_ref[a, b, 0:1, :]
                    d_im = dinv_ref[a, b, 1:2, :]
                    out_re += d_re * real[b][c] - d_im * imag[b][c]
                    out_im += d_re * imag[b][c] + d_im * real[b][c]
                for s, value in enumerate((out_re, out_im)):
                    row = ((s * orb + a) * orb + c) * block
                    for d in range(per_tile):
                        stage[d, row : row + block, :] = value[d * block : (d + 1) * block]
        for d in range(per_tile):
            target = tile * per_tile + d
            psend[target] = stage[d].astype(bf16)

            @pl.when(target < early)
            def _():
                part_copy(target).start()

        return carry

    with jax.named_scope("TILES"):
        lax.fori_loop(0, first // tile_rows + 1, one_tile, 0)

    crecv[me] = csend[me]
    grecv[me] = gsend[...]
    row_of = lax.broadcasted_iota(jnp.int32, (times, lanes), 0)
    lane_of = lax.broadcasted_iota(jnp.int32, (group_rows, width), 1)
    group_of = lax.broadcasted_iota(jnp.int32, (group_rows, width), 0)
    conn = jnp.concatenate([conn_ref[...], conn_ref[...]], axis=1)
    reach = lax.broadcasted_iota(jnp.int32, (2 * states, 2 * states), 0)
    for a in range(orb):
        for p in range(2):
            at = (2 * a + p) * lanes
            hit = jnp.where(conn[2 * a : 2 * a + 1] + p * states == reach, 1.0, 0.0) + jnp.where(
                conn[2 * a + 1 : 2 * a + 2] + p * states == reach, 1.0, 0.0
            )
            hits[:, at : at + 2 * states] = hit.astype(bf16)
    mix[cols:width, :] = jnp.zeros((width - cols, mix.shape[1]), bf16)
    mix[width + cols :, :] = jnp.zeros((width - cols, mix.shape[1]), bf16)
    line = lax.broadcasted_iota(jnp.int32, (block, 2 * states), 0) + first
    lane = lax.broadcasted_iota(jnp.int32, (block, 2 * states), 1)
    energies = jnp.concatenate([energy_ref[...], energy_ref[...]], axis=1)
    spins = energies * time_step * (current - line).astype(f32)
    free_pseudo = jnp.where(lane < states, *minus_sine_cosine(spins))
    free_pseudo = free_pseudo * jnp.where(line <= current, 1.0, 0.0)
    count = jnp.sum(mult, axis=1, keepdims=True)
    inside = (row_of <= current) & (row_of >= first)
    summed = (row_of < current) & (row_of >= first)

    def free_sums(bands, place, same, turn, keep):
        for t in range(n_hist):
            for c in range(orb):
                band_all[place, c, t * block : (t + 1) * block, :] = bands[t, c]
        pieces = []
        for c in range(orb):
            angle = jnp.where(summed, band_all[place, c] * time_step, 0.0)
            shift = 1
            while shift < times:
                after = jnp.zeros((shift, lanes), f32)
                angle = angle + jnp.concatenate([angle[shift:], after], axis=0)
                shift *= 2
            free_re, free_im = minus_sine_cosine(angle)
            free_re = jnp.where(inside, free_re, 0.0)
            free_im = jnp.where(inside, free_im, 0.0)
            if keep:
                free_all[0, c] = free_re
                free_all[1, c] = free_im
            two_re, two_im = two_parts(free_re), two_parts(free_im)
            right = jnp.concatenate([two_re[0], two_im[0], two_re[1], two_im[1]], axis=1)
            left = jnp.concatenate([stacked(same[c]), stacked(turn[c])] * 2, axis=1)
            pieces.append(folded(dot(left, right.astype(bf16), 1)))
        pieces.append(jnp.zeros((group_rows, width - cols), f32))
        return jnp.concatenate(pieces, axis=1)

    with jax.named_scope("WOPEN"):

        @pl.when(me == 0)
        def _():
            pl.semaphore_wait(barrier, n_hist * n_ka - 1)

            def one(target, carry):
                signal(opened, target, my_ka)
                return carry

            lax.fori_loop(1, n_hist, one, 0)

    @pl.when(beside_root & is_far)
    def _():
        xfree[...] = jnp.where(lane_of == cols, count, vsend[...])
        band_copy(me).start()
        pack_copy().start()
        own_copy().start()

    with jax.named_scope("TAKEE"):
        take(band_recv, got_energy)
    with jax.named_scope("FREE"):
        own = free_sums(band_recv, 0, same, turn, True) + vsend[...]
        own = jnp.where(lane_of == cols, count, own)
    give(column_copy, near, me)
    give(given_copy, near, me)
    give(part_copy, early, me)
    with jax.named_scope("WOPEN2"):

        @pl.when(me > 0)
        def _():
            pl.semaphore_wait(opened, 1)

    @pl.when(beside_root & jnp.logical_not(is_far))
    def _():
        xfree[...] = own

    for hop in range(1, n_ka):
        target = lax.rem(my_ka + hop, n_ka)

        @pl.when(beside_root & jnp.logical_not(is_far) & (target == 0))
        def _():
            local_copy(xfree, hop).start()

    with jax.named_scope("TAKEV"):

        take(vrecv.at[:, my_ka], got_sum)

    xsend[...] = lax.fori_loop(
        me + 1, n_hist, lambda source, value: value + vrecv[source, my_ka], own
    )
    for hop in range(1, n_ka):
        target = lax.rem(my_ka + hop, n_ka)

        @pl.when((me >= lead) | (target != 0))
        def _():
            local_copy(xsend, hop).start()

    with jax.named_scope("TAKEB"):

        @pl.when(is_root)
        def _():
            for t in range(lead):

                @pl.when(me == t)
                def _():
                    wait_bytes(band_far.at[pl.ds(t, n_hist - t)], got_band)

            wait_bytes(d_far, got_pack)
            wait_bytes(own_far, got_own)
            same_far = [d_far[0, c] for c in range(orb)]
            turn_far = [d_far[1, c] for c in range(orb)]
            value = free_sums(band_far, 1, same_far, turn_far, False)
            xsum[...] = value + xsend[...] + own_far[...]

    with jax.named_scope("TOTAL"):
        at = pl.ds(pl.multiple_of(first, block), block)
        for c in range(orb):
            f_re = free_all[0, c, at, :]
            f_im = free_all[1, c, at, :]
            for a in range(orb):
                d_re = dinv_ref[a, c, 0:1, :]
                d_im = dinv_ref[a, c, 1:2, :]
                row = (a * orb + c) * block
                total[row : row + block, :] = d_re * f_re - d_im * f_im
                row += rows // 2
                total[row : row + block, :] = d_re * f_im + d_im * f_re

    with jax.named_scope("TAKEC"):
        take(crecv, got_column)
        take(grecv, got_given)
    with jax.named_scope("MIX"):
        for t in range(n_hist):
            hist_p[t * half : (t + 1) * half, :] = crecv[t].astype(f32)
            hist_r[t * block : (t + 1) * block, :] = grecv[t]
        given = jnp.where(row_of >= first, hist_r[...], 0.0)
        given = jnp.concatenate(two_parts(given), axis=0).astype(bf16)
        reached = dot(given, hits[...], 0)
        reached = reached[:times] + reached[times:]
        row_weight = jnp.where(row_of == 0, 0.5 * coupling, coupling)
        row_weight = row_weight * jnp.where(row_of < current, 1.0, 0.0)
        sign = jnp.where(
            lax.broadcasted_iota(jnp.int32, (times, lanes), 1) < states, -1.0, 1.0
        )
        r_re = [reached[:, 2 * a * lanes : (2 * a + 1) * lanes] * row_weight for a in range(orb)]
        r_im = [
            reached[:, (2 * a + 1) * lanes : (2 * a + 2) * lanes] * row_weight for a in range(orb)
        ]
        for j in range(block):
            plain = jnp.where(row_of >= first, hist_p[pl.ds(j, times, stride=block), :], 0.0)
            turned = pltpu.roll(plain, states, 1) * sign
            at = slice(j * lanes, (j + 1) * lanes)
            for a in range(orb):
                low, high = a * times, (a + 1) * times
                mix[low:high, at] = (r_re[a] * plain + r_im[a] * turned).astype(bf16)
                mix[width + low : width + high, at] = (
                    r_re[a] * turned - r_im[a] * plain
                ).astype(bf16)

    with jax.named_scope("TAKED"):

        @pl.when(is_root)
        def _():
            for t in range(min(lead, n_hist - 1)):

                @pl.when(me == t)
                def _():
                    above, beside = pl.ds(t + 1, n_hist - 1 - t), pl.ds(1, n_ka - 1)
                    wait_bytes(wrecv.at[above, beside], got_direct)

            def one(source, value):
                for ka in range(1, n_ka):
                    value = value + wrecv[source, ka].astype(f32)
                return value

            xsum[...] = lax.fori_loop(me + 1, n_hist, one, xsum[...])

    with jax.named_scope("TAKEP"):
        take(precv, got_part)
        total[...] = lax.fori_loop(
            me + 1,
            n_hist,
            lambda source, value: value + precv[source].astype(f32),
            total[...] + psend[me].astype(f32),
        )
        for a in range(orb):
            for c in range(orb):
                for j in range(block):
                    at = pl.ds((a * orb + c) * block + j, 2, stride=rows // 2)
                    lattice_out[j, a, c] = total[at, :].astype(bf16)

    with jax.named_scope("TAKEX"):

        @pl.when(jnp.logical_not(is_root))
        def _():
            wait_bytes(xrecv, got_local)
            value = xsend[...]
            for hop in range(1, n_ka):
                value += xrecv[hop - 1]
            xsum[...] = value

        @pl.when(is_root)
        def _():
            wait_bytes(xrecv.at[pl.ds(1, n_ka - 2)], got_local)
            value = xsum[...]
            for hop in range(2, n_ka):
                value += xrecv[hop - 1]
            xsum[...] = value

        local = xsum[...]
    with jax.named_scope("FINAL"):
        scale = 1.0 / local[:, cols : cols + 1]
        picked = jnp.where(lane_of // times == lax.rem(group_of, orb), local, 0.0)
        picked = jnp.concatenate(
            [jnp.where(group_of < orb, picked, 0.0), jnp.where(group_of < orb, 0.0, picked)], axis=1
        )
        sums = folded(dot(stacked(picked), mix[...], 0))
        sums = jnp.sum(sums, axis=0, keepdims=True)
        for j in range(block):
            row = free_pseudo[j : j + 1] + sums[:, j * lanes : (j + 1) * lanes] * scale[:1]
            for p in range(2):
                pseudo_out[p, j : j + 1, :] = row[:, p * states : (p + 1) * states]
        local = local * scale
        for c in range(orb):
            own = pltpu.roll(local, width - first - c * times, 1)[:, :block]
            for a in range(orb):
                for p in range(2):
                    local_out[a, c, p : p + 1, :] = own[p * orb + a : p * orb + a + 1]

    with jax.named_scope("SETTLE"):
        for t in range(1, n_hist):

            @pl.when(me == t)
            def _():
                wait_bytes(band_recv.at[pl.ds(0, t)], sent_energy)
                wait_bytes(vrecv.at[pl.ds(0, t), 0], sent_sum)
                wait_bytes(csend.at[pl.ds(0, t)], sent_column)
                wait_bytes(grecv.at[pl.ds(0, t)], sent_given)
                wait_bytes(psend.at[pl.ds(0, t)], sent_part)

        for t in range(1, lead + 1):

            @pl.when(direct == t)
            def _():
                wait_bytes(wrecv.at[pl.ds(0, t), 0], sent_direct)

            @pl.when(banded + jnp.where(beside_root & is_far, 1, 0) == t)
            def _():
                wait_bytes(band_far.at[pl.ds(0, t)], sent_band)

        @pl.when(beside_root & is_far)
        def _():
            wait_bytes(d_both, sent_pack)
            wait_bytes(xfree, sent_own)
            wait_bytes(xrecv.at[pl.ds(0, n_ka - 2)], sent_local)

        @pl.when(jnp.logical_not(beside_root & is_far))
        def _():
            wait_bytes(xrecv, sent_local)


def put_out(*refs):
    sources, targets, sems = refs[:3], refs[3:6], refs[6]
    copies = [
        pltpu.make_async_copy(source, target, sems.at[i])
        for i, (source, target) in enumerate(zip(sources, targets))
    ]
    for copy in copies:
        copy.start()
    for copy in copies:
        copy.wait()


def per_device(
    n_hist,
    n_ka,
    step_index,
    band_energy,
    kernel_row,
    lattice_history,
    diagonal_inverse,
    multiplicity,
    state_energy,
    connection,
    predicted_row,
    pseudo_history,
):
    block, orb, lanes = band_energy.shape
    times = lattice_history.shape[4]
    states = state_energy.shape[0]
    pairs = 2 * orb * orb
    rows = pairs * block
    per_tile = tile_rows // block
    width = -(-(orb * times + 1) // lane_count) * lane_count
    vmem = pl.BlockSpec(memory_space=pltpu.VMEM)
    f32, bf16 = jnp.float32, jnp.bfloat16
    dma = pltpu.SemaphoreType.DMA
    operands = (
        jnp.transpose(band_energy, (1, 0, 2)),
        jnp.transpose(kernel_row, (0, 2, 3, 1, 4)),
        lattice_history,
        jnp.transpose(diagonal_inverse, (1, 2, 0, 3)),
        multiplicity[None],
        state_energy[None],
        jnp.transpose(connection),
        jnp.transpose(predicted_row, (0, 2, 1)),
        jnp.transpose(pseudo_history, (0, 1, 3, 2)),
    )
    results = pl.pallas_call(
        functools.partial(kernel, n_hist, n_ka),
        out_shape=(
            pltpu.VMEM((block, orb, orb, 2, lanes), bf16),
            pltpu.VMEM((orb, orb, 2, block), f32),
            pltpu.VMEM((2, block, states), f32),
        ),
        in_specs=[pl.BlockSpec(memory_space=pltpu.SMEM)]
        + [pl.BlockSpec(memory_space=pl.ANY)] * len(operands),
        out_specs=(vmem, vmem, vmem),
        scratch_shapes=[
            pltpu.VMEM((n_hist, *operands[0].shape), f32),
            *[pltpu.VMEM(array.shape, array.dtype) for array in operands[1:]],
            pltpu.VMEM((block, orb, orb, 2, lanes), f32),
            pltpu.VMEM((2, orb, group_rows, lanes), f32),
            pltpu.VMEM((2, orb, group_rows, lanes), f32),
            pltpu.VMEM((n_hist, *operands[0].shape), f32),
            pltpu.VMEM((2, orb, times, lanes), f32),
            pltpu.VMEM((2, orb, times, lanes), f32),
            pltpu.VMEM((group_rows, width), f32),
            pltpu.VMEM((n_hist, n_ka, group_rows, width), f32),
            pltpu.VMEM((group_rows, width), bf16),
            pltpu.VMEM((n_hist, n_ka, group_rows, width), bf16),
            pltpu.VMEM((group_rows, width), f32),
            pltpu.VMEM((group_rows, width), f32),
            pltpu.VMEM((group_rows, width), f32),
            pltpu.VMEM((group_rows, width), f32),
            pltpu.VMEM((n_ka - 1, group_rows, width), f32),
            pltpu.VMEM((n_hist, rows, lanes), bf16),
            pltpu.VMEM((n_hist, rows, lanes), bf16),
            pltpu.VMEM((n_hist, block * block, lanes), bf16),
            pltpu.VMEM((n_hist, block * block, lanes), bf16),
            pltpu.VMEM((block, 2 * states), f32),
            pltpu.VMEM((n_hist, block, 2 * states), f32),
            pltpu.VMEM((rows, lanes), f32),
            pltpu.VMEM((times * block, lanes), f32),
            pltpu.VMEM((times, lanes), f32),
            pltpu.VMEM((2 * states, 2 * orb * lanes), bf16),
            pltpu.VMEM((2 * width, 2 * block * states), bf16),
            pltpu.VMEM((per_tile, rows, lanes), f32),
            dma((len(operands) - 1 + block,)),
            *[dma] * 20,
            pltpu.SemaphoreType.REGULAR,
        ],
        compiler_params=pltpu.CompilerParams(collective_id=0, has_side_effects=True),
    )(
        step_index,
        *operands,
    )
    lattice, local, pseudo = pl.pallas_call(
        put_out,
        out_shape=tuple(jax.ShapeDtypeStruct(array.shape, array.dtype) for array in results),
        in_specs=[vmem] * 3,
        out_specs=[pl.BlockSpec(memory_space=pl.ANY)] * 3,
        scratch_shapes=[dma((3,))],
        compiler_params=pltpu.CompilerParams(vmem_limit_bytes=layout_bytes),
    )(*results)
    return (
        jnp.transpose(lattice, (0, 3, 1, 2, 4)),
        jnp.transpose(local, (2, 0, 1, 3)),
        jnp.transpose(pseudo, (0, 2, 1)),
    )


def solution(mesh):
    in_specs = (
        P(),
        P("hist", None, "ka"),
        P("hist", None, None, None, "ka"),
        P("hist", None, None, None, None, "ka"),
        P(None, None, None, "ka"),
        P("ka"),
        P(),
        P(),
        P(None, None, "hist"),
        P("hist", None, None, None),
    )
    out_specs = (
        P("hist", None, None, None, "ka"),
        P(None, None, None, "hist"),
        P(None, None, "hist"),
    )
    return jax.shard_map(
        functools.partial(per_device, mesh.shape["hist"], mesh.shape["ka"]),
        mesh=mesh,
        in_specs=in_specs,
        out_specs=out_specs,
        check_vma=False,
    )
```

```python
import functools
import math

import jax
import jax.numpy as jnp
from jax import lax
from jax.experimental import pallas as pl
from jax.experimental.pallas import tpu as pltpu
from jax.sharding import PartitionSpec as P

time_step = 0.05
coupling = 0.02
tile_rows = 16
group_rows = 8
lead = 2
lane_count = 128
unit_bytes = 4 * lane_count
layout_bytes = 4 * 1024 * 1024


def two_parts(values):
    upper = values.astype(jnp.bfloat16).astype(jnp.float32)
    return upper, values - upper


def stacked(values):
    return jnp.concatenate(two_parts(values), axis=0).astype(jnp.bfloat16)


def size_of(ref):
    size = math.prod(ref.shape) * jnp.dtype(ref.dtype).itemsize
    assert size % unit_bytes == 0
    return size // unit_bytes


def dot(left, right, contract):
    return lax.dot_general(
        left,
        right,
        (((1,), (contract,)), ((), ())),
        preferred_element_type=jnp.float32,
    )


def folded(values):
    return values[:group_rows] + values[group_rows:]


def minus_sine_cosine(angle):
    quarter = jnp.floor(angle * 0.6366197723675814 + 0.5)
    rest = angle - quarter * 1.5703125
    rest = rest - quarter * 4.837512969970703125e-4
    rest = rest - quarter * 7.54978995489188216e-8
    square = rest * rest
    sine = (-1.9515295891e-4 * square + 8.3321608736e-3) * square - 1.6666654611e-1
    sine = sine * square * rest + rest
    cosine = (2.443315711809948e-5 * square - 1.388731625493765e-3) * square
    cosine = (cosine + 4.166664568298827e-2) * square * square - 0.5 * square + 1.0
    half = jnp.floor(quarter * 0.5)
    odd = quarter - 2.0 * half > 0.5
    sign = 2.0 * (half - 2.0 * jnp.floor(half * 0.5)) - 1.0
    return sign * jnp.where(odd, cosine, sine), sign * jnp.where(odd, -sine, cosine)


def kernel(
    n_hist,
    n_ka,
    step_ref,
    band_any,
    krow_any,
    hist_any,
    dinv_any,
    mult_any,
    energy_any,
    conn_any,
    pred_any,
    pseudo_any,
    lattice_out,
    local_out,
    pseudo_out,
    band_recv,
    krow_ref,
    hist_ref,
    dinv_ref,
    mult_ref,
    energy_ref,
    conn_ref,
    pred_ref,
    pseudo_ref,
    kw,
    d_both,
    d_far,
    band_far,
    band_all,
    free_all,
    vsend,
    vrecv,
    wsend,
    wrecv,
    own_far,
    xsend,
    xfree,
    xsum,
    xrecv,
    psend,
    pair_recv,
    paired,
    precv,
    csend,
    crecv,
    gsend,
    grecv,
    total,
    hist_p,
    hist_r,
    hits,
    mix,
    stage,
    units,
    load_sem,
    sent,
    got_energy,
    got_sum,
    got_direct,
    got_far,
    got_column,
    got_pair,
    got_part,
    got_local,
    opened,
    root_in,
):
    _, orb, block, lanes = band_recv.shape
    times = hist_ref.shape[4]
    states = energy_ref.shape[1]
    pairs = 2 * orb * orb
    rows = pairs * block
    per_tile = tile_rows // block
    width = vsend.shape[1]
    cols = orb * times
    f32, bf16 = jnp.float32, jnp.bfloat16
    me = lax.axis_index("hist")
    my_ka = lax.axis_index("ka")
    first = me * block
    parity = lax.rem(me, 2)
    chip = (me - parity) // 2
    partner = me + 1 - 2 * parity

    barrier = pltpu.get_barrier_semaphore()

    def signal(sem, hist, ka):
        pl.semaphore_signal(
            sem, inc=1, device_id={"hist": hist, "ka": ka}, device_id_type=pl.DeviceIdType.MESH
        )

    def greet(target, carry):
        signal(barrier, target, my_ka)
        return carry

    lax.fori_loop(me + 1, n_hist, greet, 0)
    is_root = (my_ka == 0) & (me < lead)

    @pl.when(is_root)
    def _():
        def one(target, carry):
            for ka in range(1, n_ka):
                signal(barrier, target, ka)
            return carry

        lax.fori_loop(jnp.maximum(me, 1), n_hist, one, 0)

    @pl.when((parity == 1) & (me > 1))
    def _():
        signal(barrier, partner, my_ka)

    for ka in range(n_ka):

        @pl.when((me > 0) | (my_ka != ka))
        def _():
            signal(barrier, 0, ka)

    def load(source, target, place):
        copy = pltpu.make_async_copy(source, target, load_sem.at[place])
        copy.start()
        return copy

    small = [
        (krow_any, krow_ref), (dinv_any, dinv_ref), (mult_any, mult_ref),
        (band_any, band_recv.at[me]),
    ]
    for source, target in small:
        load(source, target, 0)
    large = [load(hist_any.at[m], hist_ref.at[m], 1 + m) for m in range(block)]
    others = [
        load(source, target, 1 + block + i)
        for i, (source, target) in enumerate(
            (
                (pred_any, pred_ref),
                (pseudo_any, pseudo_ref),
                (energy_any, energy_ref),
                (conn_any, conn_ref),
            )
        )
    ]
    is_far = my_ka == n_ka - 1
    far_class = jnp.where(is_far, 1, 0)

    def remote(src, dst, send_sem, recv_sem, hist, ka):
        return pltpu.make_async_remote_copy(
            src_ref=src,
            dst_ref=dst,
            send_sem=send_sem,
            recv_sem=recv_sem,
            device_id={"hist": hist, "ka": ka},
            device_id_type=pl.DeviceIdType.MESH,
        )

    def energy_copy(target):
        return remote(band_any, band_recv.at[me], sent, got_energy, target, my_ka)

    def sum_copy(target):
        return remote(vsend, vrecv.at[me, my_ka], sent, got_sum, target, my_ka)

    def direct_copy(target):
        return remote(wsend, wrecv.at[me, my_ka], sent, got_direct, target, 0)

    def band_copy(target):
        return remote(band_any, band_far.at[my_ka, me], sent, got_far.at[far_class], target, 0)

    def pack_copy():
        return remote(d_both.at[0], d_far.at[my_ka], sent, got_far.at[far_class], me, 0)

    def own_copy():
        return remote(xfree, own_far.at[my_ka], sent, got_far.at[far_class], me, 0)

    def pair_copy(place):
        source = psend.at[2 * place + 1 - parity]
        return remote(source, pair_recv.at[place], sent, got_pair, partner, my_ka)

    def part_copy(place):
        target = 2 * place + parity
        return remote(paired.at[place], precv.at[me], sent, got_part, target, my_ka)

    def beside_copy():
        return remote(psend.at[partner], precv.at[me], sent, got_part, partner, my_ka)

    def column_copy(target):
        return remote(csend.at[target], crecv.at[me], sent, got_column, target, my_ka)

    def given_copy(target):
        return remote(gsend, grecv.at[me], sent, got_column, target, my_ka)

    def local_copy(src, hop):
        target = lax.rem(my_ka + hop, n_ka)
        return remote(src, xrecv.at[hop - 1], sent, got_local, me, target)

    def give(copy, start, stop):
        def one(target, carry):
            copy(target).start()
            return carry

        lax.fori_loop(start, stop, one, 0)

    def wait_bytes(ref, sem):
        pltpu.make_async_copy(ref, ref, sem).wait()

    def wait_units(count, sem):
        wait_bytes(units.at[pl.ds(0, count)], sem)

    e_size, v_size, w_size = size_of(band_any), size_of(vsend), size_of(wsend)
    c_size, p_size = size_of(csend.at[0]) + size_of(gsend), size_of(psend.at[0])
    pack_size = size_of(d_far.at[0]) + size_of(own_far.at[0])

    def take(ref, sem):
        for t in range(n_hist - 1):

            @pl.when(me == t)
            def _():
                wait_bytes(ref.at[pl.ds(t + 1, n_hist - 1 - t)], sem)

    current = step_ref[0]
    weight = [
        jnp.where(first + m == 0, 0.5, 1.0) * jnp.where(first + m < current, 1.0, 0.0)
        for m in range(block)
    ]
    d_both[...] = jnp.zeros(d_both.shape, f32)
    vsend[...] = jnp.zeros(vsend.shape, f32)
    wsend[...] = jnp.zeros(wsend.shape, bf16)

    near = jnp.minimum(me, lead)
    direct = jnp.where(my_ka == 0, 0, near)
    beside_root = (my_ka != 0) & (me < lead)
    packs = (my_ka != 0) & ((me == 0) | ((me < lead) & is_far))
    shares = beside_root & jnp.logical_not(packs)
    banded = jnp.where(is_far, near, jnp.where(my_ka == 0, 0, jnp.minimum(me, 1)))
    early = jnp.minimum(chip, lead // 2)
    with jax.named_scope("WBAR"):

        @pl.when(me > 0)
        def _():
            others_in = jnp.where(beside_root, 1, 0) + jnp.where(parity == 0, 1, 0)
            pl.semaphore_wait(barrier, me + direct + others_in)

    give(band_copy, 0, banded)
    give(energy_copy, 0, me)

    @pl.when((me == 1) & (my_ka != 0))
    def _():
        signal(root_in, 0, my_ka)


    with jax.named_scope("LOAD"):
        wait_units(sum(size_of(source) for source, _ in small), load_sem.at[0])
    mult = mult_ref[...].astype(f32)
    count = jnp.sum(mult, axis=1, keepdims=True)
    lane_of = lax.broadcasted_iota(jnp.int32, (group_rows, width), 1)
    for m in range(block):
        kw[m] = krow_ref[m].astype(f32) * weight[m]
    for a in range(orb):
        for c in range(orb):
            d_re = dinv_ref[a, c, 0:1, :] * mult
            d_im = dinv_ref[a, c, 1:2, :] * mult
            d_both[0, c, a : a + 1, :] = d_re
            d_both[0, c, orb + a : orb + a + 1, :] = d_im
            d_both[1, c, a : a + 1, :] = -d_im
            d_both[1, c, orb + a : orb + a + 1, :] = d_re
    same = [d_both[0, c] for c in range(orb)]
    turn = [d_both[1, c] for c in range(orb)]
    left = []
    for m in range(block):
        left.append([])
        for b in range(orb):
            plain = jnp.zeros((group_rows, lanes), f32)
            turned = plain
            for c in range(orb):
                k_re = kw[m, c, b, 0:1, :]
                k_im = kw[m, c, b, 1:2, :]
                plain += same[c] * k_re + turn[c] * k_im
                turned += turn[c] * k_re - same[c] * k_im
            left[m] += [stacked(plain), stacked(turned)]
    sums = jnp.zeros((2 * group_rows, cols), f32)
    for m in range(block):
        with jax.named_scope("LOADH"):
            large[m].wait()
        right = [hist_ref[m, p, b].reshape(cols, lanes) for b in range(orb) for p in range(2)]
        sums += dot(jnp.concatenate(left[m], axis=1), jnp.concatenate(right, axis=1), 1)
    with jax.named_scope("VSEND"):
        sums = folded(sums)
        vsend[:, :cols] = sums
        wsend[:, :cols] = sums.astype(bf16)
        give(direct_copy, 0, direct)
        give(sum_copy, 0, me)

    @pl.when(packs)
    def _():
        @pl.when(me == 0)
        def _():
            pl.semaphore_wait(root_in, 1)

        xfree[...] = jnp.where(lane_of == cols, count, vsend[...])
        band_copy(me).start()
        own_copy().start()
        pack_copy().start()

    with jax.named_scope("PC"):
        for copy in others:
            copy.wait()
        half = block * block
        for m in range(block):
            h_re = pseudo_ref[m, 0].astype(f32)
            h_im = pseudo_ref[m, 1].astype(f32)
            both = jnp.concatenate([h_re, h_im], axis=1)
            for t in range(n_hist):
                hist_p[t * half + m * block : t * half + (m + 1) * block, :] = both[
                    t * block : (t + 1) * block
                ]
        for t in range(n_hist):
            csend[t] = hist_p[t * half : (t + 1) * half, :].astype(bf16)
        gsend[...] = jnp.concatenate([pred_ref[0], pred_ref[1]], axis=1)
    give(column_copy, 0, near)
    give(given_copy, 0, near)

    def one_tile(tile, carry):
        at = pl.ds(pl.multiple_of(tile * tile_rows, tile_rows), tile_rows)
        zero = jnp.zeros((tile_rows, lanes), f32)
        real = [[zero] * orb for _ in range(orb)]
        imag = [[zero] * orb for _ in range(orb)]
        for m in range(block):
            for b in range(orb):
                k_re = [kw[m, a, b, 0:1, :] for a in range(orb)]
                k_im = [kw[m, a, b, 1:2, :] for a in range(orb)]
                for c in range(orb):
                    h_re = hist_ref[m, 0, b, c, at, :].astype(f32)
                    h_im = hist_ref[m, 1, b, c, at, :].astype(f32)
                    for a in range(orb):
                        real[a][c] += k_re[a] * h_re - k_im[a] * h_im
                        imag[a][c] += k_re[a] * h_im + k_im[a] * h_re
        for a in range(orb):
            for c in range(orb):
                out_re, out_im = zero, zero
                for b in range(orb):
                    d_re = dinv_ref[a, b, 0:1, :]
                    d_im = dinv_ref[a, b, 1:2, :]
                    out_re += d_re * real[b][c] - d_im * imag[b][c]
                    out_im += d_re * imag[b][c] + d_im * real[b][c]
                for s, value in enumerate((out_re, out_im)):
                    row = ((s * orb + a) * orb + c) * block
                    for d in range(per_tile):
                        stage[d, row : row + block, :] = value[d * block : (d + 1) * block]
        for d in range(per_tile):
            target = tile * per_tile + d
            psend[target] = stage[d].astype(bf16)

            @pl.when((target < 2 * chip) & (parity != d % 2))
            def _():
                pair_copy(tile * (per_tile // 2) + d // 2).start()

            @pl.when((target == partner) & (parity == 1))
            def _():
                beside_copy().start()

        return carry

    with jax.named_scope("TILES"):
        lax.fori_loop(0, first // tile_rows + 1, one_tile, 0)

    crecv[me] = csend[me]
    grecv[me] = gsend[...]
    row_of = lax.broadcasted_iota(jnp.int32, (times, lanes), 0)
    group_of = lax.broadcasted_iota(jnp.int32, (group_rows, width), 0)
    conn = jnp.concatenate([conn_ref[...], conn_ref[...]], axis=1)
    reach = lax.broadcasted_iota(jnp.int32, (2 * states, 2 * states), 0)
    for a in range(orb):
        for p in range(2):
            at = (2 * a + p) * lanes
            hit = jnp.where(conn[2 * a : 2 * a + 1] + p * states == reach, 1.0, 0.0) + jnp.where(
                conn[2 * a + 1 : 2 * a + 2] + p * states == reach, 1.0, 0.0
            )
            hits[:, at : at + 2 * states] = hit.astype(bf16)
    mix[cols:width, :] = jnp.zeros((width - cols, mix.shape[1]), bf16)
    mix[width + cols :, :] = jnp.zeros((width - cols, mix.shape[1]), bf16)
    line = lax.broadcasted_iota(jnp.int32, (block, 2 * states), 0) + first
    lane = lax.broadcasted_iota(jnp.int32, (block, 2 * states), 1)
    energies = jnp.concatenate([energy_ref[...], energy_ref[...]], axis=1)
    spins = energies * time_step * (current - line).astype(f32)
    free_pseudo = jnp.where(lane < states, *minus_sine_cosine(spins))
    free_pseudo = free_pseudo * jnp.where(line <= current, 1.0, 0.0)
    inside = (row_of <= current) & (row_of >= first)
    summed = (row_of < current) & (row_of >= first)

    def free_sums(bands, place, same, turn, keep):
        for t in range(n_hist):
            for c in range(orb):
                band_all[place, c, t * block : (t + 1) * block, :] = bands[t, c]
        pieces = []
        for c in range(orb):
            angle = jnp.where(summed, band_all[place, c] * time_step, 0.0)
            shift = 1
            while shift < times:
                after = jnp.zeros((shift, lanes), f32)
                angle = angle + jnp.concatenate([angle[shift:], after], axis=0)
                shift *= 2
            free_re, free_im = minus_sine_cosine(angle)
            free_re = jnp.where(inside, free_re, 0.0)
            free_im = jnp.where(inside, free_im, 0.0)
            if keep:
                free_all[0, c] = free_re
                free_all[1, c] = free_im
            two_re, two_im = two_parts(free_re), two_parts(free_im)
            right = jnp.concatenate([two_re[0], two_im[0], two_re[1], two_im[1]], axis=1)
            left = jnp.concatenate([stacked(same[c]), stacked(turn[c])] * 2, axis=1)
            pieces.append(folded(dot(left, right.astype(bf16), 1)))
        pieces.append(jnp.zeros((group_rows, width - cols), f32))
        return jnp.concatenate(pieces, axis=1)

    with jax.named_scope("PAIR"):
        for n in range(1, n_hist // 2):

            @pl.when(chip == n)
            def _():
                wait_bytes(pair_recv.at[pl.ds(0, n)], got_pair)

        def combine(place, carry):
            value = psend[2 * place + parity].astype(f32) + pair_recv[place].astype(f32)
            paired[place] = value.astype(bf16)
            return carry

        lax.fori_loop(0, chip, combine, 0)
    give(part_copy, 0, early)

    with jax.named_scope("WOPEN"):

        @pl.when(me == 0)
        def _():
            pl.semaphore_wait(barrier, n_hist * n_ka - 1)

            def one(target, carry):
                signal(opened, target, my_ka)
                return carry

            lax.fori_loop(1, n_hist, one, 0)

    with jax.named_scope("TAKEE"):
        take(band_recv, got_energy)
    with jax.named_scope("FREE"):
        own = free_sums(band_recv, 0, same, turn, True) + vsend[...]
        own = jnp.where(lane_of == cols, count, own)
    give(column_copy, near, me)
    give(given_copy, near, me)
    give(part_copy, early, chip)
    with jax.named_scope("WOPEN2"):

        @pl.when(me > 0)
        def _():
            pl.semaphore_wait(opened, 1)

    @pl.when(shares)
    def _():
        xfree[...] = own

    for hop in range(1, n_ka):
        target = lax.rem(my_ka + hop, n_ka)

        @pl.when(shares & (target == 0))
        def _():
            local_copy(xfree, hop).start()

    with jax.named_scope("TAKEV"):

        take(vrecv.at[:, my_ka], got_sum)

    xsend[...] = lax.fori_loop(
        me + 1, n_hist, lambda source, value: value + vrecv[source, my_ka], own
    )
    for hop in range(1, n_ka):
        target = lax.rem(my_ka + hop, n_ka)

        @pl.when((me >= lead) | (target != 0))
        def _():
            local_copy(xsend, hop).start()

    with jax.named_scope("TOTAL"):
        at = pl.ds(pl.multiple_of(first, block), block)
        for c in range(orb):
            f_re = free_all[0, c, at, :]
            f_im = free_all[1, c, at, :]
            for a in range(orb):
                d_re = dinv_ref[a, c, 0:1, :]
                d_im = dinv_ref[a, c, 1:2, :]
                row = (a * orb + c) * block
                total[row : row + block, :] = d_re * f_re - d_im * f_im
                row += rows // 2
                total[row : row + block, :] = d_re * f_im + d_im * f_re

    with jax.named_scope("TAKEC"):
        for t in range(n_hist - 1):

            @pl.when(me == t)
            def _():
                wait_units((n_hist - 1 - t) * c_size, got_column)

    with jax.named_scope("MIX"):
        for t in range(n_hist):
            hist_p[t * half : (t + 1) * half, :] = crecv[t].astype(f32)
            hist_r[t * block : (t + 1) * block, :] = grecv[t]
        given = jnp.where(row_of >= first, hist_r[...], 0.0)
        given = jnp.concatenate(two_parts(given), axis=0).astype(bf16)
        reached = dot(given, hits[...], 0)
        reached = reached[:times] + reached[times:]
        row_weight = jnp.where(row_of == 0, 0.5 * coupling, coupling)
        row_weight = row_weight * jnp.where(row_of < current, 1.0, 0.0)
        sign = jnp.where(
            lax.broadcasted_iota(jnp.int32, (times, lanes), 1) < states, -1.0, 1.0
        )
        r_re = [reached[:, 2 * a * lanes : (2 * a + 1) * lanes] * row_weight for a in range(orb)]
        r_im = [
            reached[:, (2 * a + 1) * lanes : (2 * a + 2) * lanes] * row_weight for a in range(orb)
        ]
        for j in range(block):
            plain = jnp.where(row_of >= first, hist_p[pl.ds(j, times, stride=block), :], 0.0)
            turned = pltpu.roll(plain, states, 1) * sign
            at = slice(j * lanes, (j + 1) * lanes)
            for a in range(orb):
                low, high = a * times, (a + 1) * times
                mix[low:high, at] = (r_re[a] * plain + r_im[a] * turned).astype(bf16)
                mix[width + low : width + high, at] = (
                    r_re[a] * turned - r_im[a] * plain
                ).astype(bf16)

    def far_sums(ka):
        same_far = [d_far[ka, c] for c in range(orb)]
        turn_far = [
            jnp.concatenate(
                [-far[orb : 2 * orb], far[:orb], jnp.zeros((group_rows - 2 * orb, lanes), f32)],
                axis=0,
            )
            for far in same_far
        ]
        return free_sums(band_far.at[ka], ka, same_far, turn_far, False) + own_far[ka]

    with jax.named_scope("TAKEB"):

        @pl.when(is_root & (me == 0))
        def _():
            line_size = n_hist * e_size + pack_size
            wait_units((n_ka - 2) * line_size, got_far.at[0])
            value = xsend[...]
            for ka in range(1, n_ka - 1):
                value += far_sums(ka)
            wait_units(line_size, got_far.at[1])
            xsum[...] = value + far_sums(n_ka - 1)

        @pl.when(is_root & (me > 0))
        def _():
            for t in range(1, lead):

                @pl.when(me == t)
                def _():
                    wait_units((n_hist - t) * e_size + pack_size, got_far.at[1])

            xsum[...] = xsend[...] + far_sums(n_ka - 1)

    with jax.named_scope("TAKED"):

        @pl.when(is_root)
        def _():
            for t in range(min(lead, n_hist - 1)):

                @pl.when(me == t)
                def _():
                    above, beside = pl.ds(t + 1, n_hist - 1 - t), pl.ds(1, n_ka - 1)
                    wait_bytes(wrecv.at[above, beside], got_direct)

            def one(source, value):
                for ka in range(1, n_ka):
                    value = value + wrecv[source, ka].astype(f32)
                return value

            xsum[...] = lax.fori_loop(me + 1, n_hist, one, xsum[...])

    with jax.named_scope("TAKEP"):
        for t in range(n_hist - 1):
            above = n_hist // 2 - 1 - t // 2 + (1 - t % 2)

            @pl.when(me == t)
            def _():
                wait_bytes(precv.at[pl.ds(0, above)], got_part)

        total[...] = lax.fori_loop(
            chip + 1,
            n_hist // 2,
            lambda place, value: value + precv[2 * place + parity].astype(f32),
            total[...] + psend[me].astype(f32),
        )

        @pl.when(parity == 0)
        def _():
            total[...] += precv[partner].astype(f32)

        for a in range(orb):
            for c in range(orb):
                for j in range(block):
                    at = pl.ds((a * orb + c) * block + j, 2, stride=rows // 2)
                    lattice_out[j, a, c] = total[at, :].astype(bf16)

    with jax.named_scope("TAKEX"):

        @pl.when(jnp.logical_not(is_root))
        def _():
            wait_bytes(xrecv, got_local)
            value = xsend[...]
            for hop in range(1, n_ka):
                value += xrecv[hop - 1]
            xsum[...] = value

        @pl.when(is_root & (me > 0))
        def _():
            wait_bytes(xrecv.at[pl.ds(1, n_ka - 2)], got_local)
            value = xsum[...]
            for hop in range(2, n_ka):
                value += xrecv[hop - 1]
            xsum[...] = value

        local = xsum[...]
    with jax.named_scope("FINAL"):
        scale = 1.0 / local[:, cols : cols + 1]
        picked = jnp.where(lane_of // times == lax.rem(group_of, orb), local, 0.0)
        picked = jnp.concatenate(
            [jnp.where(group_of < orb, picked, 0.0), jnp.where(group_of < orb, 0.0, picked)], axis=1
        )
        sums = folded(dot(stacked(picked), mix[...], 0))
        sums = jnp.sum(sums, axis=0, keepdims=True)
        for j in range(block):
            row = free_pseudo[j : j + 1] + sums[:, j * lanes : (j + 1) * lanes] * scale[:1]
            for p in range(2):
                pseudo_out[p, j : j + 1, :] = row[:, p * states : (p + 1) * states]
        local = local * scale
        for c in range(orb):
            own = pltpu.roll(local, width - first - c * times, 1)[:, :block]
            for a in range(orb):
                for p in range(2):
                    local_out[a, c, p : p + 1, :] = own[p * orb + a : p * orb + a + 1]

    with jax.named_scope("SETTLE"):
        for t in range(n_hist):
            line = t * (e_size + v_size + c_size) + (2 * (t // 2) + t % 2) * p_size
            leads = min(t, lead)
            for kind in range(3):
                if kind == 0:
                    at, bands, packed, directs = my_ka == 0, 0, 0, 0
                elif kind == 1:
                    at = (my_ka > 0) & (my_ka < n_ka - 1)
                    bands, packed, directs = 1, int(t == 0), leads
                else:
                    at, packed, directs = is_far, int(t < lead), leads
                    bands = leads + packed
                size = line + directs * w_size + bands * e_size + packed * pack_size
                size += (n_ka - 1 - packed) * v_size

                @pl.when((me == t) & at)
                def _():
                    wait_units(size, sent)


def put_out(*refs):
    sources, targets, sems = refs[:3], refs[3:6], refs[6]
    copies = [
        pltpu.make_async_copy(source, target, sems.at[i])
        for i, (source, target) in enumerate(zip(sources, targets))
    ]
    for copy in copies:
        copy.start()
    for copy in copies:
        copy.wait()


def per_device(
    n_hist,
    n_ka,
    step_index,
    band_energy,
    kernel_row,
    lattice_history,
    diagonal_inverse,
    multiplicity,
    state_energy,
    connection,
    predicted_row,
    pseudo_history,
):
    block, orb, lanes = band_energy.shape
    times = lattice_history.shape[4]
    states = state_energy.shape[0]
    pairs = 2 * orb * orb
    rows = pairs * block
    per_tile = tile_rows // block
    width = -(-(orb * times + 1) // lane_count) * lane_count
    band_bytes = 4 * orb * block * lanes
    tile_bytes = 4 * group_rows * width
    most = n_hist * (
        band_bytes + tile_bytes + (2 * block + 8) * block * lanes + 2 * rows * lanes
    )
    most += (n_ka + lead + n_hist) * tile_bytes + n_ka * n_hist * band_bytes
    most //= unit_bytes
    vmem = pl.BlockSpec(memory_space=pltpu.VMEM)
    f32, bf16 = jnp.float32, jnp.bfloat16
    dma = pltpu.SemaphoreType.DMA
    operands = (
        jnp.transpose(band_energy, (1, 0, 2)),
        jnp.transpose(kernel_row, (0, 2, 3, 1, 4)),
        lattice_history,
        jnp.transpose(diagonal_inverse, (1, 2, 0, 3)),
        multiplicity[None],
        state_energy[None],
        jnp.transpose(connection),
        jnp.transpose(predicted_row, (0, 2, 1)),
        jnp.transpose(pseudo_history, (0, 1, 3, 2)),
    )
    results = pl.pallas_call(
        functools.partial(kernel, n_hist, n_ka),
        out_shape=(
            pltpu.VMEM((block, orb, orb, 2, lanes), bf16),
            pltpu.VMEM((orb, orb, 2, block), f32),
            pltpu.VMEM((2, block, states), f32),
        ),
        in_specs=[pl.BlockSpec(memory_space=pltpu.SMEM)]
        + [pl.BlockSpec(memory_space=pl.ANY)] * len(operands),
        out_specs=(vmem, vmem, vmem),
        scratch_shapes=[
            pltpu.VMEM((n_hist, *operands[0].shape), f32),
            *[pltpu.VMEM(array.shape, array.dtype) for array in operands[1:]],
            pltpu.VMEM((block, orb, orb, 2, lanes), f32),
            pltpu.VMEM((2, orb, group_rows, lanes), f32),
            pltpu.VMEM((n_ka, orb, group_rows, lanes), f32),
            pltpu.VMEM((n_ka, n_hist, *operands[0].shape), f32),
            pltpu.VMEM((n_ka, orb, times, lanes), f32),
            pltpu.VMEM((2, orb, times, lanes), f32),
            pltpu.VMEM((group_rows, width), f32),
            pltpu.VMEM((n_hist, n_ka, group_rows, width), f32),
            pltpu.VMEM((group_rows, width), bf16),
            pltpu.VMEM((n_hist, n_ka, group_rows, width), bf16),
            pltpu.VMEM((n_ka, group_rows, width), f32),
            pltpu.VMEM((group_rows, width), f32),
            pltpu.VMEM((group_rows, width), f32),
            pltpu.VMEM((group_rows, width), f32),
            pltpu.VMEM((n_ka - 1, group_rows, width), f32),
            pltpu.VMEM((n_hist, rows, lanes), bf16),
            pltpu.VMEM((n_hist // 2, rows, lanes), bf16),
            pltpu.VMEM((n_hist // 2, rows, lanes), bf16),
            pltpu.VMEM((n_hist, rows, lanes), bf16),
            pltpu.VMEM((n_hist, block * block, lanes), bf16),
            pltpu.VMEM((n_hist, block * block, lanes), bf16),
            pltpu.VMEM((block, 2 * states), f32),
            pltpu.VMEM((n_hist, block, 2 * states), f32),
            pltpu.VMEM((rows, lanes), f32),
            pltpu.VMEM((times * block, lanes), f32),
            pltpu.VMEM((times, lanes), f32),
            pltpu.VMEM((2 * states, 2 * orb * lanes), bf16),
            pltpu.VMEM((2 * width, 2 * block * states), bf16),
            pltpu.VMEM((per_tile, rows, lanes), f32),
            pltpu.VMEM((most, 1, lane_count), f32),
            dma((block + 5,)),
            *[dma] * 4,
            dma((2,)),
            *[dma] * 4,
            pltpu.SemaphoreType.REGULAR,
            pltpu.SemaphoreType.REGULAR,
        ],
        compiler_params=pltpu.CompilerParams(collective_id=0, has_side_effects=True),
    )(
        step_index,
        *operands,
    )
    lattice, local, pseudo = pl.pallas_call(
        put_out,
        out_shape=tuple(jax.ShapeDtypeStruct(array.shape, array.dtype) for array in results),
        in_specs=[vmem] * 3,
        out_specs=[pl.BlockSpec(memory_space=pl.ANY)] * 3,
        scratch_shapes=[dma((3,))],
        compiler_params=pltpu.CompilerParams(vmem_limit_bytes=layout_bytes),
    )(*results)
    return (
        jnp.transpose(lattice, (0, 3, 1, 2, 4)),
        jnp.transpose(local, (2, 0, 1, 3)),
        jnp.transpose(pseudo, (0, 2, 1)),
    )


def solution(mesh):
    in_specs = (
        P(),
        P("hist", None, "ka"),
        P("hist", None, None, None, "ka"),
        P("hist", None, None, None, None, "ka"),
        P(None, None, None, "ka"),
        P("ka"),
        P(),
        P(),
        P(None, None, "hist"),
        P("hist", None, None, None),
    )
    out_specs = (
        P("hist", None, None, None, "ka"),
        P(None, None, None, "hist"),
        P(None, None, "hist"),
    )
    return jax.shard_map(
        functools.partial(per_device, mesh.shape["hist"], mesh.shape["ka"]),
        mesh=mesh,
        in_specs=in_specs,
        out_specs=out_specs,
        check_vma=False,
    )
```

```python
import functools
import math

import jax
import jax.numpy as jnp
from jax import lax
from jax.experimental import pallas as pl
from jax.experimental.pallas import tpu as pltpu
from jax.sharding import PartitionSpec as P

time_step = 0.05
coupling = 0.02
tile_rows = 16
group_rows = 8
lead = 2
lane_count = 128
unit_bytes = 4 * lane_count
layout_bytes = 4 * 1024 * 1024


def two_parts(values):
    upper = values.astype(jnp.bfloat16).astype(jnp.float32)
    return upper, values - upper


def stacked(values):
    return jnp.concatenate(two_parts(values), axis=0).astype(jnp.bfloat16)


def size_of(ref):
    size = math.prod(ref.shape) * jnp.dtype(ref.dtype).itemsize
    assert size % unit_bytes == 0
    return size // unit_bytes


def dot(left, right, contract):
    return lax.dot_general(
        left,
        right,
        (((1,), (contract,)), ((), ())),
        preferred_element_type=jnp.float32,
    )


def folded(values):
    return values[:group_rows] + values[group_rows:]


def minus_sine_cosine(angle):
    quarter = jnp.floor(angle * 0.6366197723675814 + 0.5)
    rest = angle - quarter * 1.5703125
    rest = rest - quarter * 4.837512969970703125e-4
    rest = rest - quarter * 7.54978995489188216e-8
    square = rest * rest
    sine = (-1.9515295891e-4 * square + 8.3321608736e-3) * square - 1.6666654611e-1
    sine = sine * square * rest + rest
    cosine = (2.443315711809948e-5 * square - 1.388731625493765e-3) * square
    cosine = (cosine + 4.166664568298827e-2) * square * square - 0.5 * square + 1.0
    half = jnp.floor(quarter * 0.5)
    odd = quarter - 2.0 * half > 0.5
    sign = 2.0 * (half - 2.0 * jnp.floor(half * 0.5)) - 1.0
    return sign * jnp.where(odd, cosine, sine), sign * jnp.where(odd, -sine, cosine)


def kernel(
    n_hist,
    n_ka,
    step_ref,
    band_any,
    krow_any,
    hist_any,
    dinv_any,
    mult_any,
    energy_any,
    conn_any,
    pred_any,
    pseudo_any,
    lattice_out,
    local_out,
    pseudo_out,
    band_recv,
    krow_ref,
    hist_ref,
    dinv_ref,
    mult_ref,
    energy_ref,
    conn_ref,
    pred_ref,
    pseudo_ref,
    kw,
    d_both,
    d_far,
    band_far,
    band_all,
    free_all,
    vsend,
    vrecv,
    wsend,
    wrecv,
    own_far,
    xsend,
    xfree,
    xsum,
    xrecv,
    psend,
    pair_recv,
    paired,
    precv,
    csend,
    crecv,
    gsend,
    grecv,
    total,
    hist_p,
    hist_r,
    hits,
    mix,
    stage,
    units,
    load_sem,
    sent,
    got_energy,
    got_sum,
    got_direct,
    got_far,
    got_column,
    got_pair,
    got_part,
    got_local,
    opened,
    root_in,
):
    _, orb, block, lanes = band_recv.shape
    times = hist_ref.shape[4]
    states = energy_ref.shape[1]
    pairs = 2 * orb * orb
    rows = pairs * block
    per_tile = tile_rows // block
    width = vsend.shape[1]
    cols = orb * times
    f32, bf16 = jnp.float32, jnp.bfloat16
    me = lax.axis_index("hist")
    my_ka = lax.axis_index("ka")
    first = me * block
    parity = lax.rem(me, 2)
    chip = (me - parity) // 2
    partner = me + 1 - 2 * parity

    def load(source, target, place):
        copy = pltpu.make_async_copy(source, target, load_sem.at[place])
        copy.start()
        return copy

    small = [
        (krow_any, krow_ref), (dinv_any, dinv_ref), (mult_any, mult_ref),
        (band_any, band_recv.at[me]),
    ]
    for source, target in small:
        load(source, target, 0)
    large = [load(hist_any.at[m], hist_ref.at[m], 1 + m) for m in range(block)]
    others = [
        load(source, target, 1 + block + i)
        for i, (source, target) in enumerate(
            (
                (pred_any, pred_ref),
                (pseudo_any, pseudo_ref),
                (energy_any, energy_ref),
                (conn_any, conn_ref),
            )
        )
    ]
    barrier = pltpu.get_barrier_semaphore()

    def signal(sem, hist, ka):
        pl.semaphore_signal(
            sem, inc=1, device_id={"hist": hist, "ka": ka}, device_id_type=pl.DeviceIdType.MESH
        )

    def greet(target, carry):
        signal(barrier, target, my_ka)
        return carry

    lax.fori_loop(me + 1, n_hist, greet, 0)
    is_root = (my_ka == 0) & (me < lead)

    @pl.when(is_root)
    def _():
        def one(target, carry):
            for ka in range(1, n_ka):
                signal(barrier, target, ka)
            return carry

        lax.fori_loop(jnp.maximum(me, 1), n_hist, one, 0)

    @pl.when((parity == 1) & (me > 1))
    def _():
        signal(barrier, partner, my_ka)

    for ka in range(n_ka):

        @pl.when((me > 0) | (my_ka != ka))
        def _():
            signal(barrier, 0, ka)

    is_far = my_ka == n_ka - 1
    far_class = jnp.where(is_far, 1, 0)

    def remote(src, dst, send_sem, recv_sem, hist, ka):
        return pltpu.make_async_remote_copy(
            src_ref=src,
            dst_ref=dst,
            send_sem=send_sem,
            recv_sem=recv_sem,
            device_id={"hist": hist, "ka": ka},
            device_id_type=pl.DeviceIdType.MESH,
        )

    def energy_copy(target):
        return remote(band_any, band_recv.at[me], sent, got_energy, target, my_ka)

    def sum_copy(target):
        return remote(vsend, vrecv.at[me, my_ka], sent, got_sum, target, my_ka)

    def direct_copy(target):
        return remote(wsend, wrecv.at[me, my_ka], sent, got_direct, target, 0)

    def band_copy(target):
        return remote(band_any, band_far.at[my_ka, me], sent, got_far.at[far_class], target, 0)

    def pack_copy():
        return remote(d_both.at[0], d_far.at[my_ka], sent, got_far.at[far_class], me, 0)

    def own_copy():
        return remote(xfree, own_far.at[my_ka], sent, got_far.at[far_class], me, 0)

    def pair_copy(place):
        source = psend.at[2 * place + 1 - parity]
        return remote(source, pair_recv.at[place], sent, got_pair, partner, my_ka)

    def part_copy(place):
        target = 2 * place + parity
        return remote(paired.at[place], precv.at[me], sent, got_part, target, my_ka)

    def beside_copy():
        return remote(psend.at[partner], precv.at[me], sent, got_part, partner, my_ka)

    def column_copy(target):
        return remote(csend.at[target], crecv.at[me], sent, got_column, target, my_ka)

    def given_copy(target):
        return remote(gsend, grecv.at[me], sent, got_column, target, my_ka)

    def local_copy(src, hop):
        target = lax.rem(my_ka + hop, n_ka)
        return remote(src, xrecv.at[hop - 1], sent, got_local, me, target)

    def give(copy, start, stop):
        def one(target, carry):
            copy(target).start()
            return carry

        lax.fori_loop(start, stop, one, 0)

    def wait_bytes(ref, sem):
        pltpu.make_async_copy(ref, ref, sem).wait()

    def wait_units(count, sem):
        wait_bytes(units.at[pl.ds(0, count)], sem)

    e_size, v_size, w_size = size_of(band_any), size_of(vsend), size_of(wsend)
    c_size, p_size = size_of(csend.at[0]) + size_of(gsend), size_of(psend.at[0])
    pack_size = size_of(d_far.at[0]) + size_of(own_far.at[0])

    def take(ref, sem):
        for t in range(n_hist - 1):

            @pl.when(me == t)
            def _():
                wait_bytes(ref.at[pl.ds(t + 1, n_hist - 1 - t)], sem)

    current = step_ref[0]
    weight = [
        jnp.where(first + m == 0, 0.5, 1.0) * jnp.where(first + m < current, 1.0, 0.0)
        for m in range(block)
    ]
    d_both[...] = jnp.zeros(d_both.shape, f32)
    vsend[...] = jnp.zeros(vsend.shape, f32)
    wsend[...] = jnp.zeros(wsend.shape, bf16)

    near = jnp.minimum(me, lead)
    direct = jnp.where(my_ka == 0, 0, near)
    beside_root = (my_ka != 0) & (me < lead)
    packs = (my_ka != 0) & ((me == 0) | ((me < lead) & is_far))
    shares = beside_root & jnp.logical_not(packs)
    banded = jnp.where(is_far, near, jnp.where(my_ka == 0, 0, jnp.minimum(me, 1)))
    early = jnp.minimum(chip, lead // 2)
    with jax.named_scope("WBAR"):

        @pl.when(me > 0)
        def _():
            others_in = jnp.where(beside_root, 1, 0) + jnp.where(parity == 0, 1, 0)
            pl.semaphore_wait(barrier, me + direct + others_in)

    give(band_copy, 0, banded)
    give(energy_copy, 0, me)

    @pl.when((me == 1) & (my_ka != 0))
    def _():
        signal(root_in, 0, my_ka)


    with jax.named_scope("LOAD"):
        wait_units(sum(size_of(source) for source, _ in small), load_sem.at[0])
    mult = mult_ref[...].astype(f32)
    count = jnp.sum(mult, axis=1, keepdims=True)
    lane_of = lax.broadcasted_iota(jnp.int32, (group_rows, width), 1)
    for m in range(block):
        kw[m] = krow_ref[m].astype(f32) * weight[m]
    for a in range(orb):
        for c in range(orb):
            d_re = dinv_ref[a, c, 0:1, :] * mult
            d_im = dinv_ref[a, c, 1:2, :] * mult
            d_both[0, c, a : a + 1, :] = d_re
            d_both[0, c, orb + a : orb + a + 1, :] = d_im
            d_both[1, c, a : a + 1, :] = -d_im
            d_both[1, c, orb + a : orb + a + 1, :] = d_re
    same = [d_both[0, c] for c in range(orb)]
    turn = [d_both[1, c] for c in range(orb)]
    left = []
    for m in range(block):
        left.append([])
        for b in range(orb):
            plain = jnp.zeros((group_rows, lanes), f32)
            turned = plain
            for c in range(orb):
                k_re = kw[m, c, b, 0:1, :]
                k_im = kw[m, c, b, 1:2, :]
                plain += same[c] * k_re + turn[c] * k_im
                turned += turn[c] * k_re - same[c] * k_im
            left[m] += [stacked(plain), stacked(turned)]
    sums = jnp.zeros((2 * group_rows, cols), f32)
    for m in range(block):
        with jax.named_scope("LOADH"):
            large[m].wait()
        right = [hist_ref[m, p, b].reshape(cols, lanes) for b in range(orb) for p in range(2)]
        for x in range(orb):
            sums += dot(jnp.concatenate(left[m][2*x:2*x+2], axis=1), jnp.concatenate(right[2*x:2*x+2], axis=1), 1)
    with jax.named_scope("VSEND"):
        sums = folded(sums)
        vsend[:, :cols] = sums
        wsend[:, :cols] = sums.astype(bf16)
        give(direct_copy, 0, direct)
        give(sum_copy, 0, me)

    @pl.when(packs)
    def _():
        @pl.when(me == 0)
        def _():
            pl.semaphore_wait(root_in, 1)

        xfree[...] = jnp.where(lane_of == cols, count, vsend[...])
        band_copy(me).start()
        own_copy().start()
        pack_copy().start()

    with jax.named_scope("PC"):
        for copy in others:
            copy.wait()
        half = block * block
        for m in range(block):
            h_re = pseudo_ref[m, 0].astype(f32)
            h_im = pseudo_ref[m, 1].astype(f32)
            both = jnp.concatenate([h_re, h_im], axis=1)
            for t in range(n_hist):
                hist_p[t * half + m * block : t * half + (m + 1) * block, :] = both[
                    t * block : (t + 1) * block
                ]
        for t in range(n_hist):
            csend[t] = hist_p[t * half : (t + 1) * half, :].astype(bf16)
        gsend[...] = jnp.concatenate([pred_ref[0], pred_ref[1]], axis=1)
    give(column_copy, 0, near)
    give(given_copy, 0, near)

    def one_tile(tile, carry):
        at = pl.ds(pl.multiple_of(tile * tile_rows, tile_rows), tile_rows)
        zero = jnp.zeros((tile_rows, lanes), f32)
        real = [[zero] * orb for _ in range(orb)]
        imag = [[zero] * orb for _ in range(orb)]
        for m in range(block):
            for b in range(orb):
                k_re = [kw[m, a, b, 0:1, :] for a in range(orb)]
                k_im = [kw[m, a, b, 1:2, :] for a in range(orb)]
                for c in range(orb):
                    h_re = hist_ref[m, 0, b, c, at, :].astype(f32)
                    h_im = hist_ref[m, 1, b, c, at, :].astype(f32)
                    for a in range(orb):
                        real[a][c] += k_re[a] * h_re - k_im[a] * h_im
                        imag[a][c] += k_re[a] * h_im + k_im[a] * h_re
        for a in range(orb):
            for c in range(orb):
                out_re, out_im = zero, zero
                for b in range(orb):
                    d_re = dinv_ref[a, b, 0:1, :]
                    d_im = dinv_ref[a, b, 1:2, :]
                    out_re += d_re * real[b][c] - d_im * imag[b][c]
                    out_im += d_re * imag[b][c] + d_im * real[b][c]
                for s, value in enumerate((out_re, out_im)):
                    row = ((s * orb + a) * orb + c) * block
                    for d in range(per_tile):
                        stage[d, row : row + block, :] = value[d * block : (d + 1) * block]
        for d in range(per_tile):
            target = tile * per_tile + d
            psend[target] = stage[d].astype(bf16)

            @pl.when((target < 2 * chip) & (parity != d % 2))
            def _():
                pair_copy(tile * (per_tile // 2) + d // 2).start()

            @pl.when((target == partner) & (parity == 1))
            def _():
                beside_copy().start()

        return carry

    with jax.named_scope("TILES"):
        lax.fori_loop(0, first // tile_rows + 1, one_tile, 0)

    crecv[me] = csend[me]
    grecv[me] = gsend[...]
    row_of = lax.broadcasted_iota(jnp.int32, (times, lanes), 0)
    group_of = lax.broadcasted_iota(jnp.int32, (group_rows, width), 0)
    conn = jnp.concatenate([conn_ref[...], conn_ref[...]], axis=1)
    reach = lax.broadcasted_iota(jnp.int32, (2 * states, 2 * states), 0)
    for a in range(orb):
        for p in range(2):
            at = (2 * a + p) * lanes
            hit = jnp.where(conn[2 * a : 2 * a + 1] + p * states == reach, 1.0, 0.0) + jnp.where(
                conn[2 * a + 1 : 2 * a + 2] + p * states == reach, 1.0, 0.0
            )
            hits[:, at : at + 2 * states] = hit.astype(bf16)
    mix[cols:width, :] = jnp.zeros((width - cols, mix.shape[1]), bf16)
    mix[width + cols :, :] = jnp.zeros((width - cols, mix.shape[1]), bf16)
    line = lax.broadcasted_iota(jnp.int32, (block, 2 * states), 0) + first
    lane = lax.broadcasted_iota(jnp.int32, (block, 2 * states), 1)
    energies = jnp.concatenate([energy_ref[...], energy_ref[...]], axis=1)
    spins = energies * time_step * (current - line).astype(f32)
    free_pseudo = jnp.where(lane < states, *minus_sine_cosine(spins))
    free_pseudo = free_pseudo * jnp.where(line <= current, 1.0, 0.0)
    inside = (row_of <= current) & (row_of >= first)
    summed = (row_of < current) & (row_of >= first)

    def free_sums(bands, place, same, turn, keep):
        for t in range(n_hist):
            for c in range(orb):
                band_all[place, c, t * block : (t + 1) * block, :] = bands[t, c]
        pieces = []
        for c in range(orb):
            angle = jnp.where(summed, band_all[place, c] * time_step, 0.0)
            shift = 1
            while shift < times:
                after = jnp.zeros((shift, lanes), f32)
                angle = angle + jnp.concatenate([angle[shift:], after], axis=0)
                shift *= 2
            free_re, free_im = minus_sine_cosine(angle)
            free_re = jnp.where(inside, free_re, 0.0)
            free_im = jnp.where(inside, free_im, 0.0)
            if keep:
                free_all[0, c] = free_re
                free_all[1, c] = free_im
            two_re, two_im = two_parts(free_re), two_parts(free_im)
            right = jnp.concatenate([two_re[0], two_im[0], two_re[1], two_im[1]], axis=1)
            left = jnp.concatenate([stacked(same[c]), stacked(turn[c])] * 2, axis=1)
            pieces.append(folded(dot(left, right.astype(bf16), 1)))
        pieces.append(jnp.zeros((group_rows, width - cols), f32))
        return jnp.concatenate(pieces, axis=1)

    with jax.named_scope("PAIR"):
        for n in range(1, n_hist // 2):

            @pl.when(chip == n)
            def _():
                wait_bytes(pair_recv.at[pl.ds(0, n)], got_pair)

        def combine(place, carry):
            value = psend[2 * place + parity].astype(f32) + pair_recv[place].astype(f32)
            paired[place] = value.astype(bf16)
            return carry

        lax.fori_loop(0, chip, combine, 0)
    give(part_copy, 0, early)

    with jax.named_scope("WOPEN"):

        @pl.when(me == 0)
        def _():
            pl.semaphore_wait(barrier, n_hist * n_ka - 1)

            def one(target, carry):
                signal(opened, target, my_ka)
                return carry

            lax.fori_loop(1, n_hist, one, 0)

    with jax.named_scope("TAKEE"):
        take(band_recv, got_energy)
    with jax.named_scope("FREE"):
        own = free_sums(band_recv, 0, same, turn, True) + vsend[...]
        own = jnp.where(lane_of == cols, count, own)
    give(column_copy, near, me)
    give(given_copy, near, me)
    give(part_copy, early, chip)
    with jax.named_scope("WOPEN2"):

        @pl.when(me > 0)
        def _():
            pl.semaphore_wait(opened, 1)

    @pl.when(shares)
    def _():
        xfree[...] = own

    for hop in range(1, n_ka):
        target = lax.rem(my_ka + hop, n_ka)

        @pl.when(shares & (target == 0))
        def _():
            local_copy(xfree, hop).start()

    with jax.named_scope("TAKEV"):

        take(vrecv.at[:, my_ka], got_sum)

    xsend[...] = lax.fori_loop(
        me + 1, n_hist, lambda source, value: value + vrecv[source, my_ka], own
    )
    for hop in range(1, n_ka):
        target = lax.rem(my_ka + hop, n_ka)

        @pl.when((me >= lead) | (target != 0))
        def _():
            local_copy(xsend, hop).start()

    with jax.named_scope("TOTAL"):
        at = pl.ds(pl.multiple_of(first, block), block)
        for c in range(orb):
            f_re = free_all[0, c, at, :]
            f_im = free_all[1, c, at, :]
            for a in range(orb):
                d_re = dinv_ref[a, c, 0:1, :]
                d_im = dinv_ref[a, c, 1:2, :]
                row = (a * orb + c) * block
                total[row : row + block, :] = d_re * f_re - d_im * f_im
                row += rows // 2
                total[row : row + block, :] = d_re * f_im + d_im * f_re

    with jax.named_scope("TAKEC"):
        for t in range(n_hist - 1):

            @pl.when(me == t)
            def _():
                wait_units((n_hist - 1 - t) * c_size, got_column)

    with jax.named_scope("MIX"):
        for t in range(n_hist):
            hist_p[t * half : (t + 1) * half, :] = crecv[t].astype(f32)
            hist_r[t * block : (t + 1) * block, :] = grecv[t]
        given = jnp.where(row_of >= first, hist_r[...], 0.0)
        given = jnp.concatenate(two_parts(given), axis=0).astype(bf16)
        reached = dot(given, hits[...], 0)
        reached = reached[:times] + reached[times:]
        row_weight = jnp.where(row_of == 0, 0.5 * coupling, coupling)
        row_weight = row_weight * jnp.where(row_of < current, 1.0, 0.0)
        sign = jnp.where(
            lax.broadcasted_iota(jnp.int32, (times, lanes), 1) < states, -1.0, 1.0
        )
        r_re = [reached[:, 2 * a * lanes : (2 * a + 1) * lanes] * row_weight for a in range(orb)]
        r_im = [
            reached[:, (2 * a + 1) * lanes : (2 * a + 2) * lanes] * row_weight for a in range(orb)
        ]
        for j in range(block):
            plain = jnp.where(row_of >= first, hist_p[pl.ds(j, times, stride=block), :], 0.0)
            turned = pltpu.roll(plain, states, 1) * sign
            at = slice(j * lanes, (j + 1) * lanes)
            for a in range(orb):
                low, high = a * times, (a + 1) * times
                mix[low:high, at] = (r_re[a] * plain + r_im[a] * turned).astype(bf16)
                mix[width + low : width + high, at] = (
                    r_re[a] * turned - r_im[a] * plain
                ).astype(bf16)

    def far_sums(ka):
        same_far = [d_far[ka, c] for c in range(orb)]
        turn_far = [
            jnp.concatenate(
                [-far[orb : 2 * orb], far[:orb], jnp.zeros((group_rows - 2 * orb, lanes), f32)],
                axis=0,
            )
            for far in same_far
        ]
        return free_sums(band_far.at[ka], ka, same_far, turn_far, False) + own_far[ka]

    with jax.named_scope("TAKEB"):

        @pl.when(is_root & (me == 0))
        def _():
            line_size = n_hist * e_size + pack_size
            wait_units((n_ka - 2) * line_size, got_far.at[0])
            value = xsend[...]
            for ka in range(1, n_ka - 1):
                value += far_sums(ka)
            wait_units(line_size, got_far.at[1])
            xsum[...] = value + far_sums(n_ka - 1)

        @pl.when(is_root & (me > 0))
        def _():
            for t in range(1, lead):

                @pl.when(me == t)
                def _():
                    wait_units((n_hist - t) * e_size + pack_size, got_far.at[1])

            xsum[...] = xsend[...] + far_sums(n_ka - 1)

    with jax.named_scope("TAKED"):

        @pl.when(is_root)
        def _():
            for t in range(min(lead, n_hist - 1)):

                @pl.when(me == t)
                def _():
                    above, beside = pl.ds(t + 1, n_hist - 1 - t), pl.ds(1, n_ka - 1)
                    wait_bytes(wrecv.at[above, beside], got_direct)

            def one(source, value):
                for ka in range(1, n_ka):
                    value = value + wrecv[source, ka].astype(f32)
                return value

            xsum[...] = lax.fori_loop(me + 1, n_hist, one, xsum[...])

    with jax.named_scope("TAKEP"):
        for t in range(n_hist - 1):
            above = n_hist // 2 - 1 - t // 2 + (1 - t % 2)

            @pl.when(me == t)
            def _():
                wait_bytes(precv.at[pl.ds(0, above)], got_part)

        total[...] = lax.fori_loop(
            chip + 1,
            n_hist // 2,
            lambda place, value: value + precv[2 * place + parity].astype(f32),
            total[...] + psend[me].astype(f32),
        )

        @pl.when(parity == 0)
        def _():
            total[...] += precv[partner].astype(f32)

        for a in range(orb):
            for c in range(orb):
                for j in range(block):
                    at = pl.ds((a * orb + c) * block + j, 2, stride=rows // 2)
                    lattice_out[j, a, c] = total[at, :].astype(bf16)

    with jax.named_scope("TAKEX"):

        @pl.when(jnp.logical_not(is_root))
        def _():
            wait_bytes(xrecv, got_local)
            value = xsend[...]
            for hop in range(1, n_ka):
                value += xrecv[hop - 1]
            xsum[...] = value

        @pl.when(is_root & (me > 0))
        def _():
            wait_bytes(xrecv.at[pl.ds(1, n_ka - 2)], got_local)
            value = xsum[...]
            for hop in range(2, n_ka):
                value += xrecv[hop - 1]
            xsum[...] = value

        local = xsum[...]
    with jax.named_scope("FINAL"):
        scale = 1.0 / local[:, cols : cols + 1]
        picked = jnp.where(lane_of // times == lax.rem(group_of, orb), local, 0.0)
        picked = jnp.concatenate(
            [jnp.where(group_of < orb, picked, 0.0), jnp.where(group_of < orb, 0.0, picked)], axis=1
        )
        sums = folded(dot(stacked(picked), mix[...], 0))
        sums = jnp.sum(sums, axis=0, keepdims=True)
        for j in range(block):
            row = free_pseudo[j : j + 1] + sums[:, j * lanes : (j + 1) * lanes] * scale[:1]
            for p in range(2):
                pseudo_out[p, j : j + 1, :] = row[:, p * states : (p + 1) * states]
        local = local * scale
        for c in range(orb):
            own = pltpu.roll(local, width - first - c * times, 1)[:, :block]
            for a in range(orb):
                for p in range(2):
                    local_out[a, c, p : p + 1, :] = own[p * orb + a : p * orb + a + 1]

    with jax.named_scope("SETTLE"):
        for t in range(n_hist):
            line = t * (e_size + v_size + c_size) + (2 * (t // 2) + t % 2) * p_size
            leads = min(t, lead)
            for kind in range(3):
                if kind == 0:
                    at, bands, packed, directs = my_ka == 0, 0, 0, 0
                elif kind == 1:
                    at = (my_ka > 0) & (my_ka < n_ka - 1)
                    bands, packed, directs = 1, int(t == 0), leads
                else:
                    at, packed, directs = is_far, int(t < lead), leads
                    bands = leads + packed
                size = line + directs * w_size + bands * e_size + packed * pack_size
                size += (n_ka - 1 - packed) * v_size

                @pl.when((me == t) & at)
                def _():
                    wait_units(size, sent)


def put_out(*refs):
    sources, targets, sems = refs[:3], refs[3:6], refs[6]
    copies = [
        pltpu.make_async_copy(source, target, sems.at[i])
        for i, (source, target) in enumerate(zip(sources, targets))
    ]
    for copy in copies:
        copy.start()
    for copy in copies:
        copy.wait()


def per_device(
    n_hist,
    n_ka,
    step_index,
    band_energy,
    kernel_row,
    lattice_history,
    diagonal_inverse,
    multiplicity,
    state_energy,
    connection,
    predicted_row,
    pseudo_history,
):
    block, orb, lanes = band_energy.shape
    times = lattice_history.shape[4]
    states = state_energy.shape[0]
    pairs = 2 * orb * orb
    rows = pairs * block
    per_tile = tile_rows // block
    width = -(-(orb * times + 1) // lane_count) * lane_count
    band_bytes = 4 * orb * block * lanes
    tile_bytes = 4 * group_rows * width
    most = n_hist * (
        band_bytes + tile_bytes + (2 * block + 8) * block * lanes + 2 * rows * lanes
    )
    most += (n_ka + lead + n_hist) * tile_bytes + n_ka * n_hist * band_bytes
    most //= unit_bytes
    vmem = pl.BlockSpec(memory_space=pltpu.VMEM)
    f32, bf16 = jnp.float32, jnp.bfloat16
    dma = pltpu.SemaphoreType.DMA
    operands = (
        jnp.transpose(band_energy, (1, 0, 2)),
        jnp.transpose(kernel_row, (0, 2, 3, 1, 4)),
        lattice_history,
        jnp.transpose(diagonal_inverse, (1, 2, 0, 3)),
        multiplicity[None],
        state_energy[None],
        jnp.transpose(connection),
        jnp.transpose(predicted_row, (0, 2, 1)),
        jnp.transpose(pseudo_history, (0, 1, 3, 2)),
    )
    results = pl.pallas_call(
        functools.partial(kernel, n_hist, n_ka),
        out_shape=(
            pltpu.VMEM((block, orb, orb, 2, lanes), bf16),
            pltpu.VMEM((orb, orb, 2, block), f32),
            pltpu.VMEM((2, block, states), f32),
        ),
        in_specs=[pl.BlockSpec(memory_space=pltpu.SMEM)]
        + [pl.BlockSpec(memory_space=pl.ANY)] * len(operands),
        out_specs=(vmem, vmem, vmem),
        scratch_shapes=[
            pltpu.VMEM((n_hist, *operands[0].shape), f32),
            *[pltpu.VMEM(array.shape, array.dtype) for array in operands[1:]],
            pltpu.VMEM((block, orb, orb, 2, lanes), f32),
            pltpu.VMEM((2, orb, group_rows, lanes), f32),
            pltpu.VMEM((n_ka, orb, group_rows, lanes), f32),
            pltpu.VMEM((n_ka, n_hist, *operands[0].shape), f32),
            pltpu.VMEM((n_ka, orb, times, lanes), f32),
            pltpu.VMEM((2, orb, times, lanes), f32),
            pltpu.VMEM((group_rows, width), f32),
            pltpu.VMEM((n_hist, n_ka, group_rows, width), f32),
            pltpu.VMEM((group_rows, width), bf16),
            pltpu.VMEM((n_hist, n_ka, group_rows, width), bf16),
            pltpu.VMEM((n_ka, group_rows, width), f32),
            pltpu.VMEM((group_rows, width), f32),
            pltpu.VMEM((group_rows, width), f32),
            pltpu.VMEM((group_rows, width), f32),
            pltpu.VMEM((n_ka - 1, group_rows, width), f32),
            pltpu.VMEM((n_hist, rows, lanes), bf16),
            pltpu.VMEM((n_hist // 2, rows, lanes), bf16),
            pltpu.VMEM((n_hist // 2, rows, lanes), bf16),
            pltpu.VMEM((n_hist, rows, lanes), bf16),
            pltpu.VMEM((n_hist, block * block, lanes), bf16),
            pltpu.VMEM((n_hist, block * block, lanes), bf16),
            pltpu.VMEM((block, 2 * states), f32),
            pltpu.VMEM((n_hist, block, 2 * states), f32),
            pltpu.VMEM((rows, lanes), f32),
            pltpu.VMEM((times * block, lanes), f32),
            pltpu.VMEM((times, lanes), f32),
            pltpu.VMEM((2 * states, 2 * orb * lanes), bf16),
            pltpu.VMEM((2 * width, 2 * block * states), bf16),
            pltpu.VMEM((per_tile, rows, lanes), f32),
            pltpu.VMEM((most, 1, lane_count), f32),
            dma((block + 5,)),
            *[dma] * 4,
            dma((2,)),
            *[dma] * 4,
            pltpu.SemaphoreType.REGULAR,
            pltpu.SemaphoreType.REGULAR,
        ],
        compiler_params=pltpu.CompilerParams(collective_id=0, has_side_effects=True),
    )(
        step_index,
        *operands,
    )
    lattice, local, pseudo = pl.pallas_call(
        put_out,
        out_shape=tuple(jax.ShapeDtypeStruct(array.shape, array.dtype) for array in results),
        in_specs=[vmem] * 3,
        out_specs=[pl.BlockSpec(memory_space=pl.ANY)] * 3,
        scratch_shapes=[dma((3,))],
        compiler_params=pltpu.CompilerParams(vmem_limit_bytes=layout_bytes),
    )(*results)
    return (
        jnp.transpose(lattice, (0, 3, 1, 2, 4)),
        jnp.transpose(local, (2, 0, 1, 3)),
        jnp.transpose(pseudo, (0, 2, 1)),
    )


def solution(mesh):
    in_specs = (
        P(),
        P("hist", None, "ka"),
        P("hist", None, None, None, "ka"),
        P("hist", None, None, None, None, "ka"),
        P(None, None, None, "ka"),
        P("ka"),
        P(),
        P(),
        P(None, None, "hist"),
        P("hist", None, None, None),
    )
    out_specs = (
        P("hist", None, None, None, "ka"),
        P(None, None, None, "hist"),
        P(None, None, "hist"),
    )
    return jax.shard_map(
        functools.partial(per_device, mesh.shape["hist"], mesh.shape["ka"]),
        mesh=mesh,
        in_specs=in_specs,
        out_specs=out_specs,
        check_vma=False,
    )
```

```python
import functools
import math

import jax
import jax.numpy as jnp
from jax import lax
from jax.experimental import pallas as pl
from jax.experimental.pallas import tpu as pltpu
from jax.sharding import PartitionSpec as P

time_step = 0.05
coupling = 0.02
tile_rows = 16
group_rows = 8
lead = 2
lane_count = 128
unit_bytes = 4 * lane_count
layout_bytes = 4 * 1024 * 1024


def two_parts(values):
    upper = values.astype(jnp.bfloat16).astype(jnp.float32)
    return upper, values - upper


def stacked(values):
    return jnp.concatenate(two_parts(values), axis=0).astype(jnp.bfloat16)


def size_of(ref):
    size = math.prod(ref.shape) * jnp.dtype(ref.dtype).itemsize
    assert size % unit_bytes == 0
    return size // unit_bytes


def dot(left, right, contract):
    return lax.dot_general(
        left,
        right,
        (((1,), (contract,)), ((), ())),
        preferred_element_type=jnp.float32,
    )


def folded(values):
    return values[:group_rows] + values[group_rows:]


def minus_sine_cosine(angle):
    quarter = jnp.floor(angle * 0.6366197723675814 + 0.5)
    rest = angle - quarter * 1.5703125
    rest = rest - quarter * 4.837512969970703125e-4
    rest = rest - quarter * 7.54978995489188216e-8
    square = rest * rest
    sine = (-1.9515295891e-4 * square + 8.3321608736e-3) * square - 1.6666654611e-1
    sine = sine * square * rest + rest
    cosine = (2.443315711809948e-5 * square - 1.388731625493765e-3) * square
    cosine = (cosine + 4.166664568298827e-2) * square * square - 0.5 * square + 1.0
    half = jnp.floor(quarter * 0.5)
    odd = quarter - 2.0 * half > 0.5
    sign = 2.0 * (half - 2.0 * jnp.floor(half * 0.5)) - 1.0
    return sign * jnp.where(odd, cosine, sine), sign * jnp.where(odd, -sine, cosine)


def kernel(
    n_hist,
    n_ka,
    step_ref,
    band_any,
    krow_any,
    hist_any,
    dinv_any,
    mult_any,
    energy_any,
    conn_any,
    pred_any,
    pseudo_any,
    lattice_out,
    local_out,
    pseudo_out,
    band_recv,
    krow_ref,
    hist_ref,
    dinv_ref,
    mult_ref,
    energy_ref,
    conn_ref,
    pred_ref,
    pseudo_ref,
    kw,
    d_both,
    d_far,
    band_far,
    band_all,
    free_all,
    vsend,
    vrecv,
    wsend,
    wrecv,
    own_far,
    xsend,
    xfree,
    xsum,
    xrecv,
    psend,
    pair_recv,
    paired,
    precv,
    csend,
    crecv,
    gsend,
    grecv,
    total,
    hist_p,
    hist_r,
    hits,
    mix,
    stage,
    units,
    load_sem,
    sent,
    got_energy,
    got_sum,
    got_direct,
    got_far,
    got_column,
    got_pair,
    got_part,
    got_local,
    opened,
    root_in,
):
    _, orb, block, lanes = band_recv.shape
    times = hist_ref.shape[4]
    states = energy_ref.shape[1]
    pairs = 2 * orb * orb
    rows = pairs * block
    per_tile = tile_rows // block
    width = vsend.shape[1]
    cols = orb * times
    f32, bf16 = jnp.float32, jnp.bfloat16
    me = lax.axis_index("hist")
    my_ka = lax.axis_index("ka")
    first = me * block
    parity = lax.rem(me, 2)
    chip = (me - parity) // 2
    partner = me + 1 - 2 * parity

    def load(source, target, place):
        copy = pltpu.make_async_copy(source, target, load_sem.at[place])
        copy.start()
        return copy

    small = [
        (krow_any, krow_ref), (dinv_any, dinv_ref), (mult_any, mult_ref),
        (band_any, band_recv.at[me]),
    ]
    for source, target in small:
        load(source, target, 0)
    large = [load(hist_any.at[m], hist_ref.at[m], 1 + m) for m in range(block)]
    others = [
        load(source, target, 1 + block + i)
        for i, (source, target) in enumerate(
            (
                (pred_any, pred_ref),
                (pseudo_any, pseudo_ref),
                (energy_any, energy_ref),
                (conn_any, conn_ref),
            )
        )
    ]
    barrier = pltpu.get_barrier_semaphore()

    def signal(sem, hist, ka):
        pl.semaphore_signal(
            sem, inc=1, device_id={"hist": hist, "ka": ka}, device_id_type=pl.DeviceIdType.MESH
        )

    def greet(target, carry):
        signal(barrier, target, my_ka)
        return carry

    lax.fori_loop(me + 1, n_hist, greet, 0)
    is_root = (my_ka == 0) & (me < lead)

    @pl.when(is_root)
    def _():
        def one(target, carry):
            for ka in range(1, n_ka):
                signal(barrier, target, ka)
            return carry

        lax.fori_loop(jnp.maximum(me, 1), n_hist, one, 0)

    @pl.when((parity == 1) & (me > 1))
    def _():
        signal(barrier, partner, my_ka)

    for ka in range(n_ka):

        @pl.when((me > 0) | (my_ka != ka))
        def _():
            signal(barrier, 0, ka)

    is_far = my_ka == n_ka - 1
    far_class = jnp.where(is_far, 1, 0)

    def remote(src, dst, send_sem, recv_sem, hist, ka):
        return pltpu.make_async_remote_copy(
            src_ref=src,
            dst_ref=dst,
            send_sem=send_sem,
            recv_sem=recv_sem,
            device_id={"hist": hist, "ka": ka},
            device_id_type=pl.DeviceIdType.MESH,
        )

    def energy_copy(target):
        return remote(band_any, band_recv.at[me], sent, got_energy, target, my_ka)

    def sum_copy(target):
        return remote(vsend, vrecv.at[me, my_ka], sent, got_sum, target, my_ka)

    def direct_copy(target):
        return remote(wsend, wrecv.at[me, my_ka], sent, got_direct, target, 0)

    def band_copy(target):
        return remote(band_any, band_far.at[my_ka, me], sent, got_far.at[far_class], target, 0)

    def pack_copy():
        return remote(d_both.at[0], d_far.at[my_ka], sent, got_far.at[far_class], me, 0)

    def own_copy():
        return remote(xfree, own_far.at[my_ka], sent, got_far.at[far_class], me, 0)

    def pair_copy(place):
        source = psend.at[2 * place + 1 - parity]
        return remote(source, pair_recv.at[place], sent, got_pair, partner, my_ka)

    def part_copy(place):
        target = 2 * place + parity
        return remote(paired.at[place], precv.at[me], sent, got_part, target, my_ka)

    def beside_copy():
        return remote(psend.at[partner], precv.at[me], sent, got_part, partner, my_ka)

    def column_copy(target):
        return remote(csend.at[target], crecv.at[me], sent, got_column, target, my_ka)

    def given_copy(target):
        return remote(gsend, grecv.at[me], sent, got_column, target, my_ka)

    def local_copy(src, hop):
        target = lax.rem(my_ka + hop, n_ka)
        return remote(src, xrecv.at[hop - 1], sent, got_local, me, target)

    def give(copy, start, stop):
        def one(target, carry):
            copy(target).start()
            return carry

        lax.fori_loop(start, stop, one, 0)

    def wait_bytes(ref, sem):
        pltpu.make_async_copy(ref, ref, sem).wait()

    def wait_units(count, sem):
        wait_bytes(units.at[pl.ds(0, count)], sem)

    e_size, v_size, w_size = size_of(band_any), size_of(vsend), size_of(wsend)
    c_size, p_size = size_of(csend.at[0]) + size_of(gsend), size_of(psend.at[0])
    pack_size = size_of(d_far.at[0]) + size_of(own_far.at[0])

    def take(ref, sem):
        for t in range(n_hist - 1):

            @pl.when(me == t)
            def _():
                wait_bytes(ref.at[pl.ds(t + 1, n_hist - 1 - t)], sem)

    current = step_ref[0]
    weight = [
        jnp.where(first + m == 0, 0.5, 1.0) * jnp.where(first + m < current, 1.0, 0.0)
        for m in range(block)
    ]
    d_both[...] = jnp.zeros(d_both.shape, f32)
    vsend[...] = jnp.zeros(vsend.shape, f32)
    wsend[...] = jnp.zeros(wsend.shape, bf16)

    near = jnp.minimum(me, lead)
    direct = jnp.where(my_ka == 0, 0, near)
    beside_root = (my_ka != 0) & (me < lead)
    packs = (my_ka != 0) & ((me == 0) | ((me < lead) & is_far))
    shares = beside_root & jnp.logical_not(packs)
    banded = jnp.where(is_far, near, jnp.where(my_ka == 0, 0, jnp.minimum(me, 1)))
    early = jnp.minimum(chip, lead // 2)
    with jax.named_scope("WBAR"):

        @pl.when(me > 0)
        def _():
            others_in = jnp.where(beside_root, 1, 0) + jnp.where(parity == 0, 1, 0)
            pl.semaphore_wait(barrier, me + direct + others_in)

    give(band_copy, 0, banded)
    give(energy_copy, 0, me)

    @pl.when((me == 1) & (my_ka != 0))
    def _():
        signal(root_in, 0, my_ka)


    with jax.named_scope("LOAD"):
        wait_units(sum(size_of(source) for source, _ in small), load_sem.at[0])
    mult = mult_ref[...].astype(f32)
    count = jnp.sum(mult, axis=1, keepdims=True)
    lane_of = lax.broadcasted_iota(jnp.int32, (group_rows, width), 1)
    for m in range(block):
        kw[m] = krow_ref[m].astype(f32) * weight[m]
    for a in range(orb):
        for c in range(orb):
            d_re = dinv_ref[a, c, 0:1, :] * mult
            d_im = dinv_ref[a, c, 1:2, :] * mult
            d_both[0, c, a : a + 1, :] = d_re
            d_both[0, c, orb + a : orb + a + 1, :] = d_im
            d_both[1, c, a : a + 1, :] = -d_im
            d_both[1, c, orb + a : orb + a + 1, :] = d_re
    same = [d_both[0, c] for c in range(orb)]
    turn = [d_both[1, c] for c in range(orb)]
    left = []
    for m in range(block):
        left.append([])
        for b in range(orb):
            plain = jnp.zeros((group_rows, lanes), f32)
            turned = plain
            for c in range(orb):
                k_re = kw[m, c, b, 0:1, :]
                k_im = kw[m, c, b, 1:2, :]
                plain += same[c] * k_re + turn[c] * k_im
                turned += turn[c] * k_re - same[c] * k_im
            left[m] += [stacked(plain), stacked(turned)]
    sums = jnp.zeros((2 * group_rows, cols), f32)
    for m in range(block):
        with jax.named_scope("LOADH"):
            large[m].wait()
        right = [hist_ref[m, p, b].reshape(cols, lanes) for b in range(orb) for p in range(2)]
        for x in range(orb):
            sums += dot(jnp.concatenate(left[m][2*x:2*x+2], axis=1), jnp.concatenate(right[2*x:2*x+2], axis=1), 1)
    with jax.named_scope("VSEND"):
        sums = folded(sums)
        vsend[:, :cols] = sums
        wsend[:, :cols] = sums.astype(bf16)
        give(direct_copy, 0, direct)
        next_chip = jnp.minimum(me, lead + 1)
        give(sum_copy, near, next_chip)
        give(sum_copy, 0, near)
        give(sum_copy, next_chip, me)

    @pl.when(packs)
    def _():
        @pl.when(me == 0)
        def _():
            pl.semaphore_wait(root_in, 1)

        xfree[...] = jnp.where(lane_of == cols, count, vsend[...])
        band_copy(me).start()
        own_copy().start()
        pack_copy().start()

    with jax.named_scope("PC"):
        for copy in others:
            copy.wait()
        half = block * block
        for m in range(block):
            h_re = pseudo_ref[m, 0].astype(f32)
            h_im = pseudo_ref[m, 1].astype(f32)
            both = jnp.concatenate([h_re, h_im], axis=1)
            for t in range(n_hist):
                hist_p[t * half + m * block : t * half + (m + 1) * block, :] = both[
                    t * block : (t + 1) * block
                ]
        for t in range(n_hist):
            csend[t] = hist_p[t * half : (t + 1) * half, :].astype(bf16)
        gsend[...] = jnp.concatenate([pred_ref[0], pred_ref[1]], axis=1)
    give(column_copy, 0, near)
    give(given_copy, 0, near)

    def one_tile(tile, carry):
        at = pl.ds(pl.multiple_of(tile * tile_rows, tile_rows), tile_rows)
        zero = jnp.zeros((tile_rows, lanes), f32)
        real = [[zero] * orb for _ in range(orb)]
        imag = [[zero] * orb for _ in range(orb)]
        for m in range(block):
            for b in range(orb):
                k_re = [kw[m, a, b, 0:1, :] for a in range(orb)]
                k_im = [kw[m, a, b, 1:2, :] for a in range(orb)]
                for c in range(orb):
                    h_re = hist_ref[m, 0, b, c, at, :].astype(f32)
                    h_im = hist_ref[m, 1, b, c, at, :].astype(f32)
                    for a in range(orb):
                        real[a][c] += k_re[a] * h_re - k_im[a] * h_im
                        imag[a][c] += k_re[a] * h_im + k_im[a] * h_re
        for a in range(orb):
            for c in range(orb):
                out_re, out_im = zero, zero
                for b in range(orb):
                    d_re = dinv_ref[a, b, 0:1, :]
                    d_im = dinv_ref[a, b, 1:2, :]
                    out_re += d_re * real[b][c] - d_im * imag[b][c]
                    out_im += d_re * imag[b][c] + d_im * real[b][c]
                for s, value in enumerate((out_re, out_im)):
                    row = ((s * orb + a) * orb + c) * block
                    for d in range(per_tile):
                        stage[d, row : row + block, :] = value[d * block : (d + 1) * block]
        for d in range(per_tile):
            target = tile * per_tile + d
            psend[target] = stage[d].astype(bf16)

            @pl.when((target < 2 * chip) & (parity != d % 2))
            def _():
                pair_copy(tile * (per_tile // 2) + d // 2).start()

            @pl.when((target == partner) & (parity == 1))
            def _():
                beside_copy().start()

        return carry

    with jax.named_scope("TILES"):
        lax.fori_loop(0, first // tile_rows + 1, one_tile, 0)

    crecv[me] = csend[me]
    grecv[me] = gsend[...]
    row_of = lax.broadcasted_iota(jnp.int32, (times, lanes), 0)
    group_of = lax.broadcasted_iota(jnp.int32, (group_rows, width), 0)
    conn = jnp.concatenate([conn_ref[...], conn_ref[...]], axis=1)
    reach = lax.broadcasted_iota(jnp.int32, (2 * states, 2 * states), 0)
    for a in range(orb):
        for p in range(2):
            at = (2 * a + p) * lanes
            hit = jnp.where(conn[2 * a : 2 * a + 1] + p * states == reach, 1.0, 0.0) + jnp.where(
                conn[2 * a + 1 : 2 * a + 2] + p * states == reach, 1.0, 0.0
            )
            hits[:, at : at + 2 * states] = hit.astype(bf16)
    mix[cols:width, :] = jnp.zeros((width - cols, mix.shape[1]), bf16)
    mix[width + cols :, :] = jnp.zeros((width - cols, mix.shape[1]), bf16)
    line = lax.broadcasted_iota(jnp.int32, (block, 2 * states), 0) + first
    lane = lax.broadcasted_iota(jnp.int32, (block, 2 * states), 1)
    energies = jnp.concatenate([energy_ref[...], energy_ref[...]], axis=1)
    spins = energies * time_step * (current - line).astype(f32)
    free_pseudo = jnp.where(lane < states, *minus_sine_cosine(spins))
    free_pseudo = free_pseudo * jnp.where(line <= current, 1.0, 0.0)
    inside = (row_of <= current) & (row_of >= first)
    summed = (row_of < current) & (row_of >= first)

    def free_sums(bands, place, same, turn, keep):
        for t in range(n_hist):
            for c in range(orb):
                band_all[place, c, t * block : (t + 1) * block, :] = bands[t, c]
        pieces = []
        for c in range(orb):
            angle = jnp.where(summed, band_all[place, c] * time_step, 0.0)
            shift = 1
            while shift < times:
                after = jnp.zeros((shift, lanes), f32)
                angle = angle + jnp.concatenate([angle[shift:], after], axis=0)
                shift *= 2
            free_re, free_im = minus_sine_cosine(angle)
            free_re = jnp.where(inside, free_re, 0.0)
            free_im = jnp.where(inside, free_im, 0.0)
            if keep:
                free_all[0, c] = free_re
                free_all[1, c] = free_im
            two_re, two_im = two_parts(free_re), two_parts(free_im)
            right = jnp.concatenate([two_re[0], two_im[0], two_re[1], two_im[1]], axis=1)
            left = jnp.concatenate([stacked(same[c]), stacked(turn[c])] * 2, axis=1)
            pieces.append(folded(dot(left, right.astype(bf16), 1)))
        pieces.append(jnp.zeros((group_rows, width - cols), f32))
        return jnp.concatenate(pieces, axis=1)

    with jax.named_scope("PAIR"):
        for n in range(1, n_hist // 2):

            @pl.when(chip == n)
            def _():
                wait_bytes(pair_recv.at[pl.ds(0, n)], got_pair)

        def combine(place, carry):
            value = psend[2 * place + parity].astype(f32) + pair_recv[place].astype(f32)
            paired[place] = value.astype(bf16)
            return carry

        lax.fori_loop(0, chip, combine, 0)
    give(part_copy, 0, early)

    with jax.named_scope("WOPEN"):

        @pl.when(me == 0)
        def _():
            pl.semaphore_wait(barrier, n_hist * n_ka - 1)

            def one(target, carry):
                signal(opened, target, my_ka)
                return carry

            lax.fori_loop(1, n_hist, one, 0)

    with jax.named_scope("TAKEE"):
        take(band_recv, got_energy)
    with jax.named_scope("FREE"):
        own = free_sums(band_recv, 0, same, turn, True) + vsend[...]
        own = jnp.where(lane_of == cols, count, own)
    give(column_copy, near, me)
    give(given_copy, near, me)
    give(part_copy, early, chip)
    with jax.named_scope("WOPEN2"):

        @pl.when(me > 0)
        def _():
            pl.semaphore_wait(opened, 1)

    @pl.when(shares)
    def _():
        xfree[...] = own

    for hop in range(1, n_ka):
        target = lax.rem(my_ka + hop, n_ka)

        @pl.when(shares & (target == 0))
        def _():
            local_copy(xfree, hop).start()

    with jax.named_scope("TAKEV"):

        take(vrecv.at[:, my_ka], got_sum)

    xsend[...] = lax.fori_loop(
        me + 1, n_hist, lambda source, value: value + vrecv[source, my_ka], own
    )
    for hop in range(1, n_ka):
        target = lax.rem(my_ka + hop, n_ka)

        @pl.when((me >= lead) | (target != 0))
        def _():
            local_copy(xsend, hop).start()

    with jax.named_scope("TOTAL"):
        at = pl.ds(pl.multiple_of(first, block), block)
        for c in range(orb):
            f_re = free_all[0, c, at, :]
            f_im = free_all[1, c, at, :]
            for a in range(orb):
                d_re = dinv_ref[a, c, 0:1, :]
                d_im = dinv_ref[a, c, 1:2, :]
                row = (a * orb + c) * block
                total[row : row + block, :] = d_re * f_re - d_im * f_im
                row += rows // 2
                total[row : row + block, :] = d_re * f_im + d_im * f_re

    with jax.named_scope("TAKEC"):
        for t in range(n_hist - 1):

            @pl.when(me == t)
            def _():
                wait_units((n_hist - 1 - t) * c_size, got_column)

    with jax.named_scope("MIX"):
        for t in range(n_hist):
            hist_p[t * half : (t + 1) * half, :] = crecv[t].astype(f32)
            hist_r[t * block : (t + 1) * block, :] = grecv[t]
        given = jnp.where(row_of >= first, hist_r[...], 0.0)
        given = jnp.concatenate(two_parts(given), axis=0).astype(bf16)
        reached = dot(given, hits[...], 0)
        reached = reached[:times] + reached[times:]
        row_weight = jnp.where(row_of == 0, 0.5 * coupling, coupling)
        row_weight = row_weight * jnp.where(row_of < current, 1.0, 0.0)
        sign = jnp.where(
            lax.broadcasted_iota(jnp.int32, (times, lanes), 1) < states, -1.0, 1.0
        )
        r_re = [reached[:, 2 * a * lanes : (2 * a + 1) * lanes] * row_weight for a in range(orb)]
        r_im = [
            reached[:, (2 * a + 1) * lanes : (2 * a + 2) * lanes] * row_weight for a in range(orb)
        ]
        for j in range(block):
            plain = jnp.where(row_of >= first, hist_p[pl.ds(j, times, stride=block), :], 0.0)
            turned = pltpu.roll(plain, states, 1) * sign
            at = slice(j * lanes, (j + 1) * lanes)
            for a in range(orb):
                low, high = a * times, (a + 1) * times
                mix[low:high, at] = (r_re[a] * plain + r_im[a] * turned).astype(bf16)
                mix[width + low : width + high, at] = (
                    r_re[a] * turned - r_im[a] * plain
                ).astype(bf16)

    def far_sums(ka):
        same_far = [d_far[ka, c] for c in range(orb)]
        turn_far = [
            jnp.concatenate(
                [-far[orb : 2 * orb], far[:orb], jnp.zeros((group_rows - 2 * orb, lanes), f32)],
                axis=0,
            )
            for far in same_far
        ]
        return free_sums(band_far.at[ka], ka, same_far, turn_far, False) + own_far[ka]

    with jax.named_scope("TAKEB"):

        @pl.when(is_root & (me == 0))
        def _():
            line_size = n_hist * e_size + pack_size
            wait_units((n_ka - 2) * line_size, got_far.at[0])
            value = xsend[...]
            for ka in range(1, n_ka - 1):
                value += far_sums(ka)
            wait_units(line_size, got_far.at[1])
            xsum[...] = value + far_sums(n_ka - 1)

        @pl.when(is_root & (me > 0))
        def _():
            for t in range(1, lead):

                @pl.when(me == t)
                def _():
                    wait_units((n_hist - t) * e_size + pack_size, got_far.at[1])

            xsum[...] = xsend[...] + far_sums(n_ka - 1)

    with jax.named_scope("SETTLE"):
        for t in range(n_hist):
            line = t * (e_size + v_size + c_size) + (2 * (t // 2) + t % 2) * p_size
            leads = min(t, lead)
            for kind in range(3):
                if kind == 0:
                    at, bands, packed, directs = my_ka == 0, 0, 0, 0
                elif kind == 1:
                    at = (my_ka > 0) & (my_ka < n_ka - 1)
                    bands, packed, directs = 1, int(t == 0), leads
                else:
                    at, packed, directs = is_far, int(t < lead), leads
                    bands = leads + packed
                size = line + directs * w_size + bands * e_size + packed * pack_size
                size += (n_ka - 1 - packed) * v_size

                @pl.when((me == t) & at)
                def _():
                    wait_units(size, sent)

    with jax.named_scope("TAKEP"):
        for t in range(n_hist - 1):
            above = n_hist // 2 - 1 - t // 2 + (1 - t % 2)

            @pl.when(me == t)
            def _():
                wait_bytes(precv.at[pl.ds(0, above)], got_part)

        total[...] = lax.fori_loop(
            chip + 1,
            n_hist // 2,
            lambda place, value: value + precv[2 * place + parity].astype(f32),
            total[...] + psend[me].astype(f32),
        )

        @pl.when(parity == 0)
        def _():
            total[...] += precv[partner].astype(f32)

        for a in range(orb):
            for c in range(orb):
                for j in range(block):
                    at = pl.ds((a * orb + c) * block + j, 2, stride=rows // 2)
                    lattice_out[j, a, c] = total[at, :].astype(bf16)

    with jax.named_scope("TAKED"):

        @pl.when(is_root)
        def _():
            for t in range(min(lead, n_hist - 1)):

                @pl.when(me == t)
                def _():
                    above, beside = pl.ds(t + 1, n_hist - 1 - t), pl.ds(1, n_ka - 1)
                    wait_bytes(wrecv.at[above, beside], got_direct)

            def one(source, value):
                for ka in range(1, n_ka):
                    value = value + wrecv[source, ka].astype(f32)
                return value

            xsum[...] = lax.fori_loop(me + 1, n_hist, one, xsum[...])

    with jax.named_scope("TAKEX"):

        @pl.when(jnp.logical_not(is_root))
        def _():
            wait_bytes(xrecv, got_local)
            value = xsend[...]
            for hop in range(1, n_ka):
                value += xrecv[hop - 1]
            xsum[...] = value

        @pl.when(is_root & (me > 0))
        def _():
            wait_bytes(xrecv.at[pl.ds(1, n_ka - 2)], got_local)
            value = xsum[...]
            for hop in range(2, n_ka):
                value += xrecv[hop - 1]
            xsum[...] = value

        local = xsum[...]
    with jax.named_scope("FINAL"):
        scale = 1.0 / local[:, cols : cols + 1]
        picked = jnp.where(lane_of // times == lax.rem(group_of, orb), local, 0.0)
        picked = jnp.concatenate(
            [jnp.where(group_of < orb, picked, 0.0), jnp.where(group_of < orb, 0.0, picked)], axis=1
        )
        sums = folded(dot(stacked(picked), mix[...], 0))
        sums = jnp.sum(sums, axis=0, keepdims=True)
        for j in range(block):
            row = free_pseudo[j : j + 1] + sums[:, j * lanes : (j + 1) * lanes] * scale[:1]
            for p in range(2):
                pseudo_out[p, j : j + 1, :] = row[:, p * states : (p + 1) * states]
        local = local * scale
        for c in range(orb):
            own = pltpu.roll(local, width - first - c * times, 1)[:, :block]
            for a in range(orb):
                for p in range(2):
                    local_out[a, c, p : p + 1, :] = own[p * orb + a : p * orb + a + 1]


def put_out(*refs):
    sources, targets, sems = refs[:3], refs[3:6], refs[6]
    copies = [
        pltpu.make_async_copy(source, target, sems.at[i])
        for i, (source, target) in enumerate(zip(sources, targets))
    ]
    for copy in copies:
        copy.start()
    for copy in copies:
        copy.wait()


def per_device(
    n_hist,
    n_ka,
    step_index,
    band_energy,
    kernel_row,
    lattice_history,
    diagonal_inverse,
    multiplicity,
    state_energy,
    connection,
    predicted_row,
    pseudo_history,
):
    block, orb, lanes = band_energy.shape
    times = lattice_history.shape[4]
    states = state_energy.shape[0]
    pairs = 2 * orb * orb
    rows = pairs * block
    per_tile = tile_rows // block
    width = -(-(orb * times + 1) // lane_count) * lane_count
    band_bytes = 4 * orb * block * lanes
    tile_bytes = 4 * group_rows * width
    most = n_hist * (
        band_bytes + tile_bytes + (2 * block + 8) * block * lanes + 2 * rows * lanes
    )
    most += (n_ka + lead + n_hist) * tile_bytes + n_ka * n_hist * band_bytes
    most //= unit_bytes
    vmem = pl.BlockSpec(memory_space=pltpu.VMEM)
    f32, bf16 = jnp.float32, jnp.bfloat16
    dma = pltpu.SemaphoreType.DMA
    operands = (
        jnp.transpose(band_energy, (1, 0, 2)),
        jnp.transpose(kernel_row, (0, 2, 3, 1, 4)),
        lattice_history,
        jnp.transpose(diagonal_inverse, (1, 2, 0, 3)),
        multiplicity[None],
        state_energy[None],
        jnp.transpose(connection),
        jnp.transpose(predicted_row, (0, 2, 1)),
        jnp.transpose(pseudo_history, (0, 1, 3, 2)),
    )
    results = pl.pallas_call(
        functools.partial(kernel, n_hist, n_ka),
        out_shape=(
            pltpu.VMEM((block, orb, orb, 2, lanes), bf16),
            pltpu.VMEM((orb, orb, 2, block), f32),
            pltpu.VMEM((2, block, states), f32),
        ),
        in_specs=[pl.BlockSpec(memory_space=pltpu.SMEM)]
        + [pl.BlockSpec(memory_space=pl.ANY)] * len(operands),
        out_specs=(vmem, vmem, vmem),
        scratch_shapes=[
            pltpu.VMEM((n_hist, *operands[0].shape), f32),
            *[pltpu.VMEM(array.shape, array.dtype) for array in operands[1:]],
            pltpu.VMEM((block, orb, orb, 2, lanes), f32),
            pltpu.VMEM((2, orb, group_rows, lanes), f32),
            pltpu.VMEM((n_ka, orb, group_rows, lanes), f32),
            pltpu.VMEM((n_ka, n_hist, *operands[0].shape), f32),
            pltpu.VMEM((n_ka, orb, times, lanes), f32),
            pltpu.VMEM((2, orb, times, lanes), f32),
            pltpu.VMEM((group_rows, width), f32),
            pltpu.VMEM((n_hist, n_ka, group_rows, width), f32),
            pltpu.VMEM((group_rows, width), bf16),
            pltpu.VMEM((n_hist, n_ka, group_rows, width), bf16),
            pltpu.VMEM((n_ka, group_rows, width), f32),
            pltpu.VMEM((group_rows, width), f32),
            pltpu.VMEM((group_rows, width), f32),
            pltpu.VMEM((group_rows, width), f32),
            pltpu.VMEM((n_ka - 1, group_rows, width), f32),
            pltpu.VMEM((n_hist, rows, lanes), bf16),
            pltpu.VMEM((n_hist // 2, rows, lanes), bf16),
            pltpu.VMEM((n_hist // 2, rows, lanes), bf16),
            pltpu.VMEM((n_hist, rows, lanes), bf16),
            pltpu.VMEM((n_hist, block * block, lanes), bf16),
            pltpu.VMEM((n_hist, block * block, lanes), bf16),
            pltpu.VMEM((block, 2 * states), f32),
            pltpu.VMEM((n_hist, block, 2 * states), f32),
            pltpu.VMEM((rows, lanes), f32),
            pltpu.VMEM((times * block, lanes), f32),
            pltpu.VMEM((times, lanes), f32),
            pltpu.VMEM((2 * states, 2 * orb * lanes), bf16),
            pltpu.VMEM((2 * width, 2 * block * states), bf16),
            pltpu.VMEM((per_tile, rows, lanes), f32),
            pltpu.VMEM((most, 1, lane_count), f32),
            dma((block + 5,)),
            *[dma] * 4,
            dma((2,)),
            *[dma] * 4,
            pltpu.SemaphoreType.REGULAR,
            pltpu.SemaphoreType.REGULAR,
        ],
        compiler_params=pltpu.CompilerParams(collective_id=0, has_side_effects=True),
    )(
        step_index,
        *operands,
    )
    lattice, local, pseudo = pl.pallas_call(
        put_out,
        out_shape=tuple(jax.ShapeDtypeStruct(array.shape, array.dtype) for array in results),
        in_specs=[vmem] * 3,
        out_specs=[pl.BlockSpec(memory_space=pl.ANY)] * 3,
        scratch_shapes=[dma((3,))],
        compiler_params=pltpu.CompilerParams(vmem_limit_bytes=layout_bytes),
    )(*results)
    return (
        jnp.transpose(lattice, (0, 3, 1, 2, 4)),
        jnp.transpose(local, (2, 0, 1, 3)),
        jnp.transpose(pseudo, (0, 2, 1)),
    )


def solution(mesh):
    in_specs = (
        P(),
        P("hist", None, "ka"),
        P("hist", None, None, None, "ka"),
        P("hist", None, None, None, None, "ka"),
        P(None, None, None, "ka"),
        P("ka"),
        P(),
        P(),
        P(None, None, "hist"),
        P("hist", None, None, None),
    )
    out_specs = (
        P("hist", None, None, None, "ka"),
        P(None, None, None, "hist"),
        P(None, None, "hist"),
    )
    return jax.shard_map(
        functools.partial(per_device, mesh.shape["hist"], mesh.shape["ka"]),
        mesh=mesh,
        in_specs=in_specs,
        out_specs=out_specs,
        check_vma=False,
    )
```

```python
import functools
import math

import jax
import jax.numpy as jnp
from jax import lax
from jax.experimental import pallas as pl
from jax.experimental.pallas import tpu as pltpu
from jax.sharding import PartitionSpec as P

time_step = 0.05
coupling = 0.02
tile_rows = 16
group_rows = 8
lead = 2
lane_count = 128
unit_bytes = 4 * lane_count
layout_bytes = 4 * 1024 * 1024


def two_parts(values):
    upper = values.astype(jnp.bfloat16).astype(jnp.float32)
    return upper, values - upper


def stacked(values):
    return jnp.concatenate(two_parts(values), axis=0).astype(jnp.bfloat16)


def size_of(ref):
    size = math.prod(ref.shape) * jnp.dtype(ref.dtype).itemsize
    assert size % unit_bytes == 0
    return size // unit_bytes


def dot(left, right, contract):
    return lax.dot_general(
        left,
        right,
        (((1,), (contract,)), ((), ())),
        preferred_element_type=jnp.float32,
    )


def folded(values):
    return values[:group_rows] + values[group_rows:]


def minus_sine_cosine(angle):
    quarter = jnp.floor(angle * 0.6366197723675814 + 0.5)
    rest = angle - quarter * 1.5703125
    rest = rest - quarter * 4.837512969970703125e-4
    rest = rest - quarter * 7.54978995489188216e-8
    square = rest * rest
    sine = (-1.9515295891e-4 * square + 8.3321608736e-3) * square - 1.6666654611e-1
    sine = sine * square * rest + rest
    cosine = (2.443315711809948e-5 * square - 1.388731625493765e-3) * square
    cosine = (cosine + 4.166664568298827e-2) * square * square - 0.5 * square + 1.0
    half = jnp.floor(quarter * 0.5)
    odd = quarter - 2.0 * half > 0.5
    sign = 2.0 * (half - 2.0 * jnp.floor(half * 0.5)) - 1.0
    return sign * jnp.where(odd, cosine, sine), sign * jnp.where(odd, -sine, cosine)


def kernel(
    n_hist,
    n_ka,
    step_ref,
    band_any,
    krow_any,
    hist_any,
    dinv_any,
    mult_any,
    energy_any,
    conn_any,
    pred_any,
    pseudo_any,
    lattice_out,
    local_out,
    pseudo_out,
    band_recv,
    krow_ref,
    hist_ref,
    dinv_ref,
    mult_ref,
    energy_ref,
    conn_ref,
    pred_ref,
    pseudo_ref,
    kw,
    d_both,
    d_far,
    band_far,
    band_all,
    free_all,
    vsend,
    vrecv,
    wsend,
    wrecv,
    own_far,
    xsend,
    xfree,
    xsum,
    xrecv,
    psend,
    pair_recv,
    paired,
    precv,
    csend,
    crecv,
    gsend,
    grecv,
    total,
    hist_p,
    hist_r,
    hits,
    mix,
    stage,
    units,
    load_sem,
    sent,
    got_energy,
    got_sum,
    got_direct,
    got_far,
    got_column,
    got_pair,
    got_part,
    got_local,
    opened,
    root_in,
):
    _, orb, block, lanes = band_recv.shape
    times = hist_ref.shape[4]
    states = energy_ref.shape[1]
    pairs = 2 * orb * orb
    rows = pairs * block
    per_tile = tile_rows // block
    width = vsend.shape[1]
    cols = orb * times
    f32, bf16 = jnp.float32, jnp.bfloat16
    me = lax.axis_index("hist")
    my_ka = lax.axis_index("ka")
    first = me * block
    parity = lax.rem(me, 2)
    chip = (me - parity) // 2
    partner = me + 1 - 2 * parity

    def load(source, target, place):
        copy = pltpu.make_async_copy(source, target, load_sem.at[place])
        copy.start()
        return copy

    small = [
        (krow_any, krow_ref), (dinv_any, dinv_ref), (mult_any, mult_ref),
        (band_any, band_recv.at[me]),
    ]
    for source, target in small:
        load(source, target, 0)
    large = [load(hist_any.at[m], hist_ref.at[m], 1 + m) for m in range(block)]
    others = [
        load(source, target, 1 + block + i)
        for i, (source, target) in enumerate(
            (
                (pred_any, pred_ref),
                (pseudo_any, pseudo_ref),
                (energy_any, energy_ref),
                (conn_any, conn_ref),
            )
        )
    ]
    barrier = pltpu.get_barrier_semaphore()

    def signal(sem, hist, ka):
        pl.semaphore_signal(
            sem, inc=1, device_id={"hist": hist, "ka": ka}, device_id_type=pl.DeviceIdType.MESH
        )

    def greet(target, carry):
        signal(barrier, target, my_ka)
        return carry

    lax.fori_loop(me + 1, n_hist, greet, 0)
    is_root = (my_ka == 0) & (me < lead)

    @pl.when(is_root)
    def _():
        def one(target, carry):
            for ka in range(1, n_ka):
                signal(barrier, target, ka)
            return carry

        lax.fori_loop(jnp.maximum(me, 1), n_hist, one, 0)

    @pl.when((parity == 1) & (me > 1))
    def _():
        signal(barrier, partner, my_ka)

    for ka in range(n_ka):

        @pl.when((me > 0) | (my_ka != ka))
        def _():
            signal(barrier, 0, ka)

    is_far = my_ka == n_ka - 1
    far_class = jnp.where(is_far, 1, 0)

    def remote(src, dst, send_sem, recv_sem, hist, ka):
        return pltpu.make_async_remote_copy(
            src_ref=src,
            dst_ref=dst,
            send_sem=send_sem,
            recv_sem=recv_sem,
            device_id={"hist": hist, "ka": ka},
            device_id_type=pl.DeviceIdType.MESH,
        )

    def energy_copy(target):
        return remote(band_any, band_recv.at[me], sent, got_energy, target, my_ka)

    def sum_copy(target):
        return remote(vsend, vrecv.at[me, my_ka], sent, got_sum, target, my_ka)

    def direct_copy(target):
        return remote(wsend, wrecv.at[me, my_ka], sent, got_direct, target, 0)

    def band_copy(target):
        return remote(band_any, band_far.at[my_ka, me], sent, got_far.at[far_class], target, 0)

    def pack_copy():
        return remote(d_both.at[0], d_far.at[my_ka], sent, got_far.at[far_class], me, 0)

    def own_copy():
        return remote(xfree, own_far.at[my_ka], sent, got_far.at[far_class], me, 0)

    def pair_copy(place):
        source = psend.at[2 * place + 1 - parity]
        return remote(source, pair_recv.at[place], sent, got_pair, partner, my_ka)

    def part_copy(place):
        target = 2 * place + parity
        return remote(paired.at[place], precv.at[me], sent, got_part, target, my_ka)

    def beside_copy():
        return remote(psend.at[partner], precv.at[me], sent, got_part, partner, my_ka)

    def column_copy(target):
        return remote(csend.at[target], crecv.at[me], sent, got_column, target, my_ka)

    def given_copy(target):
        return remote(gsend, grecv.at[me], sent, got_column, target, my_ka)

    def local_copy(src, hop):
        target = lax.rem(my_ka + hop, n_ka)
        return remote(src, xrecv.at[hop - 1], sent, got_local, me, target)

    def give(copy, start, stop):
        def one(target, carry):
            copy(target).start()
            return carry

        lax.fori_loop(start, stop, one, 0)

    def wait_bytes(ref, sem):
        pltpu.make_async_copy(ref, ref, sem).wait()

    def wait_units(count, sem):
        wait_bytes(units.at[pl.ds(0, count)], sem)

    e_size, v_size, w_size = size_of(band_any), size_of(vsend), size_of(wsend)
    c_size, p_size = size_of(csend.at[0]) + size_of(gsend), size_of(psend.at[0])
    pack_size = size_of(d_far.at[0]) + size_of(own_far.at[0])

    def take(ref, sem):
        for t in range(n_hist - 1):

            @pl.when(me == t)
            def _():
                wait_bytes(ref.at[pl.ds(t + 1, n_hist - 1 - t)], sem)

    current = step_ref[0]
    weight = [
        jnp.where(first + m == 0, 0.5, 1.0) * jnp.where(first + m < current, 1.0, 0.0)
        for m in range(block)
    ]
    d_both[...] = jnp.zeros(d_both.shape, f32)
    vsend[...] = jnp.zeros(vsend.shape, f32)
    wsend[...] = jnp.zeros(wsend.shape, bf16)

    near = jnp.minimum(me, lead)
    direct = jnp.where(my_ka == 0, 0, near)
    beside_root = (my_ka != 0) & (me < lead)
    packs = (my_ka != 0) & ((me == 0) | ((me < lead) & is_far))
    shares = beside_root & jnp.logical_not(packs)
    banded = jnp.where(is_far, near, jnp.where(my_ka == 0, 0, jnp.minimum(me, 1)))
    early = jnp.minimum(chip, lead // 2)
    with jax.named_scope("WBAR"):

        @pl.when(me > 0)
        def _():
            others_in = jnp.where(beside_root, 1, 0) + jnp.where(parity == 0, 1, 0)
            pl.semaphore_wait(barrier, me + direct + others_in)

    give(band_copy, 0, banded)
    give(energy_copy, 0, me)

    @pl.when((me == 1) & (my_ka != 0))
    def _():
        signal(root_in, 0, my_ka)


    with jax.named_scope("LOAD"):
        wait_units(sum(size_of(source) for source, _ in small), load_sem.at[0])
    mult = mult_ref[...].astype(f32)
    count = jnp.sum(mult, axis=1, keepdims=True)
    lane_of = lax.broadcasted_iota(jnp.int32, (group_rows, width), 1)
    for m in range(block):
        kw[m] = krow_ref[m].astype(f32) * weight[m]
    for a in range(orb):
        for c in range(orb):
            d_re = dinv_ref[a, c, 0:1, :] * mult
            d_im = dinv_ref[a, c, 1:2, :] * mult
            d_both[0, c, a : a + 1, :] = d_re
            d_both[0, c, orb + a : orb + a + 1, :] = d_im
            d_both[1, c, a : a + 1, :] = -d_im
            d_both[1, c, orb + a : orb + a + 1, :] = d_re
    same = [d_both[0, c] for c in range(orb)]
    turn = [d_both[1, c] for c in range(orb)]
    def factors(m):
        found = []
        for b in range(orb):
            plain = jnp.zeros((group_rows, lanes), f32)
            turned = plain
            for c in range(orb):
                k_re = kw[m, c, b, 0:1, :]
                k_im = kw[m, c, b, 1:2, :]
                plain += same[c] * k_re + turn[c] * k_im
                turned += turn[c] * k_re - same[c] * k_im
            found.append(jnp.concatenate([stacked(plain), stacked(turned)], axis=1))
        return found

    sums = jnp.zeros((2 * group_rows, cols), f32)
    left = factors(0)
    for m in range(block):
        with jax.named_scope("LOADH"):
            large[m].wait()
        for b in range(orb):
            right = [hist_ref[m, p, b].reshape(cols, lanes) for p in range(2)]
            sums += dot(left[b], jnp.concatenate(right, axis=1), 1)
        if m + 1 < block:
            left = factors(m + 1)
    with jax.named_scope("VSEND"):
        sums = folded(sums)
        vsend[:, :cols] = sums
        wsend[:, :cols] = sums.astype(bf16)
        give(direct_copy, 0, direct)
        next_chip = jnp.minimum(me, lead + 1)
        give(sum_copy, near, next_chip)
        give(sum_copy, 0, near)
        give(sum_copy, next_chip, me)

    @pl.when(packs)
    def _():
        @pl.when(me == 0)
        def _():
            pl.semaphore_wait(root_in, 1)

        xfree[...] = jnp.where(lane_of == cols, count, vsend[...])
        band_copy(me).start()
        own_copy().start()
        pack_copy().start()

    with jax.named_scope("PC"):
        for copy in others:
            copy.wait()
        half = block * block
        for m in range(block):
            h_re = pseudo_ref[m, 0].astype(f32)
            h_im = pseudo_ref[m, 1].astype(f32)
            both = jnp.concatenate([h_re, h_im], axis=1)
            for t in range(n_hist):
                hist_p[t * half + m * block : t * half + (m + 1) * block, :] = both[
                    t * block : (t + 1) * block
                ]
        for t in range(n_hist):
            csend[t] = hist_p[t * half : (t + 1) * half, :].astype(bf16)
        gsend[...] = jnp.concatenate([pred_ref[0], pred_ref[1]], axis=1)
    give(column_copy, 0, near)
    give(given_copy, 0, near)

    def one_tile(tile, carry):
        at = pl.ds(pl.multiple_of(tile * tile_rows, tile_rows), tile_rows)
        zero = jnp.zeros((tile_rows, lanes), f32)
        real = [[zero] * orb for _ in range(orb)]
        imag = [[zero] * orb for _ in range(orb)]
        for m in range(block):
            for b in range(orb):
                k_re = [kw[m, a, b, 0:1, :] for a in range(orb)]
                k_im = [kw[m, a, b, 1:2, :] for a in range(orb)]
                for c in range(orb):
                    h_re = hist_ref[m, 0, b, c, at, :].astype(f32)
                    h_im = hist_ref[m, 1, b, c, at, :].astype(f32)
                    for a in range(orb):
                        real[a][c] += k_re[a] * h_re - k_im[a] * h_im
                        imag[a][c] += k_re[a] * h_im + k_im[a] * h_re
        for a in range(orb):
            for c in range(orb):
                out_re, out_im = zero, zero
                for b in range(orb):
                    d_re = dinv_ref[a, b, 0:1, :]
                    d_im = dinv_ref[a, b, 1:2, :]
                    out_re += d_re * real[b][c] - d_im * imag[b][c]
                    out_im += d_re * imag[b][c] + d_im * real[b][c]
                for s, value in enumerate((out_re, out_im)):
                    row = ((s * orb + a) * orb + c) * block
                    for d in range(per_tile):
                        stage[d, row : row + block, :] = value[d * block : (d + 1) * block]
        for d in range(per_tile):
            target = tile * per_tile + d
            psend[target] = stage[d].astype(bf16)

            @pl.when((target < 2 * chip) & (parity != d % 2))
            def _():
                pair_copy(tile * (per_tile // 2) + d // 2).start()

            @pl.when((target == partner) & (parity == 1))
            def _():
                beside_copy().start()

        return carry

    with jax.named_scope("TILES"):
        lax.fori_loop(0, first // tile_rows + 1, one_tile, 0)

    crecv[me] = csend[me]
    grecv[me] = gsend[...]
    row_of = lax.broadcasted_iota(jnp.int32, (times, lanes), 0)
    group_of = lax.broadcasted_iota(jnp.int32, (group_rows, width), 0)
    conn = jnp.concatenate([conn_ref[...], conn_ref[...]], axis=1)
    reach = lax.broadcasted_iota(jnp.int32, (2 * states, 2 * states), 0)
    for a in range(orb):
        for p in range(2):
            at = (2 * a + p) * lanes
            hit = jnp.where(conn[2 * a : 2 * a + 1] + p * states == reach, 1.0, 0.0) + jnp.where(
                conn[2 * a + 1 : 2 * a + 2] + p * states == reach, 1.0, 0.0
            )
            hits[:, at : at + 2 * states] = hit.astype(bf16)
    mix[cols:width, :] = jnp.zeros((width - cols, mix.shape[1]), bf16)
    mix[width + cols :, :] = jnp.zeros((width - cols, mix.shape[1]), bf16)
    line = lax.broadcasted_iota(jnp.int32, (block, 2 * states), 0) + first
    lane = lax.broadcasted_iota(jnp.int32, (block, 2 * states), 1)
    energies = jnp.concatenate([energy_ref[...], energy_ref[...]], axis=1)
    spins = energies * time_step * (current - line).astype(f32)
    free_pseudo = jnp.where(lane < states, *minus_sine_cosine(spins))
    free_pseudo = free_pseudo * jnp.where(line <= current, 1.0, 0.0)
    inside = (row_of <= current) & (row_of >= first)
    summed = (row_of < current) & (row_of >= first)

    def free_sums(bands, place, same, turn, keep):
        for t in range(n_hist):
            for c in range(orb):
                band_all[place, c, t * block : (t + 1) * block, :] = bands[t, c]
        pieces = []
        for c in range(orb):
            angle = jnp.where(summed, band_all[place, c] * time_step, 0.0)
            shift = 1
            while shift < times:
                after = jnp.zeros((shift, lanes), f32)
                angle = angle + jnp.concatenate([angle[shift:], after], axis=0)
                shift *= 2
            free_re, free_im = minus_sine_cosine(angle)
            free_re = jnp.where(inside, free_re, 0.0)
            free_im = jnp.where(inside, free_im, 0.0)
            if keep:
                free_all[0, c] = free_re
                free_all[1, c] = free_im
            two_re, two_im = two_parts(free_re), two_parts(free_im)
            right = jnp.concatenate([two_re[0], two_im[0], two_re[1], two_im[1]], axis=1)
            left = jnp.concatenate([stacked(same[c]), stacked(turn[c])] * 2, axis=1)
            pieces.append(folded(dot(left, right.astype(bf16), 1)))
        pieces.append(jnp.zeros((group_rows, width - cols), f32))
        return jnp.concatenate(pieces, axis=1)

    with jax.named_scope("PAIR"):
        for n in range(1, n_hist // 2):

            @pl.when(chip == n)
            def _():
                wait_bytes(pair_recv.at[pl.ds(0, n)], got_pair)

        def combine(place, carry):
            value = psend[2 * place + parity].astype(f32) + pair_recv[place].astype(f32)
            paired[place] = value.astype(bf16)
            return carry

        lax.fori_loop(0, chip, combine, 0)
    give(part_copy, 0, early)

    with jax.named_scope("WOPEN"):

        @pl.when(me == 0)
        def _():
            pl.semaphore_wait(barrier, n_hist * n_ka - 1)

            def one(target, carry):
                signal(opened, target, my_ka)
                return carry

            lax.fori_loop(1, n_hist, one, 0)

    with jax.named_scope("TAKEE"):
        take(band_recv, got_energy)
    with jax.named_scope("FREE"):
        own = free_sums(band_recv, 0, same, turn, True) + vsend[...]
        own = jnp.where(lane_of == cols, count, own)
    give(column_copy, near, me)
    give(given_copy, near, me)
    give(part_copy, early, chip)
    with jax.named_scope("WOPEN2"):

        @pl.when(me > 0)
        def _():
            pl.semaphore_wait(opened, 1)

    @pl.when(shares)
    def _():
        xfree[...] = own

    for hop in range(1, n_ka):
        target = lax.rem(my_ka + hop, n_ka)

        @pl.when(shares & (target == 0))
        def _():
            local_copy(xfree, hop).start()

    with jax.named_scope("TAKEV"):

        take(vrecv.at[:, my_ka], got_sum)

    xsend[...] = lax.fori_loop(
        me + 1, n_hist, lambda source, value: value + vrecv[source, my_ka], own
    )
    for hop in range(1, n_ka):
        target = lax.rem(my_ka + hop, n_ka)

        @pl.when((me >= lead) | (target != 0))
        def _():
            local_copy(xsend, hop).start()

    with jax.named_scope("TOTAL"):
        at = pl.ds(pl.multiple_of(first, block), block)
        for c in range(orb):
            f_re = free_all[0, c, at, :]
            f_im = free_all[1, c, at, :]
            for a in range(orb):
                d_re = dinv_ref[a, c, 0:1, :]
                d_im = dinv_ref[a, c, 1:2, :]
                row = (a * orb + c) * block
                total[row : row + block, :] = d_re * f_re - d_im * f_im
                row += rows // 2
                total[row : row + block, :] = d_re * f_im + d_im * f_re

    with jax.named_scope("TAKEC"):
        for t in range(n_hist - 1):

            @pl.when(me == t)
            def _():
                wait_units((n_hist - 1 - t) * c_size, got_column)

    with jax.named_scope("MIX"):
        for t in range(n_hist):
            hist_p[t * half : (t + 1) * half, :] = crecv[t].astype(f32)
            hist_r[t * block : (t + 1) * block, :] = grecv[t]
        given = jnp.where(row_of >= first, hist_r[...], 0.0)
        given = jnp.concatenate(two_parts(given), axis=0).astype(bf16)
        reached = dot(given, hits[...], 0)
        reached = reached[:times] + reached[times:]
        row_weight = jnp.where(row_of == 0, 0.5 * coupling, coupling)
        row_weight = row_weight * jnp.where(row_of < current, 1.0, 0.0)
        sign = jnp.where(
            lax.broadcasted_iota(jnp.int32, (times, lanes), 1) < states, -1.0, 1.0
        )
        r_re = [reached[:, 2 * a * lanes : (2 * a + 1) * lanes] * row_weight for a in range(orb)]
        r_im = [
            reached[:, (2 * a + 1) * lanes : (2 * a + 2) * lanes] * row_weight for a in range(orb)
        ]
        for j in range(block):
            plain = jnp.where(row_of >= first, hist_p[pl.ds(j, times, stride=block), :], 0.0)
            turned = pltpu.roll(plain, states, 1) * sign
            at = slice(j * lanes, (j + 1) * lanes)
            for a in range(orb):
                low, high = a * times, (a + 1) * times
                mix[low:high, at] = (r_re[a] * plain + r_im[a] * turned).astype(bf16)
                mix[width + low : width + high, at] = (
                    r_re[a] * turned - r_im[a] * plain
                ).astype(bf16)

    def far_sums(ka):
        same_far = [d_far[ka, c] for c in range(orb)]
        turn_far = [
            jnp.concatenate(
                [-far[orb : 2 * orb], far[:orb], jnp.zeros((group_rows - 2 * orb, lanes), f32)],
                axis=0,
            )
            for far in same_far
        ]
        return free_sums(band_far.at[ka], ka, same_far, turn_far, False) + own_far[ka]

    with jax.named_scope("TAKEB"):

        @pl.when(is_root & (me == 0))
        def _():
            line_size = n_hist * e_size + pack_size
            wait_units((n_ka - 2) * line_size, got_far.at[0])
            value = xsend[...]
            for ka in range(1, n_ka - 1):
                value += far_sums(ka)
            wait_units(line_size, got_far.at[1])
            xsum[...] = value + far_sums(n_ka - 1)

        @pl.when(is_root & (me > 0))
        def _():
            for t in range(1, lead):

                @pl.when(me == t)
                def _():
                    wait_units((n_hist - t) * e_size + pack_size, got_far.at[1])

            xsum[...] = xsend[...] + far_sums(n_ka - 1)

    with jax.named_scope("SETTLE"):
        for t in range(n_hist):
            line = t * (e_size + v_size + c_size) + (2 * (t // 2) + t % 2) * p_size
            leads = min(t, lead)
            for kind in range(3):
                if kind == 0:
                    at, bands, packed, directs = my_ka == 0, 0, 0, 0
                elif kind == 1:
                    at = (my_ka > 0) & (my_ka < n_ka - 1)
                    bands, packed, directs = 1, int(t == 0), leads
                else:
                    at, packed, directs = is_far, int(t < lead), leads
                    bands = leads + packed
                size = line + directs * w_size + bands * e_size + packed * pack_size
                size += (n_ka - 1 - packed) * v_size

                @pl.when((me == t) & at)
                def _():
                    wait_units(size, sent)

    with jax.named_scope("TAKEP"):
        for t in range(n_hist - 1):
            above = n_hist // 2 - 1 - t // 2 + (1 - t % 2)

            @pl.when(me == t)
            def _():
                wait_bytes(precv.at[pl.ds(0, above)], got_part)

        total[...] = lax.fori_loop(
            chip + 1,
            n_hist // 2,
            lambda place, value: value + precv[2 * place + parity].astype(f32),
            total[...] + psend[me].astype(f32),
        )

        @pl.when(parity == 0)
        def _():
            total[...] += precv[partner].astype(f32)

        for a in range(orb):
            for c in range(orb):
                for j in range(block):
                    at = pl.ds((a * orb + c) * block + j, 2, stride=rows // 2)
                    lattice_out[j, a, c] = total[at, :].astype(bf16)

    with jax.named_scope("TAKED"):

        @pl.when(is_root)
        def _():
            for t in range(min(lead, n_hist - 1)):

                @pl.when(me == t)
                def _():
                    above, beside = pl.ds(t + 1, n_hist - 1 - t), pl.ds(1, n_ka - 1)
                    wait_bytes(wrecv.at[above, beside], got_direct)

            def one(source, value):
                for ka in range(1, n_ka):
                    value = value + wrecv[source, ka].astype(f32)
                return value

            xsum[...] = lax.fori_loop(me + 1, n_hist, one, xsum[...])

    with jax.named_scope("TAKEX"):

        @pl.when(jnp.logical_not(is_root))
        def _():
            wait_bytes(xrecv, got_local)
            value = xsend[...]
            for hop in range(1, n_ka):
                value += xrecv[hop - 1]
            xsum[...] = value

        @pl.when(is_root & (me > 0))
        def _():
            wait_bytes(xrecv.at[pl.ds(1, n_ka - 2)], got_local)
            value = xsum[...]
            for hop in range(2, n_ka):
                value += xrecv[hop - 1]
            xsum[...] = value

        local = xsum[...]
    with jax.named_scope("FINAL"):
        scale = 1.0 / local[:, cols : cols + 1]
        picked = jnp.where(lane_of // times == lax.rem(group_of, orb), local, 0.0)
        picked = jnp.concatenate(
            [jnp.where(group_of < orb, picked, 0.0), jnp.where(group_of < orb, 0.0, picked)], axis=1
        )
        sums = folded(dot(stacked(picked), mix[...], 0))
        sums = jnp.sum(sums, axis=0, keepdims=True)
        for j in range(block):
            row = free_pseudo[j : j + 1] + sums[:, j * lanes : (j + 1) * lanes] * scale[:1]
            for p in range(2):
                pseudo_out[p, j : j + 1, :] = row[:, p * states : (p + 1) * states]
        local = local * scale
        for c in range(orb):
            own = pltpu.roll(local, width - first - c * times, 1)[:, :block]
            for a in range(orb):
                for p in range(2):
                    local_out[a, c, p : p + 1, :] = own[p * orb + a : p * orb + a + 1]


def put_out(*refs):
    sources, targets, sems = refs[:3], refs[3:6], refs[6]
    copies = [
        pltpu.make_async_copy(source, target, sems.at[i])
        for i, (source, target) in enumerate(zip(sources, targets))
    ]
    for copy in copies:
        copy.start()
    for copy in copies:
        copy.wait()


def per_device(
    n_hist,
    n_ka,
    step_index,
    band_energy,
    kernel_row,
    lattice_history,
    diagonal_inverse,
    multiplicity,
    state_energy,
    connection,
    predicted_row,
    pseudo_history,
):
    block, orb, lanes = band_energy.shape
    times = lattice_history.shape[4]
    states = state_energy.shape[0]
    pairs = 2 * orb * orb
    rows = pairs * block
    per_tile = tile_rows // block
    width = -(-(orb * times + 1) // lane_count) * lane_count
    band_bytes = 4 * orb * block * lanes
    tile_bytes = 4 * group_rows * width
    most = n_hist * (
        band_bytes + tile_bytes + (2 * block + 8) * block * lanes + 2 * rows * lanes
    )
    most += (n_ka + lead + n_hist) * tile_bytes + n_ka * n_hist * band_bytes
    most //= unit_bytes
    vmem = pl.BlockSpec(memory_space=pltpu.VMEM)
    f32, bf16 = jnp.float32, jnp.bfloat16
    dma = pltpu.SemaphoreType.DMA
    operands = (
        jnp.transpose(band_energy, (1, 0, 2)),
        jnp.transpose(kernel_row, (0, 2, 3, 1, 4)),
        lattice_history,
        jnp.transpose(diagonal_inverse, (1, 2, 0, 3)),
        multiplicity[None],
        state_energy[None],
        jnp.transpose(connection),
        jnp.transpose(predicted_row, (0, 2, 1)),
        jnp.transpose(pseudo_history, (0, 1, 3, 2)),
    )
    results = pl.pallas_call(
        functools.partial(kernel, n_hist, n_ka),
        out_shape=(
            pltpu.VMEM((block, orb, orb, 2, lanes), bf16),
            pltpu.VMEM((orb, orb, 2, block), f32),
            pltpu.VMEM((2, block, states), f32),
        ),
        in_specs=[pl.BlockSpec(memory_space=pltpu.SMEM)]
        + [pl.BlockSpec(memory_space=pl.ANY)] * len(operands),
        out_specs=(vmem, vmem, vmem),
        scratch_shapes=[
            pltpu.VMEM((n_hist, *operands[0].shape), f32),
            *[pltpu.VMEM(array.shape, array.dtype) for array in operands[1:]],
            pltpu.VMEM((block, orb, orb, 2, lanes), f32),
            pltpu.VMEM((2, orb, group_rows, lanes), f32),
            pltpu.VMEM((n_ka, orb, group_rows, lanes), f32),
            pltpu.VMEM((n_ka, n_hist, *operands[0].shape), f32),
            pltpu.VMEM((n_ka, orb, times, lanes), f32),
            pltpu.VMEM((2, orb, times, lanes), f32),
            pltpu.VMEM((group_rows, width), f32),
            pltpu.VMEM((n_hist, n_ka, group_rows, width), f32),
            pltpu.VMEM((group_rows, width), bf16),
            pltpu.VMEM((n_hist, n_ka, group_rows, width), bf16),
            pltpu.VMEM((n_ka, group_rows, width), f32),
            pltpu.VMEM((group_rows, width), f32),
            pltpu.VMEM((group_rows, width), f32),
            pltpu.VMEM((group_rows, width), f32),
            pltpu.VMEM((n_ka - 1, group_rows, width), f32),
            pltpu.VMEM((n_hist, rows, lanes), bf16),
            pltpu.VMEM((n_hist // 2, rows, lanes), bf16),
            pltpu.VMEM((n_hist // 2, rows, lanes), bf16),
            pltpu.VMEM((n_hist, rows, lanes), bf16),
            pltpu.VMEM((n_hist, block * block, lanes), bf16),
            pltpu.VMEM((n_hist, block * block, lanes), bf16),
            pltpu.VMEM((block, 2 * states), f32),
            pltpu.VMEM((n_hist, block, 2 * states), f32),
            pltpu.VMEM((rows, lanes), f32),
            pltpu.VMEM((times * block, lanes), f32),
            pltpu.VMEM((times, lanes), f32),
            pltpu.VMEM((2 * states, 2 * orb * lanes), bf16),
            pltpu.VMEM((2 * width, 2 * block * states), bf16),
            pltpu.VMEM((per_tile, rows, lanes), f32),
            pltpu.VMEM((most, 1, lane_count), f32),
            dma((block + 5,)),
            *[dma] * 4,
            dma((2,)),
            *[dma] * 4,
            pltpu.SemaphoreType.REGULAR,
            pltpu.SemaphoreType.REGULAR,
        ],
        compiler_params=pltpu.CompilerParams(collective_id=0, has_side_effects=True),
    )(
        step_index,
        *operands,
    )
    lattice, local, pseudo = pl.pallas_call(
        put_out,
        out_shape=tuple(jax.ShapeDtypeStruct(array.shape, array.dtype) for array in results),
        in_specs=[vmem] * 3,
        out_specs=[pl.BlockSpec(memory_space=pl.ANY)] * 3,
        scratch_shapes=[dma((3,))],
        compiler_params=pltpu.CompilerParams(vmem_limit_bytes=layout_bytes),
    )(*results)
    return (
        jnp.transpose(lattice, (0, 3, 1, 2, 4)),
        jnp.transpose(local, (2, 0, 1, 3)),
        jnp.transpose(pseudo, (0, 2, 1)),
    )


def solution(mesh):
    in_specs = (
        P(),
        P("hist", None, "ka"),
        P("hist", None, None, None, "ka"),
        P("hist", None, None, None, None, "ka"),
        P(None, None, None, "ka"),
        P("ka"),
        P(),
        P(),
        P(None, None, "hist"),
        P("hist", None, None, None),
    )
    out_specs = (
        P("hist", None, None, None, "ka"),
        P(None, None, None, "hist"),
        P(None, None, "hist"),
    )
    return jax.shard_map(
        functools.partial(per_device, mesh.shape["hist"], mesh.shape["ka"]),
        mesh=mesh,
        in_specs=in_specs,
        out_specs=out_specs,
        check_vma=False,
    )
```
